32 devices in a mesh: dp: 16 (over z, x, core), tensor: 2 (over y).
Axes of the slice: x: 2, y: 2, z: 4, core: 2. Of those that a mesh axis runs over, the one named last changes fastest.
Arguments:
- images: bfloat16 [96, 729, 1152], P('dp', None, 'tensor'), may hold values from -6 to 6
- valid_flags: int32 [96], P('dp'), may hold values 0 or 1
- cotangent: bfloat16 [96, 729, 1152], P('dp', None, 'tensor'), may hold values from -6 to 6
- ln1_gain: bfloat16 [1152], P('tensor'), may hold values from 0.099609375 to 1.8984375
- ln1_bias: bfloat16 [1152], P('tensor'), may hold values from -3 to 3
- q_weight: bfloat16 [1152, 1152], P(None, 'tensor'), may hold values from -0.1875 to 0.1875
- q_bias: bfloat16 [1152], P('tensor'), may hold values from -3 to 3
- k_weight: bfloat16 [1152, 1152], P(None, 'tensor'), may hold values from -0.1875 to 0.1875
- v_weight: bfloat16 [1152, 1152], P(None, 'tensor'), may hold values from -0.1875 to 0.1875
- v_bias: bfloat16 [1152], P('tensor'), may hold values from -3 to 3
- o_weight: bfloat16 [1152, 1152], P('tensor'), may hold values from -2.5 to 2.5
- o_bias: bfloat16 [1152], P('tensor'), may hold values from -3 to 3
- ln2_gain: bfloat16 [1152], P('tensor'), may hold values from 0.099609375 to 1.8984375
- ln2_bias: bfloat16 [1152], P('tensor'), may hold values from -3 to 3
- fc1_weight: bfloat16 [1152, 4304], P(None, 'tensor'), may hold values from -0.1875 to 0.1875
- fc1_bias: bfloat16 [4304], P('tensor'), may hold values from -3 to 3
- fc2_weight: bfloat16 [4304, 1152], P('tensor'), may hold values from -0.09375 to 0.09375
- fc2_bias: bfloat16 [1152], P('tensor'), may hold values from -3 to 3
Outputs:
- layer_out: bfloat16 [96, 729, 1152], P('dp', None, 'tensor')
- input_grad: bfloat16 [96, 729, 1152], P('dp', None, 'tensor')
- ln1_gain_grad: float32 [1152], P('tensor')
- ln1_bias_grad: float32 [1152], P('tensor')
- q_weight_grad: float32 [1152, 1152], P(None, 'tensor')
- q_bias_grad: float32 [1152], P('tensor')
- k_weight_grad: float32 [1152, 1152], P(None, 'tensor')
- v_weight_grad: float32 [1152, 1152], P(None, 'tensor')
- v_bias_grad: float32 [1152], P('tensor')
- o_weight_grad: float32 [1152, 1152], P('tensor')
- o_bias_grad: float32 [1152], P('tensor')
- ln2_gain_grad: float32 [1152], P('tensor')
- ln2_bias_grad: float32 [1152], P('tensor')
- fc1_weight_grad: float32 [1152, 4304], P(None, 'tensor')
- fc1_bias_grad: float32 [4304], P('tensor')
- fc2_weight_grad: float32 [4304, 1152], P('tensor')
- fc2_bias_grad: float32 [1152], P('tensor')
The draws below stay inside these ranges and needn't reach their ends.
Inputs may be any that keep to these rules, and one draw needn't show every extreme that they name: `valid_flags`: 1 marks an image, 0 a padding slot.
All inputs are finite; a program needn't handle non-finite values. No bound on the sum of `valid_flags` on one device may be relied on, other than what follows from the above.
Results may differ from the reference program's by a relative error of at most 0.02.
Values may be sent and summed in bfloat16 or wider, within the bound.
No kernel may reach another device: no remote copies, remote signals or barrier semaphores. Data moves between devices by JAX's collectives and lax.ppermute only.
A program may use at most 576 MiB of HBM per device.

```python
import math
import jax
import jax.numpy as jnp
from jax import lax

D = 1152
HEADS = 16
HDIM = 72
FF = 4304
SEQ = 729
IMAGES = 96
N_TENSOR = 2


def set_ends(values, own_key, smallest, high):
    longest = values.shape.index(max(values.shape))
    spots = []
    for shift in (0, 1):
        where = [jax.random.randint(jax.random.fold_in(own_key, axis), (), 0, length) for axis, length in enumerate(values.shape)]
        where[longest] = (where[longest] + shift) % values.shape[longest]
        spots.append(tuple(where))
    return values.at[spots[0]].set(smallest).at[spots[1]].set(high)


def shard_levels(stream_key, extent, shards, least, largest):
    level, own = 1.0, jax.random.fold_in(stream_key, 6)
    for position, shards_of in shards:
        heights = jnp.exp(jax.random.uniform(jax.random.fold_in(own, position), (shards_of,), jnp.float32, least / len(shards), largest / len(shards)))
        level = level * jnp.repeat(heights, extent[position] // shards_of).reshape([-1 if axis == position else 1 for axis in range(len(extent))])
    return level


def noise(stream_key, shape, scale, reach, shards=(), dtype=jnp.bfloat16):
    gain = shard_levels(stream_key, shape, shards, -0.22, 0.18) if shards else 1.0
    drawn = jax.random.normal(stream_key, shape, jnp.float32) * scale * gain
    return jnp.minimum(jnp.maximum(drawn, -reach), reach).astype(dtype)


def setup_inputs(seed: int = 0) -> dict:
    seeds = jax.random.split(jax.random.key(seed), 19)
    images = noise(seeds[0], (IMAGES, SEQ, D), 1.0, 6.0, ((0, 16), (2, 2)))
    valid_flags = set_ends((jax.random.randint(seeds[1], (IMAGES,), 0, 4) < 3).astype(jnp.int32), jax.random.fold_in(seeds[1], 1), 0, 1)
    cotangent = noise(seeds[2], (IMAGES, SEQ, D), 1.0, 6.0, ((0, 16), (2, 2)))
    ln1_gain = jnp.clip(1.0 + 0.18 * jax.random.normal(seeds[3], (D,), jnp.float32), 0.099609375, 1.8984375).astype(jnp.bfloat16)
    ln1_bias = noise(seeds[4], (D,), 0.5, 3.0, ((0, 2),))
    q_weight = noise(seeds[5], (D, HEADS * HDIM), D ** -0.5, 0.1875, ((1, 2),))
    q_bias = noise(seeds[6], (HEADS * HDIM,), 0.5, 3.0, ((0, 2),))
    k_weight = noise(seeds[7], (D, HEADS * HDIM), D ** -0.5, 0.1875, ((1, 2),))
    v_weight = noise(seeds[8], (D, HEADS * HDIM), D ** -0.5, 0.1875, ((1, 2),))
    v_bias = noise(seeds[9], (HEADS * HDIM,), 0.5, 3.0, ((0, 2),))
    o_weight = noise(seeds[10], (HEADS * HDIM, D), (max(HEADS * HDIM * 4 // SEQ, 1)) ** -0.5, 2.5, ((0, 2),))
    o_bias = noise(seeds[11], (D,), 0.5, 3.0, ((0, 2),))
    ln2_gain = jnp.clip(1.0 + 0.18 * jax.random.normal(seeds[12], (D,), jnp.float32), 0.099609375, 1.8984375).astype(jnp.bfloat16)
    ln2_bias = noise(seeds[13], (D,), 0.5, 3.0, ((0, 2),))
    fc1_weight = noise(seeds[14], (D, FF), D ** -0.5, 0.1875, ((1, 2),))
    fc1_bias = noise(seeds[15], (FF,), 0.5, 3.0, ((0, 2),))
    fc2_weight = noise(seeds[16], (FF, D), FF ** -0.5, 0.09375, ((0, 2),))
    fc2_bias = noise(seeds[17], (D,), 0.5, 3.0, ((0, 2),))
    return {"images": images, "valid_flags": valid_flags, "cotangent": cotangent, "ln1_gain": ln1_gain, "ln1_bias": ln1_bias, "q_weight": q_weight, "q_bias": q_bias, "k_weight": k_weight, "v_weight": v_weight, "v_bias": v_bias, "o_weight": o_weight, "o_bias": o_bias, "ln2_gain": ln2_gain, "ln2_bias": ln2_bias, "fc1_weight": fc1_weight, "fc1_bias": fc1_bias, "fc2_weight": fc2_weight, "fc2_bias": fc2_bias}


EPS = 1e-06
GELU_C = math.sqrt(2.0 / math.pi)
GELU_A = 0.044715
HIGHEST_PREC = lax.Precision.HIGHEST

@jax.custom_vjp
def low(v):
    return lax.optimization_barrier(v.astype(jnp.bfloat16)).astype(jnp.float32)

@jax.custom_vjp
def low_back(v):
    return v

def low_keep(v):
    return (low(v), None)

def low_pass(kept, grad):
    return (grad,)

def back_keep(v):
    return (v, None)

def back_low(kept, grad):
    return (low(grad),)
low.defvjp(low_keep, low_pass)
low_back.defvjp(back_keep, back_low)

def layer_norm(values, gain_vec, bias_vec):
    row_mean = lax.optimization_barrier(jnp.mean(values, axis=-1, keepdims=True))
    centred = values - row_mean
    row_var = lax.optimization_barrier(jnp.mean(centred * centred, axis=-1, keepdims=True))
    return centred * lax.rsqrt(row_var + EPS) * gain_vec + bias_vec

def gelu_tanh(values):
    return 0.5 * values * (1.0 + jnp.tanh(GELU_C * (values + GELU_A * values * values * values)))

def product(left, right):
    return jnp.dot(left, right, precision=HIGHEST_PREC, preferred_element_type=jnp.float32)

def part_sum(source, weight):
    width = weight.shape[0] // N_TENSOR
    total = low(product(source[..., 0:width], weight[0:width]))
    for group_index in range(1, N_TENSOR):
        start = group_index * width
        total = total + low(product(source[..., start:start + width], weight[start:start + width]))
    return total

def group_cols(source, weight):
    width = weight.shape[1] // N_TENSOR
    pieces = []
    for group_index in range(N_TENSOR):
        start = group_index * width
        pieces.append(product(low_back(source), weight[:, start:start + width]))
    return jnp.concatenate(pieces, axis=-1)

def group_qkv(source, q_weight, k_weight, v_weight):
    width = q_weight.shape[1] // N_TENSOR
    q_pieces, k_pieces, v_pieces = ([], [], [])
    for group_index in range(N_TENSOR):
        start = group_index * width
        copy = low_back(source)
        q_pieces.append(product(copy, q_weight[:, start:start + width]))
        k_pieces.append(product(copy, k_weight[:, start:start + width]))
        v_pieces.append(product(copy, v_weight[:, start:start + width]))
    return (jnp.concatenate(q_pieces, axis=-1), jnp.concatenate(k_pieces, axis=-1), jnp.concatenate(v_pieces, axis=-1))

def block(params, group_images, group_flags):
    ln1_gain, ln1_bias, q_weight, q_bias, k_weight, v_weight, v_bias, o_weight, o_bias, ln2_gain, ln2_bias, fc1_weight, fc1_bias, fc2_weight, fc2_bias = params
    batch_size = group_images.shape[0]
    shaped = (batch_size, SEQ, HEADS, HDIM)
    first = low(layer_norm(group_images, ln1_gain, ln1_bias))
    q_raw, k_raw, v_raw = group_qkv(first, q_weight, k_weight, v_weight)
    query = low_back(low(q_raw + q_bias)).reshape(shaped)
    keys = low_back(low(k_raw)).reshape(shaped)
    values = low_back(low(v_raw + v_bias)).reshape(shaped)
    scores = low_back(jnp.einsum('nqhd,nkhd->nhqk', query, keys, precision=HIGHEST_PREC) / math.sqrt(HDIM))
    probs = low(jax.nn.softmax(scores, axis=-1))
    mixed = jnp.einsum('nhqk,nkhd->nqhd', probs, values, precision=HIGHEST_PREC)
    context = low_back(low(mixed.reshape(batch_size, SEQ, HEADS * HDIM)))
    resid = group_images + low_back(part_sum(context, o_weight)) + o_bias
    second = low(layer_norm(resid, ln2_gain, ln2_bias))
    hidden_pre = low_back(group_cols(second, fc1_weight) + fc1_bias)
    active = low(gelu_tanh(hidden_pre))
    result = resid + part_sum(active, fc2_weight) + fc2_bias
    return result * group_flags[:, None, None]

def reference(images, valid_flags, cotangent, ln1_gain, ln1_bias, q_weight, q_bias, k_weight, v_weight, v_bias, o_weight, o_bias, ln2_gain, ln2_bias, fc1_weight, fc1_bias, fc2_weight, fc2_bias):
    params = tuple((weight_arr.astype(jnp.float32) for weight_arr in (ln1_gain, ln1_bias, q_weight, q_bias, k_weight, v_weight, v_bias, o_weight, o_bias, ln2_gain, ln2_bias, fc1_weight, fc1_bias, fc2_weight, fc2_bias)))
    flag_values = valid_flags.astype(jnp.float32)
    group = 4 if IMAGES % 4 == 0 else 1

    def forward(weights, data):
        stacked = data.reshape(IMAGES // group, group, SEQ, D)
        flag_groups = flag_values.reshape(IMAGES // group, group)

        def run_group(packed):
            return block(weights, packed[0], packed[1])
        results = lax.map(jax.checkpoint(run_group), (stacked, flag_groups))
        return results.reshape(IMAGES, SEQ, D)
    result, pullback = jax.vjp(forward, params, images.astype(jnp.float32))
    grads, image_grad = pullback(cotangent.astype(jnp.float32))
    return (result.astype(jnp.bfloat16), image_grad.astype(jnp.bfloat16), grads[0], grads[1], grads[2], grads[3], grads[4], grads[5], grads[6], grads[7], grads[8], grads[9], grads[10], grads[11], grads[12], grads[13], grads[14])
```

```python
import functools
import math

import jax
import jax.numpy as jnp
from jax import lax
from jax.experimental import pallas as pl
from jax.experimental.pallas import tpu as pltpu
from jax.sharding import PartitionSpec as P

HDIM = 72
MICRO = 2


EPS = 1e-06
GELU_C = math.sqrt(2.0 / math.pi)
GELU_A = 0.044715


def matmul(left, right):
    return jnp.dot(left, right, preferred_element_type=jnp.float32)


def left_transposed(left, right):
    return lax.dot_general(
        left, right, (((0,), (0,)), ((), ())), preferred_element_type=jnp.float32
    )


def right_transposed(left, right):
    return lax.dot_general(
        left, right, (((1,), (1,)), ((), ())), preferred_element_type=jnp.float32
    )


def rounded(values):
    return values.astype(jnp.bfloat16).astype(jnp.float32)


def norm_rows(values):
    feat_total = values.shape[1] * lax.axis_size("tensor")
    row_sum, row_square = lax.psum(
        (jnp.sum(values, axis=1), jnp.sum(values * values, axis=1)), "tensor"
    )
    row_mean = row_sum / feat_total
    row_var = row_square / feat_total - row_mean * row_mean
    inverse = lax.rsqrt(row_var + EPS)
    normed = (values - row_mean[:, None]) * inverse[:, None]
    return (normed, inverse)


def norm_back(grad_normed, normed, inverse, gain_vec):
    feat_total = normed.shape[1] * lax.axis_size("tensor")
    scaled = grad_normed * gain_vec.astype(jnp.float32)
    sum_plain, sum_cross = lax.psum(
        (jnp.sum(scaled, axis=1), jnp.sum(scaled * normed, axis=1)), "tensor"
    )
    return inverse[:, None] * (
        scaled - sum_plain[:, None] / feat_total - normed * (sum_cross[:, None] / feat_total)
    )


def gather_rows(shard):
    return lax.all_gather(shard, "tensor", axis=1, tiled=True)


def gather_grads(shard):
    return lax.all_gather(shard, "tensor", axis=1, tiled=True)


def gelu_parts(pre):
    tanh_val = jnp.tanh(GELU_C * (pre + GELU_A * pre * pre * pre))
    value = 0.5 * pre * (1.0 + tanh_val)
    slope = 0.5 * (1.0 + tanh_val) + 0.5 * pre * (1.0 - tanh_val * tanh_val) * GELU_C * (
        1.0 + 3.0 * GELU_A * pre * pre
    )
    return (value, slope)


def split_device(
    images,
    valid_flags,
    cotangent,
    ln1_gain,
    ln1_bias,
    q_weight,
    q_bias,
    k_weight,
    v_weight,
    v_bias,
    o_weight,
    o_bias,
    ln2_gain,
    ln2_bias,
    fc1_weight,
    fc1_bias,
    fc2_weight,
    fc2_bias,
):
    img_local, seq_len, feat_local = images.shape
    per_micro = img_local // MICRO
    rows = per_micro * seq_len
    head_local = q_weight.shape[1] // HDIM
    scale = 1.0 / math.sqrt(HDIM)
    shaped = (per_micro, seq_len, head_local, HDIM)
    split_images = images.reshape(per_micro, MICRO, seq_len, feat_local)
    split_cot = cotangent.reshape(per_micro, MICRO, seq_len, feat_local)
    split_flags = valid_flags.reshape(per_micro, MICRO).astype(jnp.float32)
    param_list = (
        ln1_gain,
        ln1_bias,
        q_weight,
        q_bias,
        k_weight,
        v_weight,
        v_bias,
        o_weight,
        o_bias,
        ln2_gain,
        ln2_bias,
        fc1_weight,
        fc1_bias,
        fc2_weight,
        fc2_bias,
    )
    totals = tuple((jnp.zeros(weight_arr.shape, jnp.float32) for weight_arr in param_list))
    out_list = []
    grad_list = []
    for micro_index in range(MICRO):
        flag_rows = jnp.repeat(split_flags[:, micro_index], seq_len)[:, None]
        inputs = split_images[:, micro_index].reshape(rows, feat_local).astype(jnp.float32)
        normed1, inverse1 = norm_rows(inputs)
        low_first = (normed1 * ln1_gain + ln1_bias).astype(jnp.bfloat16)
        full_first = gather_rows(low_first)
        query = (matmul(full_first, q_weight) + q_bias).astype(jnp.bfloat16)
        keys = matmul(full_first, k_weight).astype(jnp.bfloat16)
        values = (matmul(full_first, v_weight) + v_bias).astype(jnp.bfloat16)
        query4 = query.reshape(shaped)
        keys4 = keys.reshape(shaped)
        values4 = values.reshape(shaped)
        scores = (
            jnp.einsum("nqhd,nkhd->nhqk", query4, keys4, preferred_element_type=jnp.float32) * scale
        )
        log_total = jax.nn.logsumexp(scores, axis=-1)
        probs_low = jnp.exp(scores - log_total[..., None]).astype(jnp.bfloat16)
        mixed = jnp.einsum(
            "nhqk,nkhd->nqhd", probs_low, values4, preferred_element_type=jnp.float32
        )
        context = mixed.reshape(rows, head_local * HDIM).astype(jnp.bfloat16)
        attended = lax.psum_scatter(
            rounded(matmul(context, o_weight)).astype(jnp.bfloat16),
            "tensor",
            scatter_dimension=1,
            tiled=True,
        ).astype(jnp.float32)
        resid = inputs + attended + o_bias
        normed2, inverse2 = norm_rows(resid)
        low_second = (normed2 * ln2_gain + ln2_bias).astype(jnp.bfloat16)
        full_second = gather_rows(low_second)
        hidden_pre = matmul(full_second, fc1_weight) + fc1_bias
        act_value, act_slope = gelu_parts(hidden_pre)
        act_low = act_value.astype(jnp.bfloat16)
        branch = lax.psum_scatter(
            rounded(matmul(act_low, fc2_weight)).astype(jnp.bfloat16),
            "tensor",
            scatter_dimension=1,
            tiled=True,
        ).astype(jnp.float32)
        layer_rows = (resid + branch + fc2_bias) * flag_rows
        out_list.append(layer_rows.astype(jnp.bfloat16).reshape(per_micro, seq_len, feat_local))
        grad_out = (
            split_cot[:, micro_index].reshape(rows, feat_local).astype(jnp.float32) * flag_rows
        )
        grad_full = gather_grads(grad_out.astype(jnp.bfloat16))
        g_fc2w = left_transposed(act_low, grad_full)
        g_fc2b = jnp.sum(grad_out, axis=0)
        hidden_grad = (right_transposed(grad_full, fc2_weight) * act_slope).astype(jnp.bfloat16)
        g_fc1w = left_transposed(full_second, hidden_grad)
        g_fc1b = jnp.sum(hidden_grad.astype(jnp.float32), axis=0)
        grad_second = lax.psum_scatter(
            rounded(right_transposed(hidden_grad, fc1_weight)).astype(jnp.bfloat16),
            "tensor",
            scatter_dimension=1,
            tiled=True,
        ).astype(jnp.float32)
        g_ln2g = jnp.sum(grad_second * normed2, axis=0)
        g_ln2b = jnp.sum(grad_second, axis=0)
        grad_resid = grad_out + norm_back(grad_second, normed2, inverse2, ln2_gain)
        g_ob = jnp.sum(grad_resid, axis=0)
        resid_full = gather_grads(grad_resid.astype(jnp.bfloat16))
        g_ow = left_transposed(context, resid_full)
        grad_context = right_transposed(resid_full, o_weight).astype(jnp.bfloat16)
        context4 = grad_context.reshape(shaped)
        probs = jnp.exp(
            jnp.einsum("nqhd,nkhd->nhqk", query4, keys4, preferred_element_type=jnp.float32) * scale
            - log_total[..., None]
        )
        probs_again = probs.astype(jnp.bfloat16)
        grad_probs = jnp.einsum(
            "nqhd,nkhd->nhqk", context4, values4, preferred_element_type=jnp.float32
        )
        row_delta = jnp.sum(probs * grad_probs, axis=-1)
        grad_scores = (probs * (grad_probs - row_delta[..., None])).astype(jnp.bfloat16)
        grad_query = (
            (
                jnp.einsum(
                    "nhqk,nkhd->nqhd", grad_scores, keys4, preferred_element_type=jnp.float32
                )
                * scale
            )
            .reshape(rows, head_local * HDIM)
            .astype(jnp.bfloat16)
        )
        grad_keys = (
            (
                jnp.einsum(
                    "nhqk,nqhd->nkhd", grad_scores, query4, preferred_element_type=jnp.float32
                )
                * scale
            )
            .reshape(rows, head_local * HDIM)
            .astype(jnp.bfloat16)
        )
        grad_values = (
            jnp.einsum("nhqk,nqhd->nkhd", probs_again, context4, preferred_element_type=jnp.float32)
            .reshape(rows, head_local * HDIM)
            .astype(jnp.bfloat16)
        )
        g_qw = left_transposed(full_first, grad_query)
        g_qb = jnp.sum(grad_query.astype(jnp.float32), axis=0)
        g_kw = left_transposed(full_first, grad_keys)
        g_vw = left_transposed(full_first, grad_values)
        g_vb = jnp.sum(grad_values.astype(jnp.float32), axis=0)
        partial_first = (
            right_transposed(grad_query, q_weight)
            + right_transposed(grad_keys, k_weight)
            + right_transposed(grad_values, v_weight)
        )
        grad_first = lax.psum_scatter(
            rounded(partial_first).astype(jnp.bfloat16), "tensor", scatter_dimension=1, tiled=True
        ).astype(jnp.float32)
        g_ln1g = jnp.sum(grad_first * normed1, axis=0)
        g_ln1b = jnp.sum(grad_first, axis=0)
        grad_input = grad_resid + norm_back(grad_first, normed1, inverse1, ln1_gain)
        grad_list.append(grad_input.astype(jnp.bfloat16).reshape(per_micro, seq_len, feat_local))
        micro_grads = (
            g_ln1g,
            g_ln1b,
            g_qw,
            g_qb,
            g_kw,
            g_vw,
            g_vb,
            g_ow,
            g_ob,
            g_ln2g,
            g_ln2b,
            g_fc1w,
            g_fc1b,
            g_fc2w,
            g_fc2b,
        )
        totals = jax.tree.map(jnp.add, totals, micro_grads)
    totals = (
        lax.psum(totals[0].astype(jnp.bfloat16), "dp").astype(jnp.float32),
        lax.psum(totals[1].astype(jnp.bfloat16), "dp").astype(jnp.float32),
        lax.psum(totals[2].astype(jnp.bfloat16), "dp").astype(jnp.float32),
        lax.psum(totals[3].astype(jnp.bfloat16), "dp").astype(jnp.float32),
        lax.psum(totals[4].astype(jnp.bfloat16), "dp").astype(jnp.float32),
        lax.psum(totals[5].astype(jnp.bfloat16), "dp").astype(jnp.float32),
        lax.psum(totals[6].astype(jnp.bfloat16), "dp").astype(jnp.float32),
        lax.psum(totals[7].astype(jnp.bfloat16), "dp").astype(jnp.float32),
        lax.psum(totals[8].astype(jnp.bfloat16), "dp").astype(jnp.float32),
        lax.psum(totals[9].astype(jnp.bfloat16), "dp").astype(jnp.float32),
        lax.psum(totals[10].astype(jnp.bfloat16), "dp").astype(jnp.float32),
        lax.psum(totals[11].astype(jnp.bfloat16), "dp").astype(jnp.float32),
        lax.psum(totals[12].astype(jnp.bfloat16), "dp").astype(jnp.float32),
        lax.psum(totals[13].astype(jnp.bfloat16), "dp").astype(jnp.float32),
        lax.psum(totals[14].astype(jnp.bfloat16), "dp").astype(jnp.float32),
    )
    layer_out = jnp.stack(out_list, axis=1).reshape(img_local, seq_len, feat_local)
    input_grad = jnp.stack(grad_list, axis=1).reshape(img_local, seq_len, feat_local)
    return (
        layer_out,
        input_grad,
        totals[0],
        totals[1],
        totals[2],
        totals[3],
        totals[4],
        totals[5],
        totals[6],
        totals[7],
        totals[8],
        totals[9],
        totals[10],
        totals[11],
        totals[12],
        totals[13],
        totals[14],
    )


F32 = jnp.float32
BF16 = jnp.bfloat16
LOG2E = math.log2(math.e)
VMEM_BYTES = 58 * 1024 * 1024
COST_SHARE = 0.02


def dot_nn(left, right):
    return jnp.dot(left, right, preferred_element_type=F32)


def dot_nt(left, right):
    return lax.dot_general(left, right, (((1,), (1,)), ((), ())), preferred_element_type=F32)


def dot_tn(left, right):
    return lax.dot_general(left, right, (((0,), (0,)), ((), ())), preferred_element_type=F32)


def cost(flops, moved, trans=0):
    return pl.CostEstimate(
        flops=int(flops * COST_SHARE),
        bytes_accessed=int(moved * COST_SHARE),
        transcendentals=int(trans * COST_SHARE),
    )


def params(grid_dims):
    return pltpu.CompilerParams(
        dimension_semantics=("arbitrary",) * grid_dims, vmem_limit_bytes=VMEM_BYTES
    )


def once(shape, spot=None):
    spot = spot or (0,) * len(shape)
    return pl.BlockSpec(shape, lambda *_: spot, pipeline_mode=pl.Buffered(1))


def image_block(shape, offset=0):
    return pl.BlockSpec((1,) + shape, lambda i, *_: (offset + i, 0, 0))


ANYWHERE = pl.BlockSpec(memory_space=pl.ANY)


def column_stats(values):
    mean = jnp.mean(values, axis=0, keepdims=True)
    centred = values - mean
    inverse = lax.rsqrt(jnp.mean(centred * centred, axis=0, keepdims=True) + EPS)
    return centred * inverse, inverse


def join_halves(first, own, other):
    return jnp.concatenate(
        [jnp.where(first, own, other), jnp.where(first, other, own)], axis=0
    )


def split_halves(first, full):
    half = full.shape[0] // 2
    low, high = full[:half], full[half:]
    return jnp.where(first, low, high), jnp.where(first, high, low)


def token_sum(values):
    return jnp.sum(values, axis=1, keepdims=True)


LN1_GAIN, LN1_BIAS, O_BIAS, LN2_GAIN, LN2_BIAS, FC2_BIAS = range(6)


def as_row(column_sum):
    rows = column_sum.shape[0]
    return jnp.broadcast_to(column_sum, (rows, 128)).T[0:1]


def column(ref, index):
    return ref[:, index : index + 1]


def write_rows(row_refs, sum_refs):
    @pl.when(pl.program_id(0) == pl.num_programs(0) - 1)
    def _():
        for row_ref, sum_ref in zip(row_refs, sum_refs):
            row_ref[...] = as_row(sum_ref[...])


def store_heads(out_ref, first, product):
    head_dim = out_ref.shape[2]
    for head in range(product.shape[0] // head_dim):
        out_ref[0, first + head] = product[head * head_dim : (head + 1) * head_dim].astype(BF16)


def first_norm_kernel(
    place_ref, own_ref, other_ref, feature_ref, q_ref, k_ref, v_ref, head_ref, *rest
):
    rows_ref, normed_ref, qkv_ref = rest[-3:]
    full = join_halves(place_ref[0] == 0, own_ref[0].astype(F32), other_ref[0].astype(F32))
    rows_ref[0] = full.astype(BF16)
    normed, _ = column_stats(full)
    low = (normed * column(feature_ref, LN1_GAIN) + column(feature_ref, LN1_BIAS)).astype(BF16)
    normed_ref[0] = low
    heads = qkv_ref.shape[1] // 3
    store_heads(qkv_ref, 0, dot_nn(q_ref[...], low) + column(head_ref, 0))
    store_heads(qkv_ref, heads, dot_nn(k_ref[...], low))
    store_heads(qkv_ref, 2 * heads, dot_nn(v_ref[...], low) + column(head_ref, 1))


def first_norm(index, count, place, images, other, features, weights, head_vectors, earlier):
    _, half, seq = images.shape
    width, feat = weights[0].shape
    groups = 3 * width // HDIM
    held = list(earlier) if earlier else []
    return pl.pallas_call(
        first_norm_kernel,
        out_shape=[
            jax.ShapeDtypeStruct((count, feat, seq), BF16),
            jax.ShapeDtypeStruct((count, feat, seq), BF16),
            jax.ShapeDtypeStruct((count, groups, HDIM, seq), BF16),
        ],
        grid_spec=pltpu.PrefetchScalarGridSpec(
            num_scalar_prefetch=1,
            grid=(1,),
            in_specs=[
                pl.BlockSpec((1, half, seq), lambda i, p: (p[0] * count + index, 0, 0)),
                once((1, half, seq)),
                once((feat, 8)),
                once((width, feat)),
                once((width, feat)),
                once((width, feat)),
                once((width, 8)),
            ]
            + [ANYWHERE] * len(held),
            out_specs=[
                once((1, feat, seq), (index, 0, 0)),
                once((1, feat, seq), (index, 0, 0)),
                once((1, groups, HDIM, seq), (index, 0, 0, 0)),
            ],
        ),
        input_output_aliases={8 + k: k for k in range(len(held))},
        compiler_params=params(1),
        cost_estimate=cost(6 * seq * feat * width, 12 << 20),
        name="first_norm",
    )(place, images, other, features, *weights, head_vectors, *held)


def project_kernel(normed_ref, q_ref, k_ref, v_ref, head_ref, qkv_ref):
    low = normed_ref[0]
    heads = qkv_ref.shape[1] // 3
    store_heads(qkv_ref, 0, dot_nn(q_ref[...], low) + column(head_ref, 2))
    store_heads(qkv_ref, heads, dot_nn(k_ref[...], low))
    store_heads(qkv_ref, 2 * heads, dot_nn(v_ref[...], low) + column(head_ref, 3))


def project(normed, weight, head_vectors, width):
    count, feat, seq = normed.shape
    groups = 3 * width // HDIM
    return pl.pallas_call(
        project_kernel,
        grid=(count,),
        out_shape=jax.ShapeDtypeStruct((count, groups, HDIM, seq), BF16),
        in_specs=[
            image_block((feat, seq)),
            once((width, feat), (0, 0)),
            once((width, feat), (1, 0)),
            once((width, feat), (2, 0)),
            once((width, 8)),
        ],
        out_specs=pl.BlockSpec((1, groups, HDIM, seq), lambda i: (i, 0, 0, 0)),
        compiler_params=params(1),
        cost_estimate=cost(6 * count * seq * feat * width, 20 << 20),
        name="project",
    )(normed, weight, weight, weight, head_vectors)


def mix_kernel(q_ref, k_ref, v_ref, *rest, scale):
    out_ref, log_ref = rest[-2:]
    factor = scale * LOG2E
    for head in range(q_ref.shape[1]):
        scores = dot_tn(k_ref[0, head], q_ref[0, head])
        top = jnp.max(scores, axis=0, keepdims=True)
        probs = jnp.exp2((scores - top) * factor)
        total = jnp.sum(probs, axis=0, keepdims=True)
        mixed = dot_nn(v_ref[0, head], probs.astype(BF16))
        out_ref[0, head] = (mixed * (1.0 / total)).astype(BF16)
        log_ref[0, head] = top * factor + jnp.log2(total)


def mix(qkv, half, start, steps, earlier, per_step=1):
    count, groups, head_dim, seq = qkv.shape
    heads = groups // 3
    blocks = heads // per_step
    block = (1, per_step, head_dim, seq)
    held = list(earlier) if earlier else []

    def at(offset):
        return pl.BlockSpec(block, lambda i, j: (start + i, offset + j, 0, 0))

    return pl.pallas_call(
        functools.partial(mix_kernel, scale=1.0 / math.sqrt(head_dim)),
        grid=(steps, blocks),
        out_shape=[
            jax.ShapeDtypeStruct((count, 2 * heads, head_dim, seq), BF16),
            jax.ShapeDtypeStruct((count, 2 * heads, 1, seq), F32),
        ],
        in_specs=[at(0), at(blocks), at(2 * blocks)] + [ANYWHERE] * len(held),
        out_specs=[
            at(half * blocks),
            pl.BlockSpec(
                (1, per_step, 1, seq), lambda i, j: (start + i, half * blocks + j, 0, 0)
            ),
        ],
        input_output_aliases={3 + k: k for k in range(len(held))},
        compiler_params=params(2),
        cost_estimate=cost(
            4 * steps * heads * seq * seq * 256,
            steps * heads * head_dim * seq * 8,
            steps * heads * seq * seq,
        ),
        name="mix",
    )(qkv, qkv, qkv, *held)


def mix_back_kernel(q_ref, k_ref, v_ref, out_ref, log_ref, grad_ref, *rest, scale, heads):
    d_ref = rest[-1]
    factor = scale * LOG2E
    per_step = q_ref.shape[1]
    first = pl.program_id(1) * per_step
    for head in range(per_step):
        query, keys, values = q_ref[0, head], k_ref[0, head], v_ref[0, head]
        grad = grad_ref[0, head]
        delta = jnp.sum(grad.astype(F32) * out_ref[0, head].astype(F32), axis=0, keepdims=True)
        probs = jnp.exp2(dot_tn(keys, query) * factor - log_ref[0, head])
        grad_scores = (probs * (dot_tn(values, grad) - delta)).astype(BF16)
        d_ref[0, 2 * heads + first + head] = dot_nt(grad, probs.astype(BF16)).astype(BF16)
        d_ref[0, first + head] = (dot_nn(keys, grad_scores) * scale).astype(BF16)
        d_ref[0, heads + first + head] = (dot_nt(query, grad_scores) * scale).astype(BF16)


def mix_back(qkv, out, log_total, grad, half, start, steps, earlier, per_step=2):
    count, groups, head_dim, seq = qkv.shape
    heads = groups // 3
    blocks = heads // per_step
    block = (1, per_step, head_dim, seq)
    held = [] if earlier is None else [earlier]

    def at(offset):
        return pl.BlockSpec(block, lambda i, j: (start + i, offset + j, 0, 0))

    return pl.pallas_call(
        functools.partial(mix_back_kernel, scale=1.0 / math.sqrt(head_dim), heads=heads),
        grid=(steps, blocks),
        out_shape=jax.ShapeDtypeStruct(qkv.shape, BF16),
        in_specs=[
            at(0),
            at(blocks),
            at(2 * blocks),
            at(half * blocks),
            pl.BlockSpec((1, per_step, 1, seq), lambda i, j: (start + i, half * blocks + j, 0, 0)),
            at(half * blocks),
        ]
        + [ANYWHERE] * len(held),
        input_output_aliases={6: 0} if held else {},
        out_specs=pl.BlockSpec((1, groups, head_dim, seq), lambda i, j: (start + i, 0, 0, 0)),
        compiler_params=params(2),
        cost_estimate=cost(
            10 * steps * heads * seq * seq * 256,
            steps * heads * head_dim * seq * 16,
            steps * heads * seq * seq,
        ),
        name="mix_back",
    )(qkv, qkv, qkv, out, log_total, grad, *held)


def second_norm_kernel(
    place_ref,
    ctx_ref,
    w_own_ref,
    w_other_ref,
    rows_ref,
    feature_ref,
    cot_own_ref,
    cot_other_ref,
    resid_ref,
    low_ref,
    grad_ref,
    row_ref,
    w_ref,
    sum_ref,
):
    step = pl.program_id(0)
    half = w_own_ref.shape[0]

    @pl.when(step == 0)
    def _():
        w_ref[:half] = w_own_ref[...]
        w_ref[half:] = w_other_ref[...]
        sum_ref[...] = jnp.zeros_like(sum_ref)

    resid = rows_ref[0].astype(F32) + dot_tn(w_ref[...], ctx_ref[0])
    resid += column(feature_ref, O_BIAS)
    resid_ref[0] = resid
    normed, _ = column_stats(resid)
    low_ref[0] = (
        normed * column(feature_ref, LN2_GAIN) + column(feature_ref, LN2_BIAS)
    ).astype(BF16)
    flag = place_ref[2 + place_ref[0] * pl.num_programs(0) + step].astype(F32)
    grad = flag * join_halves(
        place_ref[0] == 0, cot_own_ref[0].astype(F32), cot_other_ref[0].astype(F32)
    )
    grad_ref[0] = grad.astype(BF16)
    sum_ref[...] += token_sum(grad)
    write_rows((row_ref,), (sum_ref,))


def second_norm(place, ctx, w_own, w_other, rows, features, cot, cot_other):
    count, feat, seq = rows.shape
    half = w_own.shape[0]
    full = image_block((feat, seq))
    return pl.pallas_call(
        second_norm_kernel,
        out_shape=[
            jax.ShapeDtypeStruct((count, feat, seq), F32),
            jax.ShapeDtypeStruct((count, feat, seq), BF16),
            jax.ShapeDtypeStruct((count, feat, seq), BF16),
            jax.ShapeDtypeStruct((1, feat), F32),
        ],
        grid_spec=pltpu.PrefetchScalarGridSpec(
            num_scalar_prefetch=1,
            grid=(count,),
            in_specs=[
                full,
                once((half, feat)),
                once((half, feat), (3, 0)),
                full,
                once((feat, 8)),
                pl.BlockSpec((1, feat // 2, seq), lambda i, p: (p[0] * count + i, 0, 0)),
                image_block((feat // 2, seq)),
            ],
            out_specs=[full, full, full, once((1, feat))],
            scratch_shapes=[pltpu.VMEM((feat, feat), BF16), pltpu.VMEM((feat, 1), F32)],
        ),
        compiler_params=params(1),
        cost_estimate=cost(4 * count * seq * half * feat, 40 << 20),
        name="second_norm",
    )(place, ctx, w_own, w_other, rows, features, cot, cot_other)


def hidden_kernel(place_ref, low_ref, grad_ref, fc1_ref, fc2_ref, bias_ref, *rest, which):
    act_ref, back_ref, gb_ref, g1_ref, g2_ref = rest[-5:]
    g1, g2, gb = None, None, None
    for image in range(low_ref.shape[0]):
        low, grad = low_ref[image], grad_ref[image]
        pre = dot_nn(fc1_ref[...], low) + column(bias_ref, which)
        square = pre * pre
        tanh_val = jnp.tanh(pre * (GELU_C + (GELU_C * GELU_A) * square))
        half = 0.5 * tanh_val + 0.5
        act = pre * half
        slope = half + act * (1.0 - half) * (2 * GELU_C + (6 * GELU_C * GELU_A) * square)
        act = act.astype(BF16)
        act_ref[image] = act
        back = (dot_nn(fc2_ref[...], grad) * slope).astype(BF16)
        back_ref[image] = back
        parts = dot_nt(back, low), dot_nt(act, grad), token_sum(back.astype(F32))
        g1 = parts[0] if g1 is None else g1 + parts[0]
        g2 = parts[1] if g2 is None else g2 + parts[1]
        gb = parts[2] if gb is None else gb + parts[2]
    gb_ref[...] = gb
    g1_ref[...] = g1.astype(BF16)
    g2_ref[...] = g2.astype(BF16)


def quarter_rows(hidden):
    return (-(-hidden // 4) + 7) // 8 * 8


def hidden_stage(keep, place, low, grad, fc1, fc2, fc2_offset, bias, which, earlier):
    count, feat, seq = low.shape
    hidden = bias.shape[0]
    block = quarter_rows(hidden)
    held = list(earlier) if earlier else []

    def chunk(j, p):
        return j + 2 * (p[1] if keep else 1 - p[1])

    weight = pl.BlockSpec((block, feat), lambda j, p: (chunk(j, p), 0))
    tokens = pl.BlockSpec((count, block, seq), lambda j, p: (0, chunk(j, p), 0))
    grads = pl.BlockSpec((block, feat), lambda j, p: (j, 0))
    part = jax.ShapeDtypeStruct((2 * block, feat), BF16)
    return pl.pallas_call(
        functools.partial(hidden_kernel, which=which),
        out_shape=[
            jax.ShapeDtypeStruct((count, hidden, seq), BF16),
            jax.ShapeDtypeStruct((count, hidden, seq), BF16),
            jax.ShapeDtypeStruct((hidden, 1), F32),
            part,
            part,
        ],
        grid_spec=pltpu.PrefetchScalarGridSpec(
            num_scalar_prefetch=1,
            grid=(2,),
            in_specs=[
                once((count, feat, seq)),
                once((count, feat, seq)),
                weight,
                pl.BlockSpec((block, feat), lambda j, p: (fc2_offset + chunk(j, p), 0)),
                pl.BlockSpec((block, 2), lambda j, p: (chunk(j, p), 0)),
            ]
            + [ANYWHERE] * len(held),
            out_specs=[
                tokens,
                tokens,
                pl.BlockSpec((block, 1), lambda j, p: (chunk(j, p), 0)),
                grads,
                grads,
            ],
        ),
        input_output_aliases={6 + k: k for k in range(len(held))},
        compiler_params=params(1),
        cost_estimate=cost(4 * count * seq * feat * hidden, 30 << 20, count * seq * hidden // 2),
        name="hidden_stage",
    )(place, low, grad, fc1, fc2, bias, *held)


def layer_kernel(
    place_ref, act_own_ref, act_other_ref, w_own_ref, w_other_ref, resid_ref, b_ref, out_ref, send_ref
):
    hidden = act_own_ref.shape[1]
    branch = dot_tn(w_own_ref[:hidden], act_own_ref[0])
    branch += dot_tn(w_other_ref[:hidden], act_other_ref[0])
    flag = place_ref[2 + place_ref[0] * pl.num_programs(0) + pl.program_id(0)].astype(F32)
    result = (resid_ref[0] + branch + column(b_ref, FC2_BIAS)) * flag
    own, other = split_halves(place_ref[0] == 0, result)
    out_ref[0] = own.astype(BF16)
    send_ref[0] = other.astype(BF16)


def layer_result(place, act_own, act_other, w_own, w_other, resid, bias):
    count, feat, seq = resid.shape
    hidden = act_own.shape[1]
    full = image_block((hidden, seq))
    padded = 4 * quarter_rows(hidden)
    return pl.pallas_call(
        layer_kernel,
        out_shape=[
            jax.ShapeDtypeStruct((2 * count, feat // 2, seq), BF16),
            jax.ShapeDtypeStruct((count, feat // 2, seq), BF16),
        ],
        grid_spec=pltpu.PrefetchScalarGridSpec(
            num_scalar_prefetch=1,
            grid=(count,),
            in_specs=[
                full,
                full,
                once((hidden, feat)),
                once((padded, feat), (1, 0)),
                image_block((feat, seq)),
                once((feat, 8)),
            ],
            out_specs=[
                pl.BlockSpec((1, feat // 2, seq), lambda i, p: (p[0] * count + i, 0, 0)),
                image_block((feat // 2, seq)),
            ],
        ),
        compiler_params=params(1),
        cost_estimate=cost(4 * count * seq * feat * hidden, 45 << 20),
        name="layer_result",
    )(place, act_own, act_other, w_own, w_other, resid, bias)


def resid_back_kernel(
    back_own_ref,
    back_other_ref,
    w_own_ref,
    w_other_ref,
    resid_ref,
    grad_ref,
    gain_ref,
    low_ref,
    row_gain_ref,
    row_bias_ref,
    row_ob_ref,
    sum_gain_ref,
    sum_bias_ref,
    sum_ob_ref,
):
    hidden = back_own_ref.shape[1]
    grad_norm = dot_tn(w_own_ref[:hidden], back_own_ref[0])
    grad_norm += dot_tn(w_other_ref[:hidden], back_other_ref[0])
    normed, inverse = column_stats(resid_ref[0])
    scaled = grad_norm * column(gain_ref, LN2_GAIN)
    plain = jnp.mean(scaled, axis=0, keepdims=True)
    cross = jnp.mean(scaled * normed, axis=0, keepdims=True)
    grad = grad_ref[0].astype(F32) + inverse * (scaled - plain - normed * cross)
    low_ref[0] = grad.astype(BF16)

    @pl.when(pl.program_id(0) == 0)
    def _():
        sum_gain_ref[...] = jnp.zeros_like(sum_gain_ref)
        sum_bias_ref[...] = jnp.zeros_like(sum_bias_ref)
        sum_ob_ref[...] = jnp.zeros_like(sum_ob_ref)

    sum_gain_ref[...] += token_sum(grad_norm * normed)
    sum_bias_ref[...] += token_sum(grad_norm)
    sum_ob_ref[...] += token_sum(grad)
    write_rows((row_gain_ref, row_bias_ref, row_ob_ref), (sum_gain_ref, sum_bias_ref, sum_ob_ref))


def resid_back(back_own, back_other, w_own, w_other, resid, grad, gain):
    count, feat, seq = resid.shape
    hidden = back_own.shape[1]
    padded = 4 * quarter_rows(hidden)
    wide = image_block((hidden, seq))
    full = image_block((feat, seq))
    return pl.pallas_call(
        resid_back_kernel,
        grid=(count,),
        out_shape=[jax.ShapeDtypeStruct((count, feat, seq), BF16)]
        + [jax.ShapeDtypeStruct((1, feat), F32)] * 3,
        in_specs=[
            wide,
            wide,
            once((hidden, feat)),
            once((padded, feat)),
            full,
            full,
            once((feat, 8)),
        ],
        out_specs=[full] + [once((1, feat))] * 3,
        scratch_shapes=[pltpu.VMEM((feat, 1), F32)] * 3,
        compiler_params=params(1),
        cost_estimate=cost(4 * count * seq * feat * hidden, 50 << 20),
        name="resid_back",
    )(back_own, back_other, w_own, w_other, resid, grad, gain)


def context_back_kernel(
    place_ref,
    low_ref,
    ctx_ref,
    w_own_ref,
    w_other_ref,
    d_ref,
    own_keep_ref,
    own_send_ref,
    other_keep_ref,
    other_send_ref,
    acc_ref,
):
    step = pl.program_id(0)
    low = low_ref[0]
    half = w_own_ref.shape[0]
    d_ref[0, :half] = dot_nn(w_own_ref[...], low).astype(BF16)
    d_ref[0, half:] = dot_nn(w_other_ref[...], low).astype(BF16)
    product = dot_nt(ctx_ref[0], low)

    @pl.when(step == 0)
    def _():
        acc_ref[...] = product

    @pl.when(step > 0)
    def _():
        acc_ref[...] += product

    @pl.when(step == pl.num_programs(0) - 1)
    def _():
        part = half // 2
        keep = place_ref[1] * part
        send = part - keep
        own_keep_ref[...] = acc_ref[pl.ds(pl.multiple_of(keep, 8), part)].astype(BF16)
        own_send_ref[...] = acc_ref[pl.ds(pl.multiple_of(send, 8), part)].astype(BF16)
        other_keep_ref[...] = acc_ref[pl.ds(pl.multiple_of(half + keep, 8), part)].astype(BF16)
        other_send_ref[...] = acc_ref[pl.ds(pl.multiple_of(half + send, 8), part)].astype(BF16)


def context_back(place, low, ctx, w_own, w_other):
    count, feat, seq = low.shape
    half = w_own.shape[0]
    full = image_block((feat, seq))
    part = jax.ShapeDtypeStruct((half // 2, feat), BF16)
    return pl.pallas_call(
        context_back_kernel,
        out_shape=[jax.ShapeDtypeStruct((count, 2 * half, seq), BF16)] + [part] * 4,
        grid_spec=pltpu.PrefetchScalarGridSpec(
            num_scalar_prefetch=1,
            grid=(count,),
            in_specs=[
                full,
                image_block((2 * half, seq)),
                once((half, feat)),
                once((half, feat), (3, 0)),
            ],
            out_specs=[image_block((2 * half, seq))] + [once((half // 2, feat))] * 4,
            scratch_shapes=[pltpu.VMEM((2 * half, feat), F32)],
        ),
        compiler_params=params(1),
        cost_estimate=cost(8 * count * seq * half * feat, 25 << 20),
        name="context_back",
    )(place, low, ctx, w_own, w_other)


def project_back_kernel(place_ref, normed_ref, d_ref, keep_ref, send_ref, col_ref, acc_ref):
    step = pl.program_id(0)
    product = dot_nt(d_ref[0], normed_ref[0])
    column = token_sum(d_ref[0].astype(F32))

    @pl.when(step == 0)
    def _():
        acc_ref[...] = product
        col_ref[...] = column

    @pl.when(step > 0)
    def _():
        acc_ref[...] += product
        col_ref[...] += column

    @pl.when(step == pl.num_programs(0) - 1)
    def _():
        part = keep_ref.shape[0] // 3
        keep = place_ref[1] * part
        for index in range(3):
            rows = slice(index * part, (index + 1) * part)
            first = 2 * index * part
            keep_rows = pl.ds(pl.multiple_of(first + keep, 8), part)
            send_rows = pl.ds(pl.multiple_of(first + part - keep, 8), part)
            keep_ref[rows] = acc_ref[keep_rows].astype(BF16)
            send_ref[rows] = acc_ref[send_rows].astype(BF16)


def project_back(place, normed, d_qkv):
    count, feat, seq = normed.shape
    width = d_qkv.shape[1]
    part = jax.ShapeDtypeStruct((width // 2, feat), BF16)
    return pl.pallas_call(
        project_back_kernel,
        out_shape=[part, part, jax.ShapeDtypeStruct((width, 1), F32)],
        grid_spec=pltpu.PrefetchScalarGridSpec(
            num_scalar_prefetch=1,
            grid=(count,),
            in_specs=[image_block((feat, seq)), image_block((width, seq))],
            out_specs=[
                once((width // 2, feat)),
                once((width // 2, feat)),
                once((width, 1)),
            ],
            scratch_shapes=[pltpu.VMEM((width, feat), F32)],
        ),
        compiler_params=params(1),
        cost_estimate=cost(2 * count * seq * feat * width, 20 << 20),
        name="project_back",
    )(place, normed, d_qkv)


def input_back_kernel(
    place_ref,
    d_own_ref,
    d_other_ref,
    q_ref,
    k_ref,
    v_ref,
    w_other_ref,
    rows_ref,
    low_ref,
    gain_ref,
    out_ref,
    send_ref,
    row_gain_ref,
    row_bias_ref,
    w_ref,
    sum_gain_ref,
    sum_bias_ref,
):
    width = q_ref.shape[0]

    @pl.when(pl.program_id(0) == 0)
    def _():
        w_ref[:width] = q_ref[...]
        w_ref[width : 2 * width] = k_ref[...]
        w_ref[2 * width :] = v_ref[...]
        sum_gain_ref[...] = jnp.zeros_like(sum_gain_ref)
        sum_bias_ref[...] = jnp.zeros_like(sum_bias_ref)

    grad_norm = dot_tn(w_ref[...], d_own_ref[0]) + dot_tn(w_other_ref[...], d_other_ref[0])
    normed, inverse = column_stats(rows_ref[0].astype(F32))
    scaled = grad_norm * column(gain_ref, LN1_GAIN)
    plain = jnp.mean(scaled, axis=0, keepdims=True)
    cross = jnp.mean(scaled * normed, axis=0, keepdims=True)
    grad = low_ref[0].astype(F32) + inverse * (scaled - plain - normed * cross)
    own, other = split_halves(place_ref[0] == 0, grad)
    out_ref[0] = own.astype(BF16)
    send_ref[0] = other.astype(BF16)
    sum_gain_ref[...] += token_sum(grad_norm * normed)
    sum_bias_ref[...] += token_sum(grad_norm)
    write_rows((row_gain_ref, row_bias_ref), (sum_gain_ref, sum_bias_ref))


def input_back(place, d_own, d_other, weights, w_other, rows, low, gain):
    count, width, seq = d_own.shape
    feat = rows.shape[1]
    wide = image_block((width, seq))
    full = image_block((feat, seq))
    return pl.pallas_call(
        input_back_kernel,
        out_shape=[
            jax.ShapeDtypeStruct((2 * count, feat // 2, seq), BF16),
            jax.ShapeDtypeStruct((count, feat // 2, seq), BF16),
            jax.ShapeDtypeStruct((1, feat), F32),
            jax.ShapeDtypeStruct((1, feat), F32),
        ],
        grid_spec=pltpu.PrefetchScalarGridSpec(
            num_scalar_prefetch=1,
            grid=(count,),
            in_specs=[wide, wide]
            + [once((width // 3, feat))] * 3
            + [once((width, feat)), full, full, once((feat, 8))],
            out_specs=[
                pl.BlockSpec((1, feat // 2, seq), lambda i, p: (p[0] * count + i, 0, 0)),
                image_block((feat // 2, seq)),
                once((1, feat)),
                once((1, feat)),
            ],
            scratch_shapes=[
                pltpu.VMEM((width, feat), BF16),
                pltpu.VMEM((feat, 1), F32),
                pltpu.VMEM((feat, 1), F32),
            ],
        ),
        compiler_params=params(1),
        cost_estimate=cost(4 * count * seq * feat * width, 40 << 20),
        name="input_back",
    )(place, d_own, d_other, *weights, w_other, rows, low, gain)


def widen_kernel(place_ref, mine_ref, other_ref, out_ref):
    mine = pl.program_id(0) == place_ref[1]
    out_ref[...] = jnp.where(mine, mine_ref[...], other_ref[...]).astype(F32)


def widen(place, mine, other, offset, part, total, steps):
    feat = mine.shape[1]
    rows = part // steps
    spec = pl.BlockSpec((rows, feat), lambda h, i, p: (offset // rows + i, 0))
    return pl.pallas_call(
        widen_kernel,
        out_shape=jax.ShapeDtypeStruct((total, feat), F32),
        grid_spec=pltpu.PrefetchScalarGridSpec(
            num_scalar_prefetch=1,
            grid=(2, steps),
            in_specs=[spec, spec],
            out_specs=pl.BlockSpec((rows, feat), lambda h, i, p: (h * steps + i, 0)),
        ),
        compiler_params=params(2),
        cost_estimate=cost(0, 8 * total * feat),
        name="widen",
    )(place, mine, other)


def swap_tensor(value):
    return lax.ppermute(value, "tensor", [(0, 1), (1, 0)])


def swap_core(value):
    return lax.ppermute(value, "dp", [(spot, spot ^ 1) for spot in range(lax.axis_size("dp"))])


def other_weights(weights, spots, rows):
    per_weight = spots // len(weights)
    mine = lax.axis_index("dp")
    start = mine % per_weight * rows
    piece = None
    for index, weight in enumerate(weights):
        short = per_weight * rows - weight.shape[0]
        if short:
            weight = jnp.pad(weight, ((0, short), (0, 0)))
        part = lax.dynamic_slice_in_dim(weight, start, rows, 0)
        piece = part if piece is None else jnp.where(mine // per_weight == index, part, piece)
    return piece


def chip_groups(order):
    spots = lax.axis_size("dp")
    groups = [list(range(core, spots, 2)) for core in range(2)]
    if order == 1:
        return groups[::-1]
    return [group[::-1] for group in groups] if order == 2 else groups


def both(keep, send):
    return keep.astype(F32) + swap_core(send).astype(F32)


def after(value, *others):
    return lax.optimization_barrier((value, *others))[0]


def whole_device(
    images,
    valid_flags,
    cotangent,
    ln1_gain,
    ln1_bias,
    q_weight,
    q_bias,
    k_weight,
    v_weight,
    v_bias,
    o_weight,
    o_bias,
    ln2_gain,
    ln2_bias,
    fc1_weight,
    fc1_bias,
    fc2_weight,
    fc2_bias,
):
    img_local, seq, half = images.shape
    count = img_local // 2
    feat = 2 * half
    spots = lax.axis_size("dp")
    width = q_weight.shape[1]
    hidden = fc1_weight.shape[1]
    heads = width // HDIM
    tensor = lax.axis_index("tensor")
    core = lax.axis_index("dp") % 2
    place = jnp.concatenate(
        [jnp.stack([tensor, core]).astype(jnp.int32), valid_flags.astype(jnp.int32)]
    )
    images, cotangent = jnp.swapaxes(images, 1, 2), jnp.swapaxes(cotangent, 1, 2)
    in_weights = [q_weight.T, k_weight.T, v_weight.T]
    fc1_own = fc1_weight.T

    def to_other(array, index):
        return swap_tensor(
            lax.dynamic_slice_in_dim(array, (1 - tensor) * count + index, 1, 0)
        )

    small = jnp.concatenate(
        [ln1_gain, ln1_bias, o_bias, ln2_gain, ln2_bias, fc2_bias, q_bias, v_bias, fc1_bias]
    )
    cut_q, cut_v, cut_h = 6 * half, 6 * half + width, 6 * half + 2 * width
    block = quarter_rows(hidden)

    images_other = [to_other(images, 0)]
    small_other = swap_tensor(small)
    in_piece = other_weights([*in_weights, o_weight], spots, width // (spots // 4))
    in_piece = swap_tensor(after(in_piece, images_other[0]))
    images_other.append(to_other(after(images, images_other[0]), 1))
    mlp_piece = other_weights([fc1_own, fc2_weight], spots, block // 2)

    def features_of(source):
        return source[:cut_q].reshape(6, half)

    feature_own, feature_other = features_of(small), features_of(small_other)
    features = jnp.where(
        tensor == 0,
        jnp.concatenate([feature_own, feature_other], axis=1),
        jnp.concatenate([feature_other, feature_own], axis=1),
    )
    features = jnp.pad(features, ((0, 2), (0, 0))).astype(F32).T
    head_vectors = jnp.stack([small, small_other])[:, cut_q:cut_h].reshape(4, width)
    head_vectors = jnp.pad(head_vectors, ((0, 4), (0, 0))).astype(F32).T
    hidden_vectors = jnp.stack([small, small_other])[:, cut_h:].astype(F32).T

    state = None
    mixed = None
    for index in range(count):
        state = first_norm(
            index,
            count,
            place,
            images,
            images_other[index],
            features,
            in_weights,
            head_vectors,
            state,
        )
        state = list(state)
        if index == 0:
            in_piece, held = lax.optimization_barrier((in_piece, state[2]))
            state[2] = held
            in_other = lax.all_gather(in_piece, "dp", axis=0, tiled=True)
        if index == 1:
            mlp_piece, held = lax.optimization_barrier((mlp_piece, state[2]))
            state[2] = held
            mlp_other = lax.all_gather(mlp_piece, "dp", axis=0, tiled=True)
        mixed = list(mix(state[2], 0, index, 1, mixed))
        if index + 2 == len(images_other) and len(images_other) < count:
            turn = lax.optimization_barrier((images, images_other[-1], mixed[0]))
            images_other[-1], mixed[0] = turn[1:]
            images_other.append(to_other(turn[0], index + 2))
            if index == 0:
                mlp_piece = swap_tensor(after(mlp_piece, turn[1]))
        elif len(images_other) == count and index + 2 == count:
            turn = lax.optimization_barrier((cotangent, images_other[-1], mixed[0]))
            images_other[-1], mixed[0] = turn[1:]
            cot_other = jnp.concatenate([to_other(turn[0], spot) for spot in range(count)])
    rows, normed, qkv_own = state
    qkv_other = project(normed, in_other, head_vectors, width)
    ctx, logs = mix(qkv_other, 1, 0, count, mixed)
    flat = (count, 2 * width, seq)
    resid, low_second, grad_out, sum_fc2b = second_norm(
        place, ctx.reshape(flat), o_weight, in_other, rows, features, cotangent, cot_other
    )

    def stage(keep, place, weights, offset, which, earlier):
        return hidden_stage(
            keep, place, low_second, grad_out, *weights, offset, hidden_vectors, which, earlier
        )

    *held, fc1_o, fc2_o = stage(False, place, (mlp_other, mlp_other), 4, 1, None)
    *stage_other, fc1_k, fc2_k = stage(True, place, (mlp_other, mlp_other), 4, 1, held)
    fc1_send, fc2_send = both(fc1_k, fc1_o).astype(BF16), both(fc2_k, fc2_o).astype(BF16)
    place2, fc1_send, fc2_send = lax.optimization_barrier((place, fc1_send, fc2_send))
    fc1_arrived = swap_tensor(fc1_send)
    *held, fc1_o, fc2_o = stage(False, place2, (fc1_own, fc2_weight), 0, 0, None)
    fc2_send, held[2] = lax.optimization_barrier((fc2_send, held[2]))
    fc2_arrived = swap_tensor(fc2_send)
    *stage_own, fc1_k, fc2_k = stage(True, place2, (fc1_own, fc2_weight), 0, 0, held)
    g_fc1 = (both(fc1_k, fc1_o) + fc1_arrived.astype(F32)).astype(BF16)
    fc2_pair = both(fc2_k, fc2_o).astype(BF16)
    g_fc1, fc2_pair, back_own = lax.optimization_barrier((g_fc1, fc2_pair, stage_own[1]))
    g_fc1 = lax.psum(g_fc1, "dp", axis_index_groups=chip_groups(0))
    low_resid, sum_gain2, sum_bias2, sum_ob = resid_back(
        back_own, stage_other[1], fc1_own, mlp_other, resid, grad_out, features
    )
    d_ctx, *o_parts = context_back(place, low_resid, ctx.reshape(flat), o_weight, in_other)
    d_ctx, fc2_arrived, fc2_pair = lax.optimization_barrier(
        (d_ctx.reshape(ctx.shape), fc2_arrived, fc2_pair)
    )
    wide = (count, 3 * width, seq)
    d_other = mix_back(qkv_other, ctx, logs, d_ctx, 1, 0, count, None).reshape(wide)
    o_send = both(o_parts[2], o_parts[3]).astype(BF16)
    o_pair = both(o_parts[0], o_parts[1])
    d_other, o_send, o_pair = lax.optimization_barrier((d_other, o_send, o_pair))
    o_arrived = swap_tensor(o_send)
    other_keep, other_send, column_other = project_back(place, normed, d_other)
    o_arrived, other_keep = lax.optimization_barrier((o_arrived, other_keep))
    g_fc2 = fc2_pair.astype(F32) + fc2_arrived.astype(F32)
    g_late = jnp.concatenate([g_fc2, o_pair + o_arrived.astype(F32)]).astype(BF16)
    d_ctx, g_late = lax.optimization_barrier((d_ctx, g_late))
    g_late = lax.psum(g_late, "dp", axis_index_groups=chip_groups(1))

    d_own = mix_back(qkv_own, ctx, logs, d_ctx, 0, 0, 1, None)
    qkv_send = both(other_keep, other_send).astype(BF16)
    d_own, qkv_send, g_fc1 = lax.optimization_barrier((d_own, qkv_send, g_fc1))
    qkv_arrived = swap_tensor(qkv_send)
    fc1_other = swap_core(g_fc1)
    d_own = mix_back(qkv_own, ctx, logs, d_ctx, 0, 1, count - 1, d_own).reshape(wide)
    own_keep, own_send, column_own = project_back(place, normed, d_own)
    own_keep, fc1_other = lax.optimization_barrier((own_keep, fc1_other))
    out_fc1 = widen(place, g_fc1, fc1_other, 0, 2 * block, hidden, 4)
    own_swapped, qkv_arrived, out_fc1 = lax.optimization_barrier(
        (swap_core(own_send), qkv_arrived, out_fc1)
    )
    g_qkv = own_keep.astype(F32) + own_swapped.astype(F32) + qkv_arrived.astype(F32)
    g_qkv, d_own = lax.optimization_barrier((g_qkv.astype(BF16), d_own))
    g_qkv = lax.psum(g_qkv, "dp", axis_index_groups=chip_groups(2))
    in_buffer, in_send, sum_gain1, sum_bias1 = input_back(
        place, d_own, d_other, in_weights, in_other, rows, low_resid, features
    )
    in_send, act_own = lax.optimization_barrier((in_send, stage_own[0]))
    far = (1 - tensor) * count
    in_arrived = swap_tensor(in_send)
    out_buffer, out_send = layer_result(
        place, act_own, stage_other[0], fc2_weight, mlp_other, resid, features
    )
    in_arrived, out_send = lax.optimization_barrier((in_arrived, out_send))
    out_arrived = swap_tensor(out_send)
    input_grad = lax.dynamic_update_slice_in_dim(in_buffer, in_arrived, far, 0)
    layer_out = lax.dynamic_update_slice_in_dim(out_buffer, out_arrived, far, 0)

    sums = jnp.concatenate([sum_gain1, sum_bias1, sum_ob, sum_gain2, sum_bias2, sum_fc2b])

    def ordered(own, other):
        return jnp.where(tensor == 0, jnp.stack([own, other]), jnp.stack([other, own]))

    def heads_part(vector):
        return vector[:width, 0], vector[2 * width :, 0]

    (q_own, v_own), (q_other, v_other) = heads_part(column_own), heads_part(column_other)
    small_grads = jnp.concatenate(
        [
            sums.reshape(-1),
            ordered(
                jnp.concatenate([q_own, v_own, stage_own[2][:, 0]]),
                jnp.concatenate([q_other, v_other, stage_other[2][:, 0]]),
            ).reshape(-1),
        ]
    )
    step = 1
    while step < spots:
        small_grads += lax.ppermute(
            small_grads, "dp", [(spot, spot ^ step) for spot in range(spots)]
        )
        step *= 2
    small_grads += swap_tensor(small_grads)
    g_feature = lax.dynamic_slice_in_dim(
        small_grads[: 6 * feat].reshape(6, feat), tensor * half, half, 1
    )
    small_grads = lax.dynamic_index_in_dim(
        small_grads[6 * feat :].reshape(2, 2 * width + hidden), tensor, 0, keepdims=False
    )

    late_other = swap_core(g_late)
    qkv_other_core = swap_core(g_qkv)
    g_fc2 = widen(place, g_late, late_other, 0, 2 * block, hidden, 4)
    g_o = widen(
        place, g_late[2 * block :], late_other[2 * block :], 0, width // 2, width, 1
    )
    g_q, g_k, g_v = (
        widen(place, g_qkv, qkv_other_core, index * width // 2, width // 2, width, 1)
        for index in range(3)
    )
    return (
        jnp.swapaxes(layer_out, 1, 2),
        jnp.swapaxes(input_grad, 1, 2),
        g_feature[0],
        g_feature[1],
        g_q.T,
        small_grads[:width],
        g_k.T,
        g_v.T,
        small_grads[width : 2 * width],
        g_o,
        g_feature[2],
        g_feature[3],
        g_feature[4],
        out_fc1.T,
        small_grads[2 * width :],
        g_fc2,
        g_feature[5],
    )


def solution(mesh):
    in_specs = (
        P("dp", None, "tensor"),
        P("dp"),
        P("dp", None, "tensor"),
        P("tensor"),
        P("tensor"),
        P(None, "tensor"),
        P("tensor"),
        P(None, "tensor"),
        P(None, "tensor"),
        P("tensor"),
        P("tensor", None),
        P("tensor"),
        P("tensor"),
        P("tensor"),
        P(None, "tensor"),
        P("tensor"),
        P("tensor", None),
        P("tensor"),
    )
    out_specs = (
        P("dp", None, "tensor"),
        P("dp", None, "tensor"),
        P("tensor"),
        P("tensor"),
        P(None, "tensor"),
        P("tensor"),
        P(None, "tensor"),
        P(None, "tensor"),
        P("tensor"),
        P("tensor", None),
        P("tensor"),
        P("tensor"),
        P("tensor"),
        P(None, "tensor"),
        P("tensor"),
        P("tensor", None),
        P("tensor"),
    )
    whole_images = mesh.shape["tensor"] == 2 and mesh.shape["dp"] == 16
    return jax.shard_map(
        whole_device if whole_images else split_device, mesh=mesh, in_specs=in_specs, out_specs=out_specs, check_vma=False
    )
```

```python
import functools
import math

import jax
import jax.numpy as jnp
from jax import lax
from jax.experimental import pallas as pl
from jax.experimental.pallas import tpu as pltpu
from jax.sharding import PartitionSpec as P

HDIM = 72
MICRO = 2


EPS = 1e-06
GELU_C = math.sqrt(2.0 / math.pi)
GELU_A = 0.044715


def matmul(left, right):
    return jnp.dot(left, right, preferred_element_type=jnp.float32)


def left_transposed(left, right):
    return lax.dot_general(
        left, right, (((0,), (0,)), ((), ())), preferred_element_type=jnp.float32
    )


def right_transposed(left, right):
    return lax.dot_general(
        left, right, (((1,), (1,)), ((), ())), preferred_element_type=jnp.float32
    )


def rounded(values):
    return values.astype(jnp.bfloat16).astype(jnp.float32)


def norm_rows(values):
    feat_total = values.shape[1] * lax.axis_size("tensor")
    row_sum, row_square = lax.psum(
        (jnp.sum(values, axis=1), jnp.sum(values * values, axis=1)), "tensor"
    )
    row_mean = row_sum / feat_total
    row_var = row_square / feat_total - row_mean * row_mean
    inverse = lax.rsqrt(row_var + EPS)
    normed = (values - row_mean[:, None]) * inverse[:, None]
    return (normed, inverse)


def norm_back(grad_normed, normed, inverse, gain_vec):
    feat_total = normed.shape[1] * lax.axis_size("tensor")
    scaled = grad_normed * gain_vec.astype(jnp.float32)
    sum_plain, sum_cross = lax.psum(
        (jnp.sum(scaled, axis=1), jnp.sum(scaled * normed, axis=1)), "tensor"
    )
    return inverse[:, None] * (
        scaled - sum_plain[:, None] / feat_total - normed * (sum_cross[:, None] / feat_total)
    )


def gather_rows(shard):
    return lax.all_gather(shard, "tensor", axis=1, tiled=True)


def gather_grads(shard):
    return lax.all_gather(shard, "tensor", axis=1, tiled=True)


def gelu_parts(pre):
    tanh_val = jnp.tanh(GELU_C * (pre + GELU_A * pre * pre * pre))
    value = 0.5 * pre * (1.0 + tanh_val)
    slope = 0.5 * (1.0 + tanh_val) + 0.5 * pre * (1.0 - tanh_val * tanh_val) * GELU_C * (
        1.0 + 3.0 * GELU_A * pre * pre
    )
    return (value, slope)


def split_device(
    images,
    valid_flags,
    cotangent,
    ln1_gain,
    ln1_bias,
    q_weight,
    q_bias,
    k_weight,
    v_weight,
    v_bias,
    o_weight,
    o_bias,
    ln2_gain,
    ln2_bias,
    fc1_weight,
    fc1_bias,
    fc2_weight,
    fc2_bias,
):
    img_local, seq_len, feat_local = images.shape
    per_micro = img_local // MICRO
    rows = per_micro * seq_len
    head_local = q_weight.shape[1] // HDIM
    scale = 1.0 / math.sqrt(HDIM)
    shaped = (per_micro, seq_len, head_local, HDIM)
    split_images = images.reshape(per_micro, MICRO, seq_len, feat_local)
    split_cot = cotangent.reshape(per_micro, MICRO, seq_len, feat_local)
    split_flags = valid_flags.reshape(per_micro, MICRO).astype(jnp.float32)
    param_list = (
        ln1_gain,
        ln1_bias,
        q_weight,
        q_bias,
        k_weight,
        v_weight,
        v_bias,
        o_weight,
        o_bias,
        ln2_gain,
        ln2_bias,
        fc1_weight,
        fc1_bias,
        fc2_weight,
        fc2_bias,
    )
    totals = tuple((jnp.zeros(weight_arr.shape, jnp.float32) for weight_arr in param_list))
    out_list = []
    grad_list = []
    for micro_index in range(MICRO):
        flag_rows = jnp.repeat(split_flags[:, micro_index], seq_len)[:, None]
        inputs = split_images[:, micro_index].reshape(rows, feat_local).astype(jnp.float32)
        normed1, inverse1 = norm_rows(inputs)
        low_first = (normed1 * ln1_gain + ln1_bias).astype(jnp.bfloat16)
        full_first = gather_rows(low_first)
        query = (matmul(full_first, q_weight) + q_bias).astype(jnp.bfloat16)
        keys = matmul(full_first, k_weight).astype(jnp.bfloat16)
        values = (matmul(full_first, v_weight) + v_bias).astype(jnp.bfloat16)
        query4 = query.reshape(shaped)
        keys4 = keys.reshape(shaped)
        values4 = values.reshape(shaped)
        scores = (
            jnp.einsum("nqhd,nkhd->nhqk", query4, keys4, preferred_element_type=jnp.float32) * scale
        )
        log_total = jax.nn.logsumexp(scores, axis=-1)
        probs_low = jnp.exp(scores - log_total[..., None]).astype(jnp.bfloat16)
        mixed = jnp.einsum(
            "nhqk,nkhd->nqhd", probs_low, values4, preferred_element_type=jnp.float32
        )
        context = mixed.reshape(rows, head_local * HDIM).astype(jnp.bfloat16)
        attended = lax.psum_scatter(
            rounded(matmul(context, o_weight)).astype(jnp.bfloat16),
            "tensor",
            scatter_dimension=1,
            tiled=True,
        ).astype(jnp.float32)
        resid = inputs + attended + o_bias
        normed2, inverse2 = norm_rows(resid)
        low_second = (normed2 * ln2_gain + ln2_bias).astype(jnp.bfloat16)
        full_second = gather_rows(low_second)
        hidden_pre = matmul(full_second, fc1_weight) + fc1_bias
        act_value, act_slope = gelu_parts(hidden_pre)
        act_low = act_value.astype(jnp.bfloat16)
        branch = lax.psum_scatter(
            rounded(matmul(act_low, fc2_weight)).astype(jnp.bfloat16),
            "tensor",
            scatter_dimension=1,
            tiled=True,
        ).astype(jnp.float32)
        layer_rows = (resid + branch + fc2_bias) * flag_rows
        out_list.append(layer_rows.astype(jnp.bfloat16).reshape(per_micro, seq_len, feat_local))
        grad_out = (
            split_cot[:, micro_index].reshape(rows, feat_local).astype(jnp.float32) * flag_rows
        )
        grad_full = gather_grads(grad_out.astype(jnp.bfloat16))
        g_fc2w = left_transposed(act_low, grad_full)
        g_fc2b = jnp.sum(grad_out, axis=0)
        hidden_grad = (right_transposed(grad_full, fc2_weight) * act_slope).astype(jnp.bfloat16)
        g_fc1w = left_transposed(full_second, hidden_grad)
        g_fc1b = jnp.sum(hidden_grad.astype(jnp.float32), axis=0)
        grad_second = lax.psum_scatter(
            rounded(right_transposed(hidden_grad, fc1_weight)).astype(jnp.bfloat16),
            "tensor",
            scatter_dimension=1,
            tiled=True,
        ).astype(jnp.float32)
        g_ln2g = jnp.sum(grad_second * normed2, axis=0)
        g_ln2b = jnp.sum(grad_second, axis=0)
        grad_resid = grad_out + norm_back(grad_second, normed2, inverse2, ln2_gain)
        g_ob = jnp.sum(grad_resid, axis=0)
        resid_full = gather_grads(grad_resid.astype(jnp.bfloat16))
        g_ow = left_transposed(context, resid_full)
        grad_context = right_transposed(resid_full, o_weight).astype(jnp.bfloat16)
        context4 = grad_context.reshape(shaped)
        probs = jnp.exp(
            jnp.einsum("nqhd,nkhd->nhqk", query4, keys4, preferred_element_type=jnp.float32) * scale
            - log_total[..., None]
        )
        probs_again = probs.astype(jnp.bfloat16)
        grad_probs = jnp.einsum(
            "nqhd,nkhd->nhqk", context4, values4, preferred_element_type=jnp.float32
        )
        row_delta = jnp.sum(probs * grad_probs, axis=-1)
        grad_scores = (probs * (grad_probs - row_delta[..., None])).astype(jnp.bfloat16)
        grad_query = (
            (
                jnp.einsum(
                    "nhqk,nkhd->nqhd", grad_scores, keys4, preferred_element_type=jnp.float32
                )
                * scale
            )
            .reshape(rows, head_local * HDIM)
            .astype(jnp.bfloat16)
        )
        grad_keys = (
            (
                jnp.einsum(
                    "nhqk,nqhd->nkhd", grad_scores, query4, preferred_element_type=jnp.float32
                )
                * scale
            )
            .reshape(rows, head_local * HDIM)
            .astype(jnp.bfloat16)
        )
        grad_values = (
            jnp.einsum("nhqk,nqhd->nkhd", probs_again, context4, preferred_element_type=jnp.float32)
            .reshape(rows, head_local * HDIM)
            .astype(jnp.bfloat16)
        )
        g_qw = left_transposed(full_first, grad_query)
        g_qb = jnp.sum(grad_query.astype(jnp.float32), axis=0)
        g_kw = left_transposed(full_first, grad_keys)
        g_vw = left_transposed(full_first, grad_values)
        g_vb = jnp.sum(grad_values.astype(jnp.float32), axis=0)
        partial_first = (
            right_transposed(grad_query, q_weight)
            + right_transposed(grad_keys, k_weight)
            + right_transposed(grad_values, v_weight)
        )
        grad_first = lax.psum_scatter(
            rounded(partial_first).astype(jnp.bfloat16), "tensor", scatter_dimension=1, tiled=True
        ).astype(jnp.float32)
        g_ln1g = jnp.sum(grad_first * normed1, axis=0)
        g_ln1b = jnp.sum(grad_first, axis=0)
        grad_input = grad_resid + norm_back(grad_first, normed1, inverse1, ln1_gain)
        grad_list.append(grad_input.astype(jnp.bfloat16).reshape(per_micro, seq_len, feat_local))
        micro_grads = (
            g_ln1g,
            g_ln1b,
            g_qw,
            g_qb,
            g_kw,
            g_vw,
            g_vb,
            g_ow,
            g_ob,
            g_ln2g,
            g_ln2b,
            g_fc1w,
            g_fc1b,
            g_fc2w,
            g_fc2b,
        )
        totals = jax.tree.map(jnp.add, totals, micro_grads)
    totals = (
        lax.psum(totals[0].astype(jnp.bfloat16), "dp").astype(jnp.float32),
        lax.psum(totals[1].astype(jnp.bfloat16), "dp").astype(jnp.float32),
        lax.psum(totals[2].astype(jnp.bfloat16), "dp").astype(jnp.float32),
        lax.psum(totals[3].astype(jnp.bfloat16), "dp").astype(jnp.float32),
        lax.psum(totals[4].astype(jnp.bfloat16), "dp").astype(jnp.float32),
        lax.psum(totals[5].astype(jnp.bfloat16), "dp").astype(jnp.float32),
        lax.psum(totals[6].astype(jnp.bfloat16), "dp").astype(jnp.float32),
        lax.psum(totals[7].astype(jnp.bfloat16), "dp").astype(jnp.float32),
        lax.psum(totals[8].astype(jnp.bfloat16), "dp").astype(jnp.float32),
        lax.psum(totals[9].astype(jnp.bfloat16), "dp").astype(jnp.float32),
        lax.psum(totals[10].astype(jnp.bfloat16), "dp").astype(jnp.float32),
        lax.psum(totals[11].astype(jnp.bfloat16), "dp").astype(jnp.float32),
        lax.psum(totals[12].astype(jnp.bfloat16), "dp").astype(jnp.float32),
        lax.psum(totals[13].astype(jnp.bfloat16), "dp").astype(jnp.float32),
        lax.psum(totals[14].astype(jnp.bfloat16), "dp").astype(jnp.float32),
    )
    layer_out = jnp.stack(out_list, axis=1).reshape(img_local, seq_len, feat_local)
    input_grad = jnp.stack(grad_list, axis=1).reshape(img_local, seq_len, feat_local)
    return (
        layer_out,
        input_grad,
        totals[0],
        totals[1],
        totals[2],
        totals[3],
        totals[4],
        totals[5],
        totals[6],
        totals[7],
        totals[8],
        totals[9],
        totals[10],
        totals[11],
        totals[12],
        totals[13],
        totals[14],
    )


F32 = jnp.float32
BF16 = jnp.bfloat16
LOG2E = math.log2(math.e)
VMEM_BYTES = 58 * 1024 * 1024
COST_SHARE = 0.4
LONG = 4.0
SHORT = 0.05


def dot_nn(left, right):
    return jnp.dot(left, right, preferred_element_type=F32)


def dot_nt(left, right):
    return lax.dot_general(left, right, (((1,), (1,)), ((), ())), preferred_element_type=F32)


def dot_tn(left, right):
    return lax.dot_general(left, right, (((0,), (0,)), ((), ())), preferred_element_type=F32)


def cost(flops, moved, trans=0, share=COST_SHARE):
    return pl.CostEstimate(
        flops=int(flops * share),
        bytes_accessed=int(moved * share),
        transcendentals=int(trans * share),
    )


def params(grid_dims):
    return pltpu.CompilerParams(
        dimension_semantics=("arbitrary",) * grid_dims, vmem_limit_bytes=VMEM_BYTES
    )


def once(shape, spot=None):
    spot = spot or (0,) * len(shape)
    return pl.BlockSpec(shape, lambda *_: spot, pipeline_mode=pl.Buffered(1))


def image_block(shape, offset=0):
    return pl.BlockSpec((1,) + shape, lambda i, *_: (offset + i, 0, 0))


ANYWHERE = pl.BlockSpec(memory_space=pl.ANY)


def column_stats(values):
    mean = jnp.mean(values, axis=0, keepdims=True)
    centred = values - mean
    inverse = lax.rsqrt(jnp.mean(centred * centred, axis=0, keepdims=True) + EPS)
    return centred * inverse, inverse


def join_halves(first, own, other):
    return jnp.concatenate(
        [jnp.where(first, own, other), jnp.where(first, other, own)], axis=0
    )


def split_halves(first, full):
    half = full.shape[0] // 2
    low, high = full[:half], full[half:]
    return jnp.where(first, low, high), jnp.where(first, high, low)


def token_sum(values):
    return jnp.sum(values, axis=1, keepdims=True)


LN1_GAIN, LN1_BIAS, O_BIAS, LN2_GAIN, LN2_BIAS, FC2_BIAS = range(6)


def as_row(column_sum):
    rows = column_sum.shape[0]
    return jnp.broadcast_to(column_sum, (rows, 128)).T[0:1]


def column(ref, index):
    return ref[:, index : index + 1]


def write_rows(row_refs, sum_refs):
    @pl.when(pl.program_id(0) == pl.num_programs(0) - 1)
    def _():
        for row_ref, sum_ref in zip(row_refs, sum_refs):
            row_ref[...] = as_row(sum_ref[...])


def store_heads(out_ref, first, product):
    head_dim = out_ref.shape[2]
    for head in range(product.shape[0] // head_dim):
        out_ref[0, first + head] = product[head * head_dim : (head + 1) * head_dim].astype(BF16)


def first_norm_kernel(
    place_ref, own_ref, other_ref, feature_ref, q_ref, k_ref, v_ref, head_ref, *rest
):
    rows_ref, normed_ref, qkv_ref = rest[-3:]
    full = join_halves(place_ref[0] == 0, own_ref[0].astype(F32), other_ref[0].astype(F32))
    rows_ref[0] = full.astype(BF16)
    normed, _ = column_stats(full)
    low = (normed * column(feature_ref, LN1_GAIN) + column(feature_ref, LN1_BIAS)).astype(BF16)
    normed_ref[0] = low
    heads = qkv_ref.shape[1] // 3
    store_heads(qkv_ref, 0, dot_nn(q_ref[...], low) + column(head_ref, 0))
    store_heads(qkv_ref, heads, dot_nn(k_ref[...], low))
    store_heads(qkv_ref, 2 * heads, dot_nn(v_ref[...], low) + column(head_ref, 1))


def first_norm(index, count, place, images, other, features, weights, head_vectors, earlier):
    _, half, seq = images.shape
    width, feat = weights[0].shape
    groups = 3 * width // HDIM
    held = list(earlier) if earlier else []
    return pl.pallas_call(
        first_norm_kernel,
        out_shape=[
            jax.ShapeDtypeStruct((count, feat, seq), BF16),
            jax.ShapeDtypeStruct((count, feat, seq), BF16),
            jax.ShapeDtypeStruct((count, groups, HDIM, seq), BF16),
        ],
        grid_spec=pltpu.PrefetchScalarGridSpec(
            num_scalar_prefetch=1,
            grid=(1,),
            in_specs=[
                pl.BlockSpec((1, half, seq), lambda i, p: (p[0] * count + index, 0, 0)),
                once((1, half, seq)),
                once((feat, 8)),
                once((width, feat)),
                once((width, feat)),
                once((width, feat)),
                once((width, 8)),
            ]
            + [ANYWHERE] * len(held),
            out_specs=[
                once((1, feat, seq), (index, 0, 0)),
                once((1, feat, seq), (index, 0, 0)),
                once((1, groups, HDIM, seq), (index, 0, 0, 0)),
            ],
        ),
        input_output_aliases={8 + k: k for k in range(len(held))},
        compiler_params=params(1),
        cost_estimate=cost(6 * seq * feat * width, 12 << 20),
        name="first_norm",
    )(place, images, other, features, *weights, head_vectors, *held)


def project_kernel(normed_ref, q_ref, k_ref, v_ref, head_ref, qkv_ref):
    low = normed_ref[0]
    heads = qkv_ref.shape[1] // 3
    store_heads(qkv_ref, 0, dot_nn(q_ref[...], low) + column(head_ref, 2))
    store_heads(qkv_ref, heads, dot_nn(k_ref[...], low))
    store_heads(qkv_ref, 2 * heads, dot_nn(v_ref[...], low) + column(head_ref, 3))


def project(normed, weight, head_vectors, width):
    count, feat, seq = normed.shape
    groups = 3 * width // HDIM
    return pl.pallas_call(
        project_kernel,
        grid=(count,),
        out_shape=jax.ShapeDtypeStruct((count, groups, HDIM, seq), BF16),
        in_specs=[
            image_block((feat, seq)),
            once((width, feat), (0, 0)),
            once((width, feat), (1, 0)),
            once((width, feat), (2, 0)),
            once((width, 8)),
        ],
        out_specs=pl.BlockSpec((1, groups, HDIM, seq), lambda i: (i, 0, 0, 0)),
        compiler_params=params(1),
        cost_estimate=cost(6 * count * seq * feat * width, 20 << 20),
        name="project",
    )(normed, weight, weight, weight, head_vectors)


def mix_kernel(q_ref, k_ref, v_ref, *rest, scale):
    out_ref, log_ref = rest[-2:]
    factor = scale * LOG2E
    for head in range(q_ref.shape[1]):
        scores = dot_tn(k_ref[0, head], q_ref[0, head])
        top = jnp.max(scores, axis=0, keepdims=True)
        probs = jnp.exp2((scores - top) * factor)
        total = jnp.sum(probs, axis=0, keepdims=True)
        mixed = dot_nn(v_ref[0, head], probs.astype(BF16))
        out_ref[0, head] = (mixed * (1.0 / total)).astype(BF16)
        log_ref[0, head] = top * factor + jnp.log2(total)


def mix(qkv, half, start, steps, earlier, per_step=1):
    count, groups, head_dim, seq = qkv.shape
    heads = groups // 3
    blocks = heads // per_step
    block = (1, per_step, head_dim, seq)
    held = list(earlier) if earlier else []

    def at(offset):
        return pl.BlockSpec(block, lambda i, j: (start + i, offset + j, 0, 0))

    return pl.pallas_call(
        functools.partial(mix_kernel, scale=1.0 / math.sqrt(head_dim)),
        grid=(steps, blocks),
        out_shape=[
            jax.ShapeDtypeStruct((count, 2 * heads, head_dim, seq), BF16),
            jax.ShapeDtypeStruct((count, 2 * heads, 1, seq), F32),
        ],
        in_specs=[at(0), at(blocks), at(2 * blocks)] + [ANYWHERE] * len(held),
        out_specs=[
            at(half * blocks),
            pl.BlockSpec(
                (1, per_step, 1, seq), lambda i, j: (start + i, half * blocks + j, 0, 0)
            ),
        ],
        input_output_aliases={3 + k: k for k in range(len(held))},
        compiler_params=params(2),
        cost_estimate=cost(
            4 * steps * heads * seq * seq * 256,
            steps * heads * head_dim * seq * 8,
            steps * heads * seq * seq,
        ),
        name="mix",
    )(qkv, qkv, qkv, *held)


def mix_back_kernel(q_ref, k_ref, v_ref, out_ref, log_ref, grad_ref, *rest, scale, heads):
    d_ref = rest[-1]
    factor = scale * LOG2E
    per_step = q_ref.shape[1]
    first = pl.program_id(1) * per_step
    for head in range(per_step):
        query, keys, values = q_ref[0, head], k_ref[0, head], v_ref[0, head]
        grad = grad_ref[0, head]
        delta = jnp.sum(grad.astype(F32) * out_ref[0, head].astype(F32), axis=0, keepdims=True)
        probs = jnp.exp2(dot_tn(keys, query) * factor - log_ref[0, head])
        grad_scores = (probs * (dot_tn(values, grad) - delta)).astype(BF16)
        d_ref[0, 2 * heads + first + head] = dot_nt(grad, probs.astype(BF16)).astype(BF16)
        d_ref[0, first + head] = (dot_nn(keys, grad_scores) * scale).astype(BF16)
        d_ref[0, heads + first + head] = (dot_nt(query, grad_scores) * scale).astype(BF16)


def mix_back(qkv, out, log_total, grad, half, start, steps, earlier, per_step=2):
    count, groups, head_dim, seq = qkv.shape
    heads = groups // 3
    blocks = heads // per_step
    block = (1, per_step, head_dim, seq)
    held = [] if earlier is None else [earlier]

    def at(offset):
        return pl.BlockSpec(block, lambda i, j: (start + i, offset + j, 0, 0))

    return pl.pallas_call(
        functools.partial(mix_back_kernel, scale=1.0 / math.sqrt(head_dim), heads=heads),
        grid=(steps, blocks),
        out_shape=jax.ShapeDtypeStruct(qkv.shape, BF16),
        in_specs=[
            at(0),
            at(blocks),
            at(2 * blocks),
            at(half * blocks),
            pl.BlockSpec((1, per_step, 1, seq), lambda i, j: (start + i, half * blocks + j, 0, 0)),
            at(half * blocks),
        ]
        + [ANYWHERE] * len(held),
        input_output_aliases={6: 0} if held else {},
        out_specs=pl.BlockSpec((1, groups, head_dim, seq), lambda i, j: (start + i, 0, 0, 0)),
        compiler_params=params(2),
        cost_estimate=cost(
            10 * steps * heads * seq * seq * 256,
            steps * heads * head_dim * seq * 16,
            steps * heads * seq * seq,
            SHORT if steps == 1 else COST_SHARE,
        ),
        name="mix_back",
    )(qkv, qkv, qkv, out, log_total, grad, *held)


def second_norm_kernel(
    place_ref,
    ctx_ref,
    w_own_ref,
    w_other_ref,
    rows_ref,
    feature_ref,
    cot_own_ref,
    *rest,
):
    *cot_refs, resid_ref, low_ref, grad_ref, row_ref, w_ref, sum_ref = rest
    step = pl.program_id(0)
    half = w_own_ref.shape[0]

    @pl.when(step == 0)
    def _():
        w_ref[:half] = w_own_ref[...]
        w_ref[half:] = w_other_ref[...]
        sum_ref[...] = jnp.zeros_like(sum_ref)

    resid = rows_ref[0].astype(F32) + dot_tn(w_ref[...], ctx_ref[0])
    resid += column(feature_ref, O_BIAS)
    resid_ref[0] = resid
    normed, _ = column_stats(resid)
    low_ref[0] = (
        normed * column(feature_ref, LN2_GAIN) + column(feature_ref, LN2_BIAS)
    ).astype(BF16)
    flag = place_ref[2 + place_ref[0] * pl.num_programs(0) + step].astype(F32)
    cot_other = cot_refs[0][0]
    for index in range(1, len(cot_refs)):
        cot_other = jnp.where(step == index, cot_refs[index][0], cot_other)
    grad = flag * join_halves(
        place_ref[0] == 0, cot_own_ref[0].astype(F32), cot_other.astype(F32)
    )
    grad_ref[0] = grad.astype(BF16)
    sum_ref[...] += token_sum(grad)
    write_rows((row_ref,), (sum_ref,))


def second_norm(place, ctx, w_own, w_other, rows, features, cot, cot_other):
    count, feat, seq = rows.shape
    half = w_own.shape[0]
    full = image_block((feat, seq))
    return pl.pallas_call(
        second_norm_kernel,
        out_shape=[
            jax.ShapeDtypeStruct((count, feat, seq), F32),
            jax.ShapeDtypeStruct((count, feat, seq), BF16),
            jax.ShapeDtypeStruct((count, feat, seq), BF16),
            jax.ShapeDtypeStruct((1, feat), F32),
        ],
        grid_spec=pltpu.PrefetchScalarGridSpec(
            num_scalar_prefetch=1,
            grid=(count,),
            in_specs=[
                full,
                once((half, feat)),
                once((half, feat), (3, 0)),
                full,
                once((feat, 8)),
                pl.BlockSpec((1, feat // 2, seq), lambda i, p: (p[0] * count + i, 0, 0)),
            ]
            + [once((1, feat // 2, seq))] * count,
            out_specs=[full, full, full, once((1, feat))],
            scratch_shapes=[pltpu.VMEM((feat, feat), BF16), pltpu.VMEM((feat, 1), F32)],
        ),
        compiler_params=params(1),
        cost_estimate=cost(4 * count * seq * half * feat, 40 << 20),
        name="second_norm",
    )(place, ctx, w_own, w_other, rows, features, cot, *cot_other)


def hidden_kernel(place_ref, low_ref, grad_ref, fc1_ref, fc2_ref, bias_ref, *rest, which):
    act_ref, back_ref, gb_ref, g1_ref, g2_ref = rest[-5:]
    g1, g2, gb = None, None, None
    for image in range(low_ref.shape[0]):
        low, grad = low_ref[image], grad_ref[image]
        pre = dot_nn(fc1_ref[...], low) + column(bias_ref, which)
        square = pre * pre
        tanh_val = jnp.tanh(pre * (GELU_C + (GELU_C * GELU_A) * square))
        half = 0.5 * tanh_val + 0.5
        act = pre * half
        slope = half + act * (1.0 - half) * (2 * GELU_C + (6 * GELU_C * GELU_A) * square)
        act = act.astype(BF16)
        act_ref[image] = act
        back = (dot_nn(fc2_ref[...], grad) * slope).astype(BF16)
        back_ref[image] = back
        parts = dot_nt(back, low), dot_nt(act, grad), token_sum(back.astype(F32))
        g1 = parts[0] if g1 is None else g1 + parts[0]
        g2 = parts[1] if g2 is None else g2 + parts[1]
        gb = parts[2] if gb is None else gb + parts[2]
    gb_ref[...] = gb
    g1_ref[...] = g1.astype(BF16)
    g2_ref[...] = g2.astype(BF16)


def quarter_rows(hidden):
    return (-(-hidden // 4) + 7) // 8 * 8


def hidden_stage(keep, place, low, grad, fc1, fc2, fc2_offset, bias, which, earlier):
    count, feat, seq = low.shape
    hidden = bias.shape[0]
    block = quarter_rows(hidden)
    held = list(earlier) if earlier else []

    def chunk(j, p):
        return j + 2 * (p[1] if keep else 1 - p[1])

    weight = pl.BlockSpec((block, feat), lambda j, p: (chunk(j, p), 0))
    tokens = pl.BlockSpec((count, block, seq), lambda j, p: (0, chunk(j, p), 0))
    grads = pl.BlockSpec((block, feat), lambda j, p: (j, 0))
    part = jax.ShapeDtypeStruct((2 * block, feat), BF16)
    return pl.pallas_call(
        functools.partial(hidden_kernel, which=which),
        out_shape=[
            jax.ShapeDtypeStruct((count, hidden, seq), BF16),
            jax.ShapeDtypeStruct((count, hidden, seq), BF16),
            jax.ShapeDtypeStruct((hidden, 1), F32),
            part,
            part,
        ],
        grid_spec=pltpu.PrefetchScalarGridSpec(
            num_scalar_prefetch=1,
            grid=(2,),
            in_specs=[
                once((count, feat, seq)),
                once((count, feat, seq)),
                weight,
                pl.BlockSpec((block, feat), lambda j, p: (fc2_offset + chunk(j, p), 0)),
                pl.BlockSpec((block, 2), lambda j, p: (chunk(j, p), 0)),
            ]
            + [ANYWHERE] * len(held),
            out_specs=[
                tokens,
                tokens,
                pl.BlockSpec((block, 1), lambda j, p: (chunk(j, p), 0)),
                grads,
                grads,
            ],
        ),
        input_output_aliases={6 + k: k for k in range(len(held))},
        compiler_params=params(1),
        cost_estimate=cost(4 * count * seq * feat * hidden, 30 << 20, 0, LONG),
        name="hidden_stage",
    )(place, low, grad, fc1, fc2, bias, *held)


def layer_kernel(
    place_ref, act_own_ref, act_other_ref, w_own_ref, w_other_ref, resid_ref, b_ref, *rest, start, count
):
    out_ref, send_ref = rest[-2:]
    hidden = act_own_ref.shape[1]
    branch = dot_tn(w_own_ref[:hidden], act_own_ref[0])
    branch += dot_tn(w_other_ref[:hidden], act_other_ref[0])
    flag = place_ref[2 + place_ref[0] * count + start + pl.program_id(0)].astype(F32)
    result = (resid_ref[0] + branch + column(b_ref, FC2_BIAS)) * flag
    own, other = split_halves(place_ref[0] == 0, result)
    out_ref[0] = own.astype(BF16)
    send_ref[0] = other.astype(BF16)


def layer_result(place, act_own, act_other, w_own, w_other, resid, features, start, steps, held):
    count, feat, seq = resid.shape
    hidden = act_own.shape[1]
    full = image_block((hidden, seq), start)
    padded = 4 * quarter_rows(hidden)
    held = [] if held is None else [held]
    return pl.pallas_call(
        functools.partial(layer_kernel, start=start, count=count),
        out_shape=[
            jax.ShapeDtypeStruct((2 * count, feat // 2, seq), BF16),
            jax.ShapeDtypeStruct((steps, feat // 2, seq), BF16),
        ],
        grid_spec=pltpu.PrefetchScalarGridSpec(
            num_scalar_prefetch=1,
            grid=(steps,),
            in_specs=[
                full,
                full,
                once((hidden, feat)),
                once((padded, feat), (1, 0)),
                image_block((feat, seq), start),
                once((feat, 8)),
            ]
            + [ANYWHERE] * len(held),
            out_specs=[
                pl.BlockSpec((1, feat // 2, seq), lambda i, p: (p[0] * count + start + i, 0, 0)),
                image_block((feat // 2, seq)),
            ],
        ),
        input_output_aliases={7: 0} if held else {},
        compiler_params=params(1),
        cost_estimate=cost(4 * steps * seq * feat * hidden, steps * (12 << 20), 0, LONG),
        name="layer_result",
    )(place, act_own, act_other, w_own, w_other, resid, features, *held)


def resid_back_kernel(
    back_own_ref,
    back_other_ref,
    w_own_ref,
    w_other_ref,
    resid_ref,
    grad_ref,
    gain_ref,
    low_ref,
    row_gain_ref,
    row_bias_ref,
    row_ob_ref,
    sum_gain_ref,
    sum_bias_ref,
    sum_ob_ref,
):
    hidden = back_own_ref.shape[1]
    grad_norm = dot_tn(w_own_ref[:hidden], back_own_ref[0])
    grad_norm += dot_tn(w_other_ref[:hidden], back_other_ref[0])
    normed, inverse = column_stats(resid_ref[0])
    scaled = grad_norm * column(gain_ref, LN2_GAIN)
    plain = jnp.mean(scaled, axis=0, keepdims=True)
    cross = jnp.mean(scaled * normed, axis=0, keepdims=True)
    grad = grad_ref[0].astype(F32) + inverse * (scaled - plain - normed * cross)
    low_ref[0] = grad.astype(BF16)

    @pl.when(pl.program_id(0) == 0)
    def _():
        sum_gain_ref[...] = jnp.zeros_like(sum_gain_ref)
        sum_bias_ref[...] = jnp.zeros_like(sum_bias_ref)
        sum_ob_ref[...] = jnp.zeros_like(sum_ob_ref)

    sum_gain_ref[...] += token_sum(grad_norm * normed)
    sum_bias_ref[...] += token_sum(grad_norm)
    sum_ob_ref[...] += token_sum(grad)
    write_rows((row_gain_ref, row_bias_ref, row_ob_ref), (sum_gain_ref, sum_bias_ref, sum_ob_ref))


def resid_back(back_own, back_other, w_own, w_other, resid, grad, gain):
    count, feat, seq = resid.shape
    hidden = back_own.shape[1]
    padded = 4 * quarter_rows(hidden)
    wide = image_block((hidden, seq))
    full = image_block((feat, seq))
    return pl.pallas_call(
        resid_back_kernel,
        grid=(count,),
        out_shape=[jax.ShapeDtypeStruct((count, feat, seq), BF16)]
        + [jax.ShapeDtypeStruct((1, feat), F32)] * 3,
        in_specs=[
            wide,
            wide,
            once((hidden, feat)),
            once((padded, feat)),
            full,
            full,
            once((feat, 8)),
        ],
        out_specs=[full] + [once((1, feat))] * 3,
        scratch_shapes=[pltpu.VMEM((feat, 1), F32)] * 3,
        compiler_params=params(1),
        cost_estimate=cost(4 * count * seq * feat * hidden, 50 << 20),
        name="resid_back",
    )(back_own, back_other, w_own, w_other, resid, grad, gain)


def context_back_kernel(
    place_ref,
    low_ref,
    ctx_ref,
    w_own_ref,
    w_other_ref,
    d_ref,
    own_keep_ref,
    own_send_ref,
    other_keep_ref,
    other_send_ref,
    acc_ref,
):
    step = pl.program_id(0)
    low = low_ref[0]
    half = w_own_ref.shape[0]
    d_ref[0, :half] = dot_nn(w_own_ref[...], low).astype(BF16)
    d_ref[0, half:] = dot_nn(w_other_ref[...], low).astype(BF16)
    product = dot_nt(ctx_ref[0], low)

    @pl.when(step == 0)
    def _():
        acc_ref[...] = product

    @pl.when(step > 0)
    def _():
        acc_ref[...] += product

    @pl.when(step == pl.num_programs(0) - 1)
    def _():
        part = half // 2
        keep = place_ref[1] * part
        send = part - keep
        own_keep_ref[...] = acc_ref[pl.ds(pl.multiple_of(keep, 8), part)].astype(BF16)
        own_send_ref[...] = acc_ref[pl.ds(pl.multiple_of(send, 8), part)].astype(BF16)
        other_keep_ref[...] = acc_ref[pl.ds(pl.multiple_of(half + keep, 8), part)].astype(BF16)
        other_send_ref[...] = acc_ref[pl.ds(pl.multiple_of(half + send, 8), part)].astype(BF16)


def context_back(place, low, ctx, w_own, w_other):
    count, feat, seq = low.shape
    half = w_own.shape[0]
    full = image_block((feat, seq))
    part = jax.ShapeDtypeStruct((half // 2, feat), BF16)
    return pl.pallas_call(
        context_back_kernel,
        out_shape=[jax.ShapeDtypeStruct((count, 2 * half, seq), BF16)] + [part] * 4,
        grid_spec=pltpu.PrefetchScalarGridSpec(
            num_scalar_prefetch=1,
            grid=(count,),
            in_specs=[
                full,
                image_block((2 * half, seq)),
                once((half, feat)),
                once((half, feat), (3, 0)),
            ],
            out_specs=[image_block((2 * half, seq))] + [once((half // 2, feat))] * 4,
            scratch_shapes=[pltpu.VMEM((2 * half, feat), F32)],
        ),
        compiler_params=params(1),
        cost_estimate=cost(8 * count * seq * half * feat, 25 << 20),
        name="context_back",
    )(place, low, ctx, w_own, w_other)


def project_back_kernel(place_ref, normed_ref, d_ref, keep_ref, send_ref, col_ref, acc_ref):
    step = pl.program_id(0)
    product = dot_nt(d_ref[0], normed_ref[0])
    column = token_sum(d_ref[0].astype(F32))

    @pl.when(step == 0)
    def _():
        acc_ref[...] = product
        col_ref[...] = column

    @pl.when(step > 0)
    def _():
        acc_ref[...] += product
        col_ref[...] += column

    @pl.when(step == pl.num_programs(0) - 1)
    def _():
        part = keep_ref.shape[0] // 3
        keep = place_ref[1] * part
        for index in range(3):
            rows = slice(index * part, (index + 1) * part)
            first = 2 * index * part
            keep_rows = pl.ds(pl.multiple_of(first + keep, 8), part)
            send_rows = pl.ds(pl.multiple_of(first + part - keep, 8), part)
            keep_ref[rows] = acc_ref[keep_rows].astype(BF16)
            send_ref[rows] = acc_ref[send_rows].astype(BF16)


def project_back(place, normed, d_qkv):
    count, feat, seq = normed.shape
    width = d_qkv.shape[1]
    part = jax.ShapeDtypeStruct((width // 2, feat), BF16)
    return pl.pallas_call(
        project_back_kernel,
        out_shape=[part, part, jax.ShapeDtypeStruct((width, 1), F32)],
        grid_spec=pltpu.PrefetchScalarGridSpec(
            num_scalar_prefetch=1,
            grid=(count,),
            in_specs=[image_block((feat, seq)), image_block((width, seq))],
            out_specs=[
                once((width // 2, feat)),
                once((width // 2, feat)),
                once((width, 1)),
            ],
            scratch_shapes=[pltpu.VMEM((width, feat), F32)],
        ),
        compiler_params=params(1),
        cost_estimate=cost(2 * count * seq * feat * width, 20 << 20),
        name="project_back",
    )(place, normed, d_qkv)


def input_back_kernel(
    place_ref,
    d_own_ref,
    d_other_ref,
    q_ref,
    k_ref,
    v_ref,
    w_other_ref,
    rows_ref,
    low_ref,
    gain_ref,
    *rest,
):
    out_ref, send_ref, row_gain_ref, row_bias_ref, w_ref, sum_gain_ref, sum_bias_ref = rest[-7:]
    width = q_ref.shape[0]

    @pl.when(pl.program_id(0) == 0)
    def _():
        w_ref[:width] = q_ref[...]
        w_ref[width : 2 * width] = k_ref[...]
        w_ref[2 * width :] = v_ref[...]
        sum_gain_ref[...] = jnp.zeros_like(sum_gain_ref)
        sum_bias_ref[...] = jnp.zeros_like(sum_bias_ref)

    grad_norm = dot_tn(w_ref[...], d_own_ref[0]) + dot_tn(w_other_ref[...], d_other_ref[0])
    normed, inverse = column_stats(rows_ref[0].astype(F32))
    scaled = grad_norm * column(gain_ref, LN1_GAIN)
    plain = jnp.mean(scaled, axis=0, keepdims=True)
    cross = jnp.mean(scaled * normed, axis=0, keepdims=True)
    grad = low_ref[0].astype(F32) + inverse * (scaled - plain - normed * cross)
    own, other = split_halves(place_ref[0] == 0, grad)
    out_ref[0] = own.astype(BF16)
    send_ref[0] = other.astype(BF16)
    sum_gain_ref[...] += token_sum(grad_norm * normed)
    sum_bias_ref[...] += token_sum(grad_norm)
    write_rows((row_gain_ref, row_bias_ref), (sum_gain_ref, sum_bias_ref))


def input_back(place, d_own, d_other, weights, w_other, rows, low, features, start, steps, held):
    count, width, seq = d_own.shape
    feat = rows.shape[1]
    wide = image_block((width, seq), start)
    full = image_block((feat, seq), start)
    held = [] if held is None else [held]
    return pl.pallas_call(
        input_back_kernel,
        out_shape=[
            jax.ShapeDtypeStruct((2 * count, feat // 2, seq), BF16),
            jax.ShapeDtypeStruct((steps, feat // 2, seq), BF16),
            jax.ShapeDtypeStruct((1, feat), F32),
            jax.ShapeDtypeStruct((1, feat), F32),
        ],
        grid_spec=pltpu.PrefetchScalarGridSpec(
            num_scalar_prefetch=1,
            grid=(steps,),
            in_specs=[wide, wide]
            + [once((width // 3, feat))] * 3
            + [once((width, feat)), full, full, once((feat, 8))]
            + [ANYWHERE] * len(held),
            out_specs=[
                pl.BlockSpec((1, feat // 2, seq), lambda i, p: (p[0] * count + start + i, 0, 0)),
                image_block((feat // 2, seq)),
                once((1, feat)),
                once((1, feat)),
            ],
            scratch_shapes=[
                pltpu.VMEM((width, feat), BF16),
                pltpu.VMEM((feat, 1), F32),
                pltpu.VMEM((feat, 1), F32),
            ],
        ),
        input_output_aliases={10: 0} if held else {},
        compiler_params=params(1),
        cost_estimate=cost(4 * steps * seq * feat * width, steps * (11 << 20) + (8 << 20), 0, LONG),
        name="input_back",
    )(place, d_own, d_other, *weights, w_other, rows, low, features, *held)


def widen_kernel(place_ref, mine_ref, other_ref, *out_refs, steps):
    half, step = pl.program_id(1), pl.program_id(2)
    mine = half == place_ref[1]
    value = jnp.where(mine, mine_ref[...], other_ref[...]).astype(F32)
    for index, out_ref in enumerate(out_refs):

        @pl.when(pl.program_id(0) == index)
        def _():
            out_ref[...] = value


def widen(place, mine, other, part, total, steps, count=1):
    feat = mine.shape[1]
    rows = part // steps
    last = 2 * steps - 1

    def mine_spot(w, h, i, p):
        used = 1 - (h - p[1]) * (h - p[1])
        return (w * steps + i * used, 0)

    def other_spot(w, h, i, p):
        used = (h - p[1]) * (h - p[1])
        return (w * steps + i * used, 0)

    def out_spot(index):
        return lambda w, h, i, p: (jnp.clip((w - index) * 2 * steps + h * steps + i, 0, last), 0)

    out = pl.pallas_call(
        functools.partial(widen_kernel, steps=steps),
        out_shape=[jax.ShapeDtypeStruct((total, feat), F32)] * count,
        grid_spec=pltpu.PrefetchScalarGridSpec(
            num_scalar_prefetch=1,
            grid=(count, 2, steps),
            in_specs=[
                pl.BlockSpec((rows, feat), mine_spot),
                pl.BlockSpec((rows, feat), other_spot),
            ],
            out_specs=[pl.BlockSpec((rows, feat), out_spot(index)) for index in range(count)],
        ),
        compiler_params=params(3),
        cost_estimate=cost(0, 8 * total * feat * count, 0, SHORT),
        name="widen",
    )(place, mine, other)
    return out if count > 1 else out[0]


def swap_tensor(value):
    return lax.ppermute(value, "tensor", [(0, 1), (1, 0)])


def swap_core(value):
    return lax.ppermute(value, "dp", [(spot, spot ^ 1) for spot in range(lax.axis_size("dp"))])


def exchange_sum(value, steps):
    total = value
    for step in steps:
        pairs = [(spot, spot ^ step) for spot in range(lax.axis_size("dp"))]
        total += lax.ppermute(value, "dp", pairs)
    return total


def other_weights(weights, spots, rows):
    per_weight = spots // len(weights)
    mine = lax.axis_index("dp")
    start = mine % per_weight * rows
    piece = None
    for index, weight in enumerate(weights):
        short = per_weight * rows - weight.shape[0]
        if short:
            weight = jnp.pad(weight, ((0, short), (0, 0)))
        part = lax.dynamic_slice_in_dim(weight, start, rows, 0)
        piece = part if piece is None else jnp.where(mine // per_weight == index, part, piece)
    return piece


def chip_groups(order):
    spots = lax.axis_size("dp")
    groups = [list(range(core, spots, 2)) for core in range(2)]
    return groups[::-1] if order else groups


def swap_step(value, step):
    return lax.ppermute(value, "dp", [(spot, spot ^ step) for spot in range(lax.axis_size("dp"))])


def side(step):
    return lax.axis_index("dp") // step % 2


def halves(value, step):
    rows = value.shape[0] // 2
    mine = side(step)
    keep = lax.dynamic_slice_in_dim(value, mine * rows, rows, 0)
    return keep, lax.dynamic_slice_in_dim(value, (1 - mine) * rows, rows, 0)


def ranked(mine, other, step):
    first = side(step) == 0
    return jnp.concatenate([jnp.where(first, mine, other), jnp.where(first, other, mine)])


def added(left, right):
    return (left.astype(F32) + right.astype(F32)).astype(BF16)


def both(keep, send):
    return keep.astype(F32) + swap_core(send).astype(F32)


def after(value, *others):
    return lax.optimization_barrier((value, *others))[0]


def whole_device(
    images,
    valid_flags,
    cotangent,
    ln1_gain,
    ln1_bias,
    q_weight,
    q_bias,
    k_weight,
    v_weight,
    v_bias,
    o_weight,
    o_bias,
    ln2_gain,
    ln2_bias,
    fc1_weight,
    fc1_bias,
    fc2_weight,
    fc2_bias,
):
    img_local, seq, half = images.shape
    count = img_local // 2
    feat = 2 * half
    spots = lax.axis_size("dp")
    width = q_weight.shape[1]
    hidden = fc1_weight.shape[1]
    heads = width // HDIM
    tensor = lax.axis_index("tensor")
    core = lax.axis_index("dp") % 2
    place = jnp.concatenate(
        [jnp.stack([tensor, core]).astype(jnp.int32), valid_flags.astype(jnp.int32)]
    )
    images, cotangent = jnp.swapaxes(images, 1, 2), jnp.swapaxes(cotangent, 1, 2)
    in_weights = [q_weight.T, k_weight.T, v_weight.T]
    fc1_own = fc1_weight.T

    def to_send(array, index, images=1):
        return lax.dynamic_slice_in_dim(array, (1 - tensor) * count + index, images, 0)

    small = jnp.concatenate(
        [ln1_gain, ln1_bias, o_bias, ln2_gain, ln2_bias, fc2_bias, q_bias, v_bias, fc1_bias]
    )
    cut_q, cut_v, cut_h = 6 * half, 6 * half + width, 6 * half + 2 * width
    block = quarter_rows(hidden)

    in_piece = other_weights([*in_weights, o_weight], spots, width // (spots // 4))
    first, in_piece = lax.optimization_barrier((to_send(images, 0), in_piece))
    in_piece = swap_tensor(in_piece)
    images_other = [swap_tensor(first)]
    small_other = swap_tensor(after(small, first))
    mlp_piece = other_weights([fc1_own, fc2_weight], spots, block // 2)
    next_image = to_send(images, 1)
    next_image, mlp_piece, images_other[0] = lax.optimization_barrier(
        (next_image, mlp_piece, images_other[0])
    )
    images_other.append(swap_tensor(next_image))
    mlp_piece = swap_tensor(mlp_piece)

    def features_of(source):
        return source[:cut_q].reshape(6, half)

    feature_own, feature_other = features_of(small), features_of(small_other)
    features = jnp.where(
        tensor == 0,
        jnp.concatenate([feature_own, feature_other], axis=1),
        jnp.concatenate([feature_other, feature_own], axis=1),
    )
    features = jnp.pad(features, ((0, 2), (0, 0))).astype(F32).T
    head_vectors = jnp.stack([small, small_other])[:, cut_q:cut_h].reshape(4, width)
    head_vectors = jnp.pad(head_vectors, ((0, 4), (0, 0))).astype(F32).T
    hidden_vectors = jnp.stack([small, small_other])[:, cut_h:].astype(F32).T

    state = None
    mixed = None
    for index in range(count):
        state = first_norm(
            index,
            count,
            place,
            images,
            images_other[index],
            features,
            in_weights,
            head_vectors,
            state,
        )
        state = list(state)
        if index == 0:
            in_piece, state[2] = lax.optimization_barrier((in_piece, state[2]))
            in_other = lax.all_gather(in_piece, "dp", axis=0, tiled=True)
        if index == 1:
            mlp_piece, state[2] = lax.optimization_barrier((mlp_piece, state[2]))
            mlp_other = lax.all_gather(mlp_piece, "dp", axis=0, tiled=True)
        mixed = list(mix(state[2], 0, index, 1, mixed))
        if index + 2 < count:
            next_image = to_send(images, index + 2)
            next_image, images_other[-1], mixed[0] = lax.optimization_barrier(
                (next_image, images_other[-1], mixed[0])
            )
            images_other.append(swap_tensor(next_image))
        elif index + 2 == count:
            late = [to_send(cotangent, spot) for spot in range(count)]
            images_other[-1], mixed[0], *late = lax.optimization_barrier(
                (images_other[-1], mixed[0], *late)
            )
            cot_other = [swap_tensor(value) for value in late]
    rows, normed, qkv_own = state
    qkv_other = project(normed, in_other, head_vectors, width)
    ctx, logs = mix(qkv_other, 1, 0, count, mixed)
    ctx, *cot_other = lax.optimization_barrier((ctx, *cot_other))
    flat = (count, 2 * width, seq)
    resid, low_second, grad_out, sum_fc2b = second_norm(
        place, ctx.reshape(flat), o_weight, in_other, rows, features, cotangent, cot_other
    )

    def stage(keep, place, weights, offset, which, earlier):
        return hidden_stage(
            keep, place, low_second, grad_out, *weights, offset, hidden_vectors, which, earlier
        )

    *held, fc1_o, fc2_o = stage(False, place, (mlp_other, mlp_other), 4, 1, None)
    *stage_other, fc1_k, fc2_k = stage(True, place, (mlp_other, mlp_other), 4, 1, held)
    rows_a = 4 * block // 3 // 8 * 8
    rows_b = 2 * block - rows_a
    fc1_r, fc2_r = swap_core(fc1_o), swap_core(fc2_o)

    def summed(keep, arrived, low, high):
        return (keep[low:high].astype(F32) + arrived[low:high].astype(F32)).astype(BF16)

    piece = summed(fc1_k, fc1_r, 0, rows_a)
    later = (
        summed(fc1_k, fc1_r, rows_a, 2 * block),
        summed(fc2_k, fc2_r, 0, rows_a - rows_b),
        summed(fc2_k, fc2_r, rows_a - rows_b, 2 * block),
    )
    place2, piece, *later = lax.optimization_barrier((place, piece, *later))
    fc1_arrived = [swap_tensor(piece)]
    *held, fc1_o, fc2_o = stage(False, place2, (fc1_own, fc2_weight), 0, 0, None)
    held[2], fc1_arrived[0], *later = lax.optimization_barrier((held[2], fc1_arrived[0], *later))
    fc1_arrived.append(swap_tensor(later[0]))
    fc2_arrived = [swap_tensor(later[1])]
    *stage_own, fc1_k, fc2_k = stage(True, place2, (fc1_own, fc2_weight), 0, 0, held)
    back_own = stage_own[1]
    back_own, fc1_arrived[1], fc2_arrived[0], last = lax.optimization_barrier(
        (back_own, fc1_arrived[1], fc2_arrived[0], later[2])
    )
    g_fc1 = (both(fc1_k, fc1_o) + jnp.concatenate(fc1_arrived).astype(F32)).astype(BF16)
    fc2_r = swap_core(fc2_o)
    g_fc1, fc2_r, back_own = lax.optimization_barrier((g_fc1, fc2_r, back_own))
    fc2_arrived.append(swap_tensor(last))
    g_fc1 = lax.psum(g_fc1, "dp", axis_index_groups=chip_groups(0))
    low_resid, sum_gain2, sum_bias2, sum_ob = resid_back(
        back_own, stage_other[1], fc1_own, mlp_other, resid, grad_out, features
    )
    low_resid, fc2_arrived[1] = lax.optimization_barrier((low_resid, fc2_arrived[1]))
    g_late = fc2_k.astype(F32) + fc2_r.astype(F32) + jnp.concatenate(fc2_arrived).astype(F32)
    g_late = g_late.astype(BF16)
    x_keep, x_send = halves(g_late, 2)
    low_resid, x_keep, x_send = lax.optimization_barrier((low_resid, x_keep, x_send))
    d_ctx, *o_parts = context_back(place, low_resid, ctx.reshape(flat), o_weight, in_other)
    d_ctx = d_ctx.reshape(ctx.shape)
    d_ctx, x_send = lax.optimization_barrier((d_ctx, x_send))
    x_recv = swap_step(x_send, 2)
    wide = (count, 3 * width, seq)
    d_other = mix_back(qkv_other, ctx, logs, d_ctx, 1, 0, count, None).reshape(wide)
    o_send = both(o_parts[2], o_parts[3]).astype(BF16)
    o_pair = both(o_parts[0], o_parts[1])
    d_other, x_recv = lax.optimization_barrier((d_other, x_recv))
    z_keep, z_send = halves(added(x_keep, x_recv), 4)
    d_other, o_send, o_pair, z_keep, z_send = lax.optimization_barrier(
        (d_other, o_send, o_pair, z_keep, z_send)
    )
    z_recv = swap_step(z_send, 4)
    o_arrived = swap_tensor(o_send)
    other_keep, other_send, column_other = project_back(place, normed, d_other)
    o_arrived, other_keep, g_fc1, z_recv = lax.optimization_barrier(
        (o_arrived, other_keep, g_fc1, z_recv)
    )
    far_keep, far_send = halves(added(z_keep, z_recv), 8)
    g_o = (o_pair + o_arrived.astype(F32)).astype(BF16)
    d_ctx, g_o, far_keep, far_send = lax.optimization_barrier((d_ctx, g_o, far_keep, far_send))
    far_recv = swap_step(far_send, 8)
    fc1_other = swap_core(g_fc1)

    d_own = mix_back(qkv_own, ctx, logs, d_ctx, 0, 0, 1, None)
    other_recv = swap_core(other_send)
    third = 3 * width // 2 * 3 // 10 // 8 * 8
    cuts = [0, third, 2 * third, 3 * width // 2]
    pieces = [summed(other_keep, other_recv, *cuts[k : k + 2]) for k in range(3)]
    d_own, far_recv = lax.optimization_barrier((d_own, far_recv))
    block_sum = added(far_keep, far_recv)
    d_own, fc1_other, block_sum, *pieces = lax.optimization_barrier(
        (d_own, fc1_other, block_sum, *pieces)
    )
    qkv_arrived = []
    for index in range(1, count):
        step = 16 >> index
        block_recv = swap_step(block_sum, step)
        qkv_arrived.append(swap_tensor(pieces[index - 1]))
        d_own = mix_back(qkv_own, ctx, logs, d_ctx, 0, index, 1, d_own)
        d_own, qkv_arrived[-1], block_recv, *pieces = lax.optimization_barrier(
            (d_own, qkv_arrived[-1], block_recv, *pieces)
        )
        block_sum = ranked(block_sum, block_recv, step)
        d_own, block_sum = lax.optimization_barrier((d_own, block_sum))
    qkv_arrived += [swap_tensor(value) for value in pieces[count - 1 :]]
    d_own = d_own.reshape(wide)
    own_keep, own_send, column_own = project_back(place, normed, d_own)
    own_keep, d_own, *qkv_arrived = lax.optimization_barrier((own_keep, d_own, *qkv_arrived))

    def inputs(start, steps, held):
        return input_back(
            place, d_own, d_other, in_weights, in_other, rows, low_resid, features, start, steps, held
        )

    def ordered(own, other):
        return jnp.where(tensor == 0, jnp.stack([own, other]), jnp.stack([other, own]))

    def heads_part(vector):
        return vector[:width, 0], vector[2 * width :, 0]

    (q_own, v_own), (q_other, v_other) = heads_part(column_own), heads_part(column_other)
    early_sums = jnp.concatenate(
        [
            jnp.concatenate([sum_ob, sum_gain2, sum_bias2, sum_fc2b], axis=1)[0],
            ordered(
                jnp.concatenate([q_own, v_own, stage_own[2][:, 0]]),
                jnp.concatenate([q_other, v_other, stage_other[2][:, 0]]),
            ).reshape(-1),
        ]
    )
    d_own, early_sums = lax.optimization_barrier((d_own, early_sums))
    in_buffer, in_send, gain_a, bias_a = inputs(0, 1, None)
    block_recv = swap_step(block_sum, 2)
    own_recv, in_buffer, in_send = lax.optimization_barrier(
        (swap_core(own_send), in_buffer, in_send)
    )
    in_arrived = [swap_tensor(in_send)]
    g_qkv = own_keep.astype(F32) + own_recv.astype(F32) + jnp.concatenate(qkv_arrived).astype(F32)
    g_qkv = jnp.concatenate([g_qkv.astype(BF16), g_o])
    g_qkv, in_buffer = lax.optimization_barrier((g_qkv, in_buffer))
    g_qkv = lax.psum(g_qkv, "dp", axis_index_groups=chip_groups(1))
    in_buffer, in_send, gain_b, bias_b = inputs(1, count - 1, in_buffer)
    norm_sums = jnp.concatenate([gain_a + gain_b, bias_a + bias_b], axis=1)
    small_grads = jnp.concatenate([norm_sums[0], early_sums])
    small_swapped = swap_tensor(small_grads)
    in_send, in_arrived[0], act_own, block_recv = lax.optimization_barrier(
        (in_send, in_arrived[0], stage_own[0], block_recv)
    )
    g_late = ranked(block_sum, block_recv, 2)
    act_own, g_late = lax.optimization_barrier((act_own, g_late))
    far = (1 - tensor) * count
    in_arrived.append(swap_tensor(in_send))
    late_other = swap_core(g_late)

    def layers(start, steps, held):
        return layer_result(
            place, act_own, stage_other[0], fc2_weight, mlp_other, resid, features, start, steps, held
        )

    out_buffer, out_send, = layers(0, count - 1, None)
    in_arrived[1], out_send, out_buffer, small_swapped = lax.optimization_barrier(
        (in_arrived[1], out_send, out_buffer, small_swapped)
    )
    small_grads += small_swapped
    out_arrived = [swap_tensor(out_send)]
    out_buffer, out_send = layers(count - 1, 1, out_buffer)
    out_send, late_other, fc1_other = lax.optimization_barrier((out_send, late_other, fc1_other))
    out_arrived.append(swap_tensor(out_send))

    out_fc1 = widen(place, g_fc1, fc1_other, 2 * block, hidden, 4)
    input_grad = lax.dynamic_update_slice_in_dim(in_buffer, jnp.concatenate(in_arrived), far, 0)
    out_fc2 = widen(place, g_late, late_other, 2 * block, hidden, 4)

    out_fc2, out_fc1, out_arrived[0] = lax.optimization_barrier((out_fc2, out_fc1, out_arrived[0]))
    small_grads = exchange_sum(small_grads, (1, 2, 3))
    out_fc2, input_grad = lax.optimization_barrier((out_fc2, input_grad))
    out_fc2, out_arrived[1] = lax.optimization_barrier((out_fc2, out_arrived[1]))
    g_qkv, small_grads, out_fc2 = lax.optimization_barrier((g_qkv, small_grads, out_fc2))
    qkv_other_core = swap_core(g_qkv)
    layer_out = lax.dynamic_update_slice_in_dim(out_buffer, jnp.concatenate(out_arrived), far, 0)
    small_grads = exchange_sum(small_grads, range(4, spots, 4))
    g_feature = lax.dynamic_slice_in_dim(
        small_grads[: 6 * feat].reshape(6, feat), tensor * half, half, 1
    )
    small_grads = lax.dynamic_index_in_dim(
        small_grads[6 * feat :].reshape(2, 2 * width + hidden), tensor, 0, keepdims=False
    )

    g_q, g_k, g_v, g_o = widen(place, g_qkv, qkv_other_core, width // 2, width, 1, 4)
    return (
        jnp.swapaxes(layer_out, 1, 2),
        jnp.swapaxes(input_grad, 1, 2),
        g_feature[0],
        g_feature[1],
        g_q.T,
        small_grads[:width],
        g_k.T,
        g_v.T,
        small_grads[width : 2 * width],
        g_o,
        g_feature[2],
        g_feature[3],
        g_feature[4],
        out_fc1.T,
        small_grads[2 * width :],
        out_fc2,
        g_feature[5],
    )


def solution(mesh):
    in_specs = (
        P("dp", None, "tensor"),
        P("dp"),
        P("dp", None, "tensor"),
        P("tensor"),
        P("tensor"),
        P(None, "tensor"),
        P("tensor"),
        P(None, "tensor"),
        P(None, "tensor"),
        P("tensor"),
        P("tensor", None),
        P("tensor"),
        P("tensor"),
        P("tensor"),
        P(None, "tensor"),
        P("tensor"),
        P("tensor", None),
        P("tensor"),
    )
    out_specs = (
        P("dp", None, "tensor"),
        P("dp", None, "tensor"),
        P("tensor"),
        P("tensor"),
        P(None, "tensor"),
        P("tensor"),
        P(None, "tensor"),
        P(None, "tensor"),
        P("tensor"),
        P("tensor", None),
        P("tensor"),
        P("tensor"),
        P("tensor"),
        P(None, "tensor"),
        P("tensor"),
        P("tensor", None),
        P("tensor"),
    )
    whole_images = mesh.shape["tensor"] == 2 and mesh.shape["dp"] == 16
    return jax.shard_map(
        whole_device if whole_images else split_device, mesh=mesh, in_specs=in_specs, out_specs=out_specs, check_vma=False
    )
```

```python
import functools
import math

import jax
import jax.numpy as jnp
from jax import lax
from jax.experimental import pallas as pl
from jax.experimental.pallas import tpu as pltpu
from jax.sharding import PartitionSpec as P

HDIM = 72
MICRO = 2


EPS = 1e-06
GELU_C = math.sqrt(2.0 / math.pi)
GELU_A = 0.044715


def matmul(left, right):
    return jnp.dot(left, right, preferred_element_type=jnp.float32)


def left_transposed(left, right):
    return lax.dot_general(
        left, right, (((0,), (0,)), ((), ())), preferred_element_type=jnp.float32
    )


def right_transposed(left, right):
    return lax.dot_general(
        left, right, (((1,), (1,)), ((), ())), preferred_element_type=jnp.float32
    )


def rounded(values):
    return values.astype(jnp.bfloat16).astype(jnp.float32)


def norm_rows(values):
    feat_total = values.shape[1] * lax.axis_size("tensor")
    row_sum, row_square = lax.psum(
        (jnp.sum(values, axis=1), jnp.sum(values * values, axis=1)), "tensor"
    )
    row_mean = row_sum / feat_total
    row_var = row_square / feat_total - row_mean * row_mean
    inverse = lax.rsqrt(row_var + EPS)
    normed = (values - row_mean[:, None]) * inverse[:, None]
    return (normed, inverse)


def norm_back(grad_normed, normed, inverse, gain_vec):
    feat_total = normed.shape[1] * lax.axis_size("tensor")
    scaled = grad_normed * gain_vec.astype(jnp.float32)
    sum_plain, sum_cross = lax.psum(
        (jnp.sum(scaled, axis=1), jnp.sum(scaled * normed, axis=1)), "tensor"
    )
    return inverse[:, None] * (
        scaled - sum_plain[:, None] / feat_total - normed * (sum_cross[:, None] / feat_total)
    )


def gather_rows(shard):
    return lax.all_gather(shard, "tensor", axis=1, tiled=True)


def gather_grads(shard):
    return lax.all_gather(shard, "tensor", axis=1, tiled=True)


def gelu_parts(pre):
    tanh_val = jnp.tanh(GELU_C * (pre + GELU_A * pre * pre * pre))
    value = 0.5 * pre * (1.0 + tanh_val)
    slope = 0.5 * (1.0 + tanh_val) + 0.5 * pre * (1.0 - tanh_val * tanh_val) * GELU_C * (
        1.0 + 3.0 * GELU_A * pre * pre
    )
    return (value, slope)


def split_device(
    images,
    valid_flags,
    cotangent,
    ln1_gain,
    ln1_bias,
    q_weight,
    q_bias,
    k_weight,
    v_weight,
    v_bias,
    o_weight,
    o_bias,
    ln2_gain,
    ln2_bias,
    fc1_weight,
    fc1_bias,
    fc2_weight,
    fc2_bias,
):
    img_local, seq_len, feat_local = images.shape
    per_micro = img_local // MICRO
    rows = per_micro * seq_len
    head_local = q_weight.shape[1] // HDIM
    scale = 1.0 / math.sqrt(HDIM)
    shaped = (per_micro, seq_len, head_local, HDIM)
    split_images = images.reshape(per_micro, MICRO, seq_len, feat_local)
    split_cot = cotangent.reshape(per_micro, MICRO, seq_len, feat_local)
    split_flags = valid_flags.reshape(per_micro, MICRO).astype(jnp.float32)
    param_list = (
        ln1_gain,
        ln1_bias,
        q_weight,
        q_bias,
        k_weight,
        v_weight,
        v_bias,
        o_weight,
        o_bias,
        ln2_gain,
        ln2_bias,
        fc1_weight,
        fc1_bias,
        fc2_weight,
        fc2_bias,
    )
    totals = tuple((jnp.zeros(weight_arr.shape, jnp.float32) for weight_arr in param_list))
    out_list = []
    grad_list = []
    for micro_index in range(MICRO):
        flag_rows = jnp.repeat(split_flags[:, micro_index], seq_len)[:, None]
        inputs = split_images[:, micro_index].reshape(rows, feat_local).astype(jnp.float32)
        normed1, inverse1 = norm_rows(inputs)
        low_first = (normed1 * ln1_gain + ln1_bias).astype(jnp.bfloat16)
        full_first = gather_rows(low_first)
        query = (matmul(full_first, q_weight) + q_bias).astype(jnp.bfloat16)
        keys = matmul(full_first, k_weight).astype(jnp.bfloat16)
        values = (matmul(full_first, v_weight) + v_bias).astype(jnp.bfloat16)
        query4 = query.reshape(shaped)
        keys4 = keys.reshape(shaped)
        values4 = values.reshape(shaped)
        scores = (
            jnp.einsum("nqhd,nkhd->nhqk", query4, keys4, preferred_element_type=jnp.float32) * scale
        )
        log_total = jax.nn.logsumexp(scores, axis=-1)
        probs_low = jnp.exp(scores - log_total[..., None]).astype(jnp.bfloat16)
        mixed = jnp.einsum(
            "nhqk,nkhd->nqhd", probs_low, values4, preferred_element_type=jnp.float32
        )
        context = mixed.reshape(rows, head_local * HDIM).astype(jnp.bfloat16)
        attended = lax.psum_scatter(
            rounded(matmul(context, o_weight)).astype(jnp.bfloat16),
            "tensor",
            scatter_dimension=1,
            tiled=True,
        ).astype(jnp.float32)
        resid = inputs + attended + o_bias
        normed2, inverse2 = norm_rows(resid)
        low_second = (normed2 * ln2_gain + ln2_bias).astype(jnp.bfloat16)
        full_second = gather_rows(low_second)
        hidden_pre = matmul(full_second, fc1_weight) + fc1_bias
        act_value, act_slope = gelu_parts(hidden_pre)
        act_low = act_value.astype(jnp.bfloat16)
        branch = lax.psum_scatter(
            rounded(matmul(act_low, fc2_weight)).astype(jnp.bfloat16),
            "tensor",
            scatter_dimension=1,
            tiled=True,
        ).astype(jnp.float32)
        layer_rows = (resid + branch + fc2_bias) * flag_rows
        out_list.append(layer_rows.astype(jnp.bfloat16).reshape(per_micro, seq_len, feat_local))
        grad_out = (
            split_cot[:, micro_index].reshape(rows, feat_local).astype(jnp.float32) * flag_rows
        )
        grad_full = gather_grads(grad_out.astype(jnp.bfloat16))
        g_fc2w = left_transposed(act_low, grad_full)
        g_fc2b = jnp.sum(grad_out, axis=0)
        hidden_grad = (right_transposed(grad_full, fc2_weight) * act_slope).astype(jnp.bfloat16)
        g_fc1w = left_transposed(full_second, hidden_grad)
        g_fc1b = jnp.sum(hidden_grad.astype(jnp.float32), axis=0)
        grad_second = lax.psum_scatter(
            rounded(right_transposed(hidden_grad, fc1_weight)).astype(jnp.bfloat16),
            "tensor",
            scatter_dimension=1,
            tiled=True,
        ).astype(jnp.float32)
        g_ln2g = jnp.sum(grad_second * normed2, axis=0)
        g_ln2b = jnp.sum(grad_second, axis=0)
        grad_resid = grad_out + norm_back(grad_second, normed2, inverse2, ln2_gain)
        g_ob = jnp.sum(grad_resid, axis=0)
        resid_full = gather_grads(grad_resid.astype(jnp.bfloat16))
        g_ow = left_transposed(context, resid_full)
        grad_context = right_transposed(resid_full, o_weight).astype(jnp.bfloat16)
        context4 = grad_context.reshape(shaped)
        probs = jnp.exp(
            jnp.einsum("nqhd,nkhd->nhqk", query4, keys4, preferred_element_type=jnp.float32) * scale
            - log_total[..., None]
        )
        probs_again = probs.astype(jnp.bfloat16)
        grad_probs = jnp.einsum(
            "nqhd,nkhd->nhqk", context4, values4, preferred_element_type=jnp.float32
        )
        row_delta = jnp.sum(probs * grad_probs, axis=-1)
        grad_scores = (probs * (grad_probs - row_delta[..., None])).astype(jnp.bfloat16)
        grad_query = (
            (
                jnp.einsum(
                    "nhqk,nkhd->nqhd", grad_scores, keys4, preferred_element_type=jnp.float32
                )
                * scale
            )
            .reshape(rows, head_local * HDIM)
            .astype(jnp.bfloat16)
        )
        grad_keys = (
            (
                jnp.einsum(
                    "nhqk,nqhd->nkhd", grad_scores, query4, preferred_element_type=jnp.float32
                )
                * scale
            )
            .reshape(rows, head_local * HDIM)
            .astype(jnp.bfloat16)
        )
        grad_values = (
            jnp.einsum("nhqk,nqhd->nkhd", probs_again, context4, preferred_element_type=jnp.float32)
            .reshape(rows, head_local * HDIM)
            .astype(jnp.bfloat16)
        )
        g_qw = left_transposed(full_first, grad_query)
        g_qb = jnp.sum(grad_query.astype(jnp.float32), axis=0)
        g_kw = left_transposed(full_first, grad_keys)
        g_vw = left_transposed(full_first, grad_values)
        g_vb = jnp.sum(grad_values.astype(jnp.float32), axis=0)
        partial_first = (
            right_transposed(grad_query, q_weight)
            + right_transposed(grad_keys, k_weight)
            + right_transposed(grad_values, v_weight)
        )
        grad_first = lax.psum_scatter(
            rounded(partial_first).astype(jnp.bfloat16), "tensor", scatter_dimension=1, tiled=True
        ).astype(jnp.float32)
        g_ln1g = jnp.sum(grad_first * normed1, axis=0)
        g_ln1b = jnp.sum(grad_first, axis=0)
        grad_input = grad_resid + norm_back(grad_first, normed1, inverse1, ln1_gain)
        grad_list.append(grad_input.astype(jnp.bfloat16).reshape(per_micro, seq_len, feat_local))
        micro_grads = (
            g_ln1g,
            g_ln1b,
            g_qw,
            g_qb,
            g_kw,
            g_vw,
            g_vb,
            g_ow,
            g_ob,
            g_ln2g,
            g_ln2b,
            g_fc1w,
            g_fc1b,
            g_fc2w,
            g_fc2b,
        )
        totals = jax.tree.map(jnp.add, totals, micro_grads)
    totals = (
        lax.psum(totals[0].astype(jnp.bfloat16), "dp").astype(jnp.float32),
        lax.psum(totals[1].astype(jnp.bfloat16), "dp").astype(jnp.float32),
        lax.psum(totals[2].astype(jnp.bfloat16), "dp").astype(jnp.float32),
        lax.psum(totals[3].astype(jnp.bfloat16), "dp").astype(jnp.float32),
        lax.psum(totals[4].astype(jnp.bfloat16), "dp").astype(jnp.float32),
        lax.psum(totals[5].astype(jnp.bfloat16), "dp").astype(jnp.float32),
        lax.psum(totals[6].astype(jnp.bfloat16), "dp").astype(jnp.float32),
        lax.psum(totals[7].astype(jnp.bfloat16), "dp").astype(jnp.float32),
        lax.psum(totals[8].astype(jnp.bfloat16), "dp").astype(jnp.float32),
        lax.psum(totals[9].astype(jnp.bfloat16), "dp").astype(jnp.float32),
        lax.psum(totals[10].astype(jnp.bfloat16), "dp").astype(jnp.float32),
        lax.psum(totals[11].astype(jnp.bfloat16), "dp").astype(jnp.float32),
        lax.psum(totals[12].astype(jnp.bfloat16), "dp").astype(jnp.float32),
        lax.psum(totals[13].astype(jnp.bfloat16), "dp").astype(jnp.float32),
        lax.psum(totals[14].astype(jnp.bfloat16), "dp").astype(jnp.float32),
    )
    layer_out = jnp.stack(out_list, axis=1).reshape(img_local, seq_len, feat_local)
    input_grad = jnp.stack(grad_list, axis=1).reshape(img_local, seq_len, feat_local)
    return (
        layer_out,
        input_grad,
        totals[0],
        totals[1],
        totals[2],
        totals[3],
        totals[4],
        totals[5],
        totals[6],
        totals[7],
        totals[8],
        totals[9],
        totals[10],
        totals[11],
        totals[12],
        totals[13],
        totals[14],
    )


F32 = jnp.float32
BF16 = jnp.bfloat16
LOG2E = math.log2(math.e)
VMEM_BYTES = 58 * 1024 * 1024
COST_SHARE = 0.4
LONG = 4.0
SHORT = 0.05


def dot_nn(left, right):
    return jnp.dot(left, right, preferred_element_type=F32)


def dot_nt(left, right):
    return lax.dot_general(left, right, (((1,), (1,)), ((), ())), preferred_element_type=F32)


def dot_tn(left, right):
    return lax.dot_general(left, right, (((0,), (0,)), ((), ())), preferred_element_type=F32)


def cost(flops, moved, trans=0, share=COST_SHARE):
    return pl.CostEstimate(
        flops=int(flops * share),
        bytes_accessed=int(moved * share),
        transcendentals=int(trans * share),
    )


def params(grid_dims):
    return pltpu.CompilerParams(
        dimension_semantics=("arbitrary",) * grid_dims, vmem_limit_bytes=VMEM_BYTES
    )


def once(shape, spot=None):
    spot = spot or (0,) * len(shape)
    return pl.BlockSpec(shape, lambda *_: spot, pipeline_mode=pl.Buffered(1))


def image_block(shape, offset=0):
    return pl.BlockSpec((1,) + shape, lambda i, *_: (offset + i, 0, 0))


ANYWHERE = pl.BlockSpec(memory_space=pl.ANY)


def column_stats(values):
    mean = jnp.mean(values, axis=0, keepdims=True)
    centred = values - mean
    inverse = lax.rsqrt(jnp.mean(centred * centred, axis=0, keepdims=True) + EPS)
    return centred * inverse, inverse


def join_halves(first, own, other):
    return jnp.concatenate(
        [jnp.where(first, own, other), jnp.where(first, other, own)], axis=0
    )


def split_halves(first, full):
    half = full.shape[0] // 2
    low, high = full[:half], full[half:]
    return jnp.where(first, low, high), jnp.where(first, high, low)


def token_sum(values):
    return jnp.sum(values, axis=1, keepdims=True)


LN1_GAIN, LN1_BIAS, O_BIAS, LN2_GAIN, LN2_BIAS, FC2_BIAS = range(6)


def as_row(column_sum):
    rows = column_sum.shape[0]
    return jnp.broadcast_to(column_sum, (rows, 128)).T[0:1]


def column(ref, index):
    return ref[:, index : index + 1]


def write_rows(row_refs, sum_refs):
    @pl.when(pl.program_id(0) == pl.num_programs(0) - 1)
    def _():
        for row_ref, sum_ref in zip(row_refs, sum_refs):
            row_ref[...] = as_row(sum_ref[...])


def store_heads(out_ref, first, product):
    head_dim = out_ref.shape[2]
    for head in range(product.shape[0] // head_dim):
        out_ref[0, first + head] = product[head * head_dim : (head + 1) * head_dim].astype(BF16)


def first_norm_kernel(
    place_ref, own_ref, other_ref, feature_ref, q_ref, k_ref, v_ref, head_ref, *rest
):
    rows_ref, normed_ref, qkv_ref = rest[-3:]
    full = join_halves(place_ref[0] == 0, own_ref[0].astype(F32), other_ref[0].astype(F32))
    rows_ref[0] = full.astype(BF16)
    normed, _ = column_stats(full)
    low = (normed * column(feature_ref, LN1_GAIN) + column(feature_ref, LN1_BIAS)).astype(BF16)
    normed_ref[0] = low
    heads = qkv_ref.shape[1] // 3
    store_heads(qkv_ref, 0, dot_nn(q_ref[...], low) + column(head_ref, 0))
    store_heads(qkv_ref, heads, dot_nn(k_ref[...], low))
    store_heads(qkv_ref, 2 * heads, dot_nn(v_ref[...], low) + column(head_ref, 1))


def first_norm(index, count, place, images, other, features, weights, head_vectors, earlier):
    _, half, seq = images.shape
    width, feat = weights[0].shape
    groups = 3 * width // HDIM
    held = list(earlier) if earlier else []
    return pl.pallas_call(
        first_norm_kernel,
        out_shape=[
            jax.ShapeDtypeStruct((count, feat, seq), BF16),
            jax.ShapeDtypeStruct((count, feat, seq), BF16),
            jax.ShapeDtypeStruct((count, groups, HDIM, seq), BF16),
        ],
        grid_spec=pltpu.PrefetchScalarGridSpec(
            num_scalar_prefetch=1,
            grid=(1,),
            in_specs=[
                pl.BlockSpec((1, half, seq), lambda i, p: (p[0] * count + index, 0, 0)),
                once((1, half, seq)),
                once((feat, 8)),
                once((width, feat)),
                once((width, feat)),
                once((width, feat)),
                once((width, 8)),
            ]
            + [ANYWHERE] * len(held),
            out_specs=[
                once((1, feat, seq), (index, 0, 0)),
                once((1, feat, seq), (index, 0, 0)),
                once((1, groups, HDIM, seq), (index, 0, 0, 0)),
            ],
        ),
        input_output_aliases={8 + k: k for k in range(len(held))},
        compiler_params=params(1),
        cost_estimate=cost(6 * seq * feat * width, 12 << 20, 0, SHORT),
        name="first_norm",
    )(place, images, other, features, *weights, head_vectors, *held)


def project_kernel(normed_ref, q_ref, k_ref, v_ref, head_ref, qkv_ref):
    low = normed_ref[0]
    heads = qkv_ref.shape[1] // 3
    store_heads(qkv_ref, 0, dot_nn(q_ref[...], low) + column(head_ref, 2))
    store_heads(qkv_ref, heads, dot_nn(k_ref[...], low))
    store_heads(qkv_ref, 2 * heads, dot_nn(v_ref[...], low) + column(head_ref, 3))


def project(normed, weight, head_vectors, width):
    count, feat, seq = normed.shape
    groups = 3 * width // HDIM
    return pl.pallas_call(
        project_kernel,
        grid=(count,),
        out_shape=jax.ShapeDtypeStruct((count, groups, HDIM, seq), BF16),
        in_specs=[
            image_block((feat, seq)),
            once((width, feat), (0, 0)),
            once((width, feat), (1, 0)),
            once((width, feat), (2, 0)),
            once((width, 8)),
        ],
        out_specs=pl.BlockSpec((1, groups, HDIM, seq), lambda i: (i, 0, 0, 0)),
        compiler_params=params(1),
        cost_estimate=cost(6 * count * seq * feat * width, 20 << 20),
        name="project",
    )(normed, weight, weight, weight, head_vectors)


def mix_kernel(q_ref, k_ref, v_ref, *rest, scale):
    out_ref, log_ref = rest[-2:]
    factor = scale * LOG2E
    for head in range(q_ref.shape[1]):
        scores = dot_tn(k_ref[0, head], q_ref[0, head])
        top = jnp.max(scores, axis=0, keepdims=True)
        probs = jnp.exp2((scores - top) * factor)
        total = jnp.sum(probs, axis=0, keepdims=True)
        mixed = dot_nn(v_ref[0, head], probs.astype(BF16))
        out_ref[0, head] = (mixed * (1.0 / total)).astype(BF16)
        log_ref[0, head] = top * factor + jnp.log2(total)


def mix(qkv, half, start, steps, earlier, per_step=1):
    count, groups, head_dim, seq = qkv.shape
    heads = groups // 3
    blocks = heads // per_step
    block = (1, per_step, head_dim, seq)
    held = list(earlier) if earlier else []

    def at(offset):
        return pl.BlockSpec(block, lambda i, j: (start + i, offset + j, 0, 0))

    return pl.pallas_call(
        functools.partial(mix_kernel, scale=1.0 / math.sqrt(head_dim)),
        grid=(steps, blocks),
        out_shape=[
            jax.ShapeDtypeStruct((count, 2 * heads, head_dim, seq), BF16),
            jax.ShapeDtypeStruct((count, 2 * heads, 1, seq), F32),
        ],
        in_specs=[at(0), at(blocks), at(2 * blocks)] + [ANYWHERE] * len(held),
        out_specs=[
            at(half * blocks),
            pl.BlockSpec(
                (1, per_step, 1, seq), lambda i, j: (start + i, half * blocks + j, 0, 0)
            ),
        ],
        input_output_aliases={3 + k: k for k in range(len(held))},
        compiler_params=params(2),
        cost_estimate=cost(
            4 * steps * heads * seq * seq * 256,
            steps * heads * head_dim * seq * 8,
            steps * heads * seq * seq,
            SHORT if steps == 1 else COST_SHARE,
        ),
        name="mix",
    )(qkv, qkv, qkv, *held)


def mix_back_kernel(q_ref, k_ref, v_ref, out_ref, log_ref, grad_ref, *rest, scale, heads):
    d_ref = rest[-1]
    factor = scale * LOG2E
    per_step = q_ref.shape[1]
    first = pl.program_id(1) * per_step
    for head in range(per_step):
        query, keys, values = q_ref[0, head], k_ref[0, head], v_ref[0, head]
        grad = grad_ref[0, head]
        delta = jnp.sum(grad.astype(F32) * out_ref[0, head].astype(F32), axis=0, keepdims=True)
        probs = jnp.exp2(dot_tn(keys, query) * factor - log_ref[0, head])
        grad_scores = (probs * (dot_tn(values, grad) - delta)).astype(BF16)
        d_ref[0, 2 * heads + first + head] = dot_nt(grad, probs.astype(BF16)).astype(BF16)
        d_ref[0, first + head] = (dot_nn(keys, grad_scores) * scale).astype(BF16)
        d_ref[0, heads + first + head] = (dot_nt(query, grad_scores) * scale).astype(BF16)


def mix_back(qkv, out, log_total, grad, half, start, steps, earlier, per_step=2):
    count, groups, head_dim, seq = qkv.shape
    heads = groups // 3
    blocks = heads // per_step
    block = (1, per_step, head_dim, seq)
    held = [] if earlier is None else [earlier]

    def at(offset):
        return pl.BlockSpec(block, lambda i, j: (start + i, offset + j, 0, 0))

    return pl.pallas_call(
        functools.partial(mix_back_kernel, scale=1.0 / math.sqrt(head_dim), heads=heads),
        grid=(steps, blocks),
        out_shape=jax.ShapeDtypeStruct(qkv.shape, BF16),
        in_specs=[
            at(0),
            at(blocks),
            at(2 * blocks),
            at(half * blocks),
            pl.BlockSpec((1, per_step, 1, seq), lambda i, j: (start + i, half * blocks + j, 0, 0)),
            at(half * blocks),
        ]
        + [ANYWHERE] * len(held),
        input_output_aliases={6: 0} if held else {},
        out_specs=pl.BlockSpec((1, groups, head_dim, seq), lambda i, j: (start + i, 0, 0, 0)),
        compiler_params=params(2),
        cost_estimate=cost(
            10 * steps * heads * seq * seq * 256,
            steps * heads * head_dim * seq * 16,
            steps * heads * seq * seq,
            SHORT if steps == 1 else COST_SHARE,
        ),
        name="mix_back",
    )(qkv, qkv, qkv, out, log_total, grad, *held)


def second_norm_kernel(
    place_ref,
    ctx_ref,
    w_own_ref,
    w_other_ref,
    rows_ref,
    feature_ref,
    cot_own_ref,
    *rest,
):
    *cot_refs, resid_ref, low_ref, grad_ref, row_ref, w_ref, sum_ref = rest
    step = pl.program_id(0)
    half = w_own_ref.shape[0]

    @pl.when(step == 0)
    def _():
        w_ref[:half] = w_own_ref[...]
        w_ref[half:] = w_other_ref[...]
        sum_ref[...] = jnp.zeros_like(sum_ref)

    resid = rows_ref[0].astype(F32) + dot_tn(w_ref[...], ctx_ref[0])
    resid += column(feature_ref, O_BIAS)
    resid_ref[0] = resid.astype(BF16)
    normed, _ = column_stats(resid)
    low_ref[0] = (
        normed * column(feature_ref, LN2_GAIN) + column(feature_ref, LN2_BIAS)
    ).astype(BF16)
    flag = place_ref[2 + place_ref[0] * pl.num_programs(0) + step].astype(F32)
    cot_other = cot_refs[0][0]
    for index in range(1, len(cot_refs)):
        cot_other = jnp.where(step == index, cot_refs[index][0], cot_other)
    grad = flag * join_halves(
        place_ref[0] == 0, cot_own_ref[0].astype(F32), cot_other.astype(F32)
    )
    grad_ref[0] = grad.astype(BF16)
    sum_ref[...] += token_sum(grad)
    write_rows((row_ref,), (sum_ref,))


def second_norm(place, ctx, w_own, w_other, rows, features, cot, cot_other):
    count, feat, seq = rows.shape
    half = w_own.shape[0]
    full = image_block((feat, seq))
    return pl.pallas_call(
        second_norm_kernel,
        out_shape=[
            jax.ShapeDtypeStruct((count, feat, seq), BF16),
            jax.ShapeDtypeStruct((count, feat, seq), BF16),
            jax.ShapeDtypeStruct((count, feat, seq), BF16),
            jax.ShapeDtypeStruct((1, feat), F32),
        ],
        grid_spec=pltpu.PrefetchScalarGridSpec(
            num_scalar_prefetch=1,
            grid=(count,),
            in_specs=[
                full,
                once((half, feat)),
                once((half, feat), (3, 0)),
                full,
                once((feat, 8)),
                pl.BlockSpec((1, feat // 2, seq), lambda i, p: (p[0] * count + i, 0, 0)),
            ]
            + [once((1, feat // 2, seq))] * count,
            out_specs=[full, full, full, once((1, feat))],
            scratch_shapes=[pltpu.VMEM((feat, feat), BF16), pltpu.VMEM((feat, 1), F32)],
        ),
        compiler_params=params(1),
        cost_estimate=cost(4 * count * seq * half * feat, 40 << 20),
        name="second_norm",
    )(place, ctx, w_own, w_other, rows, features, cot, *cot_other)


def hidden_kernel(place_ref, low_ref, grad_ref, fc1_ref, fc2_ref, bias_ref, *rest, which):
    act_ref, back_ref, gb_ref, g1_ref, g2_ref = rest[-5:]
    g1, g2, gb = None, None, None
    for image in range(low_ref.shape[0]):
        low, grad = low_ref[image], grad_ref[image]
        pre = dot_nn(fc1_ref[...], low) + column(bias_ref, which)
        square = pre * pre
        tanh_val = jnp.tanh(pre * (GELU_C + (GELU_C * GELU_A) * square))
        half = 0.5 * tanh_val + 0.5
        act = pre * half
        slope = half + act * (1.0 - half) * (2 * GELU_C + (6 * GELU_C * GELU_A) * square)
        act = act.astype(BF16)
        act_ref[image] = act
        back = (dot_nn(fc2_ref[...], grad) * slope).astype(BF16)
        back_ref[image] = back
        parts = dot_nt(back, low), dot_nt(act, grad), token_sum(back.astype(F32))
        g1 = parts[0] if g1 is None else g1 + parts[0]
        g2 = parts[1] if g2 is None else g2 + parts[1]
        gb = parts[2] if gb is None else gb + parts[2]
    gb_ref[...] = gb
    g1_ref[...] = g1.astype(BF16)
    g2_ref[...] = g2.astype(BF16)


def quarter_rows(hidden):
    return (-(-hidden // 4) + 7) // 8 * 8


def hidden_stage(keep, place, low, grad, fc1, fc2, fc2_offset, bias, which, earlier):
    count, feat, seq = low.shape
    hidden = bias.shape[0]
    block = quarter_rows(hidden)
    held = list(earlier) if earlier else []

    def chunk(j, p):
        return j + 2 * (p[1] if keep else 1 - p[1])

    weight = pl.BlockSpec((block, feat), lambda j, p: (chunk(j, p), 0))
    tokens = pl.BlockSpec((count, block, seq), lambda j, p: (0, chunk(j, p), 0))
    grads = pl.BlockSpec((block, feat), lambda j, p: (j, 0))
    part = jax.ShapeDtypeStruct((2 * block, feat), BF16)
    return pl.pallas_call(
        functools.partial(hidden_kernel, which=which),
        out_shape=[
            jax.ShapeDtypeStruct((count, hidden, seq), BF16),
            jax.ShapeDtypeStruct((count, hidden, seq), BF16),
            jax.ShapeDtypeStruct((hidden, 1), F32),
            part,
            part,
        ],
        grid_spec=pltpu.PrefetchScalarGridSpec(
            num_scalar_prefetch=1,
            grid=(2,),
            in_specs=[
                once((count, feat, seq)),
                once((count, feat, seq)),
                weight,
                pl.BlockSpec((block, feat), lambda j, p: (fc2_offset + chunk(j, p), 0)),
                pl.BlockSpec((block, 2), lambda j, p: (chunk(j, p), 0)),
            ]
            + [ANYWHERE] * len(held),
            out_specs=[
                tokens,
                tokens,
                pl.BlockSpec((block, 1), lambda j, p: (chunk(j, p), 0)),
                grads,
                grads,
            ],
        ),
        input_output_aliases={6 + k: k for k in range(len(held))},
        compiler_params=params(1),
        cost_estimate=cost(4 * count * seq * feat * hidden, 30 << 20, 0, LONG),
        name="hidden_stage",
    )(place, low, grad, fc1, fc2, bias, *held)


def layer_kernel(
    place_ref,
    act_own_ref,
    act_other_ref,
    w_own_ref,
    w_other_ref,
    resid_ref,
    b_ref,
    out_ref,
    send_ref,
    last_ref,
):
    step, count = pl.program_id(0), pl.num_programs(0)
    hidden = act_own_ref.shape[1]
    branch = dot_tn(w_own_ref[:hidden], act_own_ref[0])
    branch += dot_tn(w_other_ref[:hidden], act_other_ref[0])
    flag = place_ref[2 + place_ref[0] * count + step].astype(F32)
    result = (resid_ref[0].astype(F32) + branch + column(b_ref, FC2_BIAS)) * flag
    own, other = split_halves(place_ref[0] == 0, result)
    out_ref[0] = own.astype(BF16)
    other = other.astype(BF16)

    @pl.when(step < count - 1)
    def _():
        send_ref[0] = other

    @pl.when(step == count - 1)
    def _():
        last_ref[0] = other


def layer_result(place, act_own, act_other, w_own, w_other, resid, features):
    count, feat, seq = resid.shape
    hidden = act_own.shape[1]
    full = image_block((hidden, seq))
    padded = 4 * quarter_rows(hidden)
    part = (1, feat // 2, seq)
    return pl.pallas_call(
        layer_kernel,
        out_shape=[
            jax.ShapeDtypeStruct((2 * count, feat // 2, seq), BF16),
            jax.ShapeDtypeStruct((count - 1, feat // 2, seq), BF16),
            jax.ShapeDtypeStruct(part, BF16),
        ],
        grid_spec=pltpu.PrefetchScalarGridSpec(
            num_scalar_prefetch=1,
            grid=(count,),
            in_specs=[
                full,
                full,
                once((hidden, feat)),
                once((padded, feat), (1, 0)),
                image_block((feat, seq)),
                once((feat, 8)),
            ],
            out_specs=[
                pl.BlockSpec(part, lambda i, p: (p[0] * count + i, 0, 0)),
                pl.BlockSpec(part, lambda i, p: (jnp.minimum(i, count - 2), 0, 0)),
                once(part),
            ],
        ),
        compiler_params=params(1),
        cost_estimate=cost(4 * count * seq * feat * hidden, count * (12 << 20), 0, LONG),
        name="layer_result",
    )(place, act_own, act_other, w_own, w_other, resid, features)


def resid_back_kernel(
    back_own_ref,
    back_other_ref,
    w_own_ref,
    w_other_ref,
    resid_ref,
    grad_ref,
    gain_ref,
    low_ref,
    row_gain_ref,
    row_bias_ref,
    row_ob_ref,
    sum_gain_ref,
    sum_bias_ref,
    sum_ob_ref,
):
    hidden = back_own_ref.shape[1]
    grad_norm = dot_tn(w_own_ref[:hidden], back_own_ref[0])
    grad_norm += dot_tn(w_other_ref[:hidden], back_other_ref[0])
    normed, inverse = column_stats(resid_ref[0].astype(F32))
    scaled = grad_norm * column(gain_ref, LN2_GAIN)
    plain = jnp.mean(scaled, axis=0, keepdims=True)
    cross = jnp.mean(scaled * normed, axis=0, keepdims=True)
    grad = grad_ref[0].astype(F32) + inverse * (scaled - plain - normed * cross)
    low_ref[0] = grad.astype(BF16)

    @pl.when(pl.program_id(0) == 0)
    def _():
        sum_gain_ref[...] = jnp.zeros_like(sum_gain_ref)
        sum_bias_ref[...] = jnp.zeros_like(sum_bias_ref)
        sum_ob_ref[...] = jnp.zeros_like(sum_ob_ref)

    sum_gain_ref[...] += token_sum(grad_norm * normed)
    sum_bias_ref[...] += token_sum(grad_norm)
    sum_ob_ref[...] += token_sum(grad)
    write_rows((row_gain_ref, row_bias_ref, row_ob_ref), (sum_gain_ref, sum_bias_ref, sum_ob_ref))


def resid_back(back_own, back_other, w_own, w_other, resid, grad, gain):
    count, feat, seq = resid.shape
    hidden = back_own.shape[1]
    padded = 4 * quarter_rows(hidden)
    wide = image_block((hidden, seq))
    full = image_block((feat, seq))
    return pl.pallas_call(
        resid_back_kernel,
        grid=(count,),
        out_shape=[jax.ShapeDtypeStruct((count, feat, seq), BF16)]
        + [jax.ShapeDtypeStruct((1, feat), F32)] * 3,
        in_specs=[
            wide,
            wide,
            once((hidden, feat)),
            once((padded, feat)),
            full,
            full,
            once((feat, 8)),
        ],
        out_specs=[full] + [once((1, feat))] * 3,
        scratch_shapes=[pltpu.VMEM((feat, 1), F32)] * 3,
        compiler_params=params(1),
        cost_estimate=cost(4 * count * seq * feat * hidden, 50 << 20),
        name="resid_back",
    )(back_own, back_other, w_own, w_other, resid, grad, gain)


def context_back_kernel(
    place_ref,
    low_ref,
    ctx_ref,
    w_own_ref,
    w_other_ref,
    d_ref,
    own_keep_ref,
    own_send_ref,
    other_keep_ref,
    other_send_ref,
    acc_ref,
):
    step = pl.program_id(0)
    low = low_ref[0]
    half = w_own_ref.shape[0]
    d_ref[0, :half] = dot_nn(w_own_ref[...], low).astype(BF16)
    d_ref[0, half:] = dot_nn(w_other_ref[...], low).astype(BF16)
    product = dot_nt(ctx_ref[0], low)

    @pl.when(step == 0)
    def _():
        acc_ref[...] = product

    @pl.when(step > 0)
    def _():
        acc_ref[...] += product

    @pl.when(step == pl.num_programs(0) - 1)
    def _():
        part = half // 2
        keep = place_ref[1] * part
        send = part - keep
        own_keep_ref[...] = acc_ref[pl.ds(pl.multiple_of(keep, 8), part)].astype(BF16)
        own_send_ref[...] = acc_ref[pl.ds(pl.multiple_of(send, 8), part)].astype(BF16)
        other_keep_ref[...] = acc_ref[pl.ds(pl.multiple_of(half + keep, 8), part)].astype(BF16)
        other_send_ref[...] = acc_ref[pl.ds(pl.multiple_of(half + send, 8), part)].astype(BF16)


def context_back(place, low, ctx, w_own, w_other):
    count, feat, seq = low.shape
    half = w_own.shape[0]
    full = image_block((feat, seq))
    part = jax.ShapeDtypeStruct((half // 2, feat), BF16)
    return pl.pallas_call(
        context_back_kernel,
        out_shape=[jax.ShapeDtypeStruct((count, 2 * half, seq), BF16)] + [part] * 4,
        grid_spec=pltpu.PrefetchScalarGridSpec(
            num_scalar_prefetch=1,
            grid=(count,),
            in_specs=[
                full,
                image_block((2 * half, seq)),
                once((half, feat)),
                once((half, feat), (3, 0)),
            ],
            out_specs=[image_block((2 * half, seq))] + [once((half // 2, feat))] * 4,
            scratch_shapes=[pltpu.VMEM((2 * half, feat), F32)],
        ),
        compiler_params=params(1),
        cost_estimate=cost(8 * count * seq * half * feat, 25 << 20),
        name="context_back",
    )(place, low, ctx, w_own, w_other)


def project_back_kernel(place_ref, normed_ref, d_ref, keep_ref, send_ref, col_ref, acc_ref):
    step = pl.program_id(0)
    product = dot_nt(d_ref[0], normed_ref[0])
    column = token_sum(d_ref[0].astype(F32))

    @pl.when(step == 0)
    def _():
        acc_ref[...] = product
        col_ref[...] = column

    @pl.when(step > 0)
    def _():
        acc_ref[...] += product
        col_ref[...] += column

    @pl.when(step == pl.num_programs(0) - 1)
    def _():
        part = keep_ref.shape[0] // 3
        keep = place_ref[1] * part
        for index in range(3):
            rows = slice(index * part, (index + 1) * part)
            first = 2 * index * part
            keep_rows = pl.ds(pl.multiple_of(first + keep, 8), part)
            send_rows = pl.ds(pl.multiple_of(first + part - keep, 8), part)
            keep_ref[rows] = acc_ref[keep_rows].astype(BF16)
            send_ref[rows] = acc_ref[send_rows].astype(BF16)


def project_back(place, normed, d_qkv):
    count, feat, seq = normed.shape
    width = d_qkv.shape[1]
    part = jax.ShapeDtypeStruct((width // 2, feat), BF16)
    return pl.pallas_call(
        project_back_kernel,
        out_shape=[part, part, jax.ShapeDtypeStruct((width, 1), F32)],
        grid_spec=pltpu.PrefetchScalarGridSpec(
            num_scalar_prefetch=1,
            grid=(count,),
            in_specs=[image_block((feat, seq)), image_block((width, seq))],
            out_specs=[
                once((width // 2, feat)),
                once((width // 2, feat)),
                once((width, 1)),
            ],
            scratch_shapes=[pltpu.VMEM((width, feat), F32)],
        ),
        compiler_params=params(1),
        cost_estimate=cost(2 * count * seq * feat * width, 20 << 20),
        name="project_back",
    )(place, normed, d_qkv)


def input_back_kernel(
    place_ref,
    d_own_ref,
    d_other_ref,
    q_ref,
    k_ref,
    v_ref,
    w_other_ref,
    rows_ref,
    low_ref,
    gain_ref,
    *rest,
):
    out_ref, send_ref, row_gain_ref, row_bias_ref, w_ref, sum_gain_ref, sum_bias_ref = rest[-7:]
    width = q_ref.shape[0]

    @pl.when(pl.program_id(0) == 0)
    def _():
        w_ref[:width] = q_ref[...]
        w_ref[width : 2 * width] = k_ref[...]
        w_ref[2 * width :] = v_ref[...]
        sum_gain_ref[...] = jnp.zeros_like(sum_gain_ref)
        sum_bias_ref[...] = jnp.zeros_like(sum_bias_ref)

    grad_norm = dot_tn(w_ref[...], d_own_ref[0]) + dot_tn(w_other_ref[...], d_other_ref[0])
    normed, inverse = column_stats(rows_ref[0].astype(F32))
    scaled = grad_norm * column(gain_ref, LN1_GAIN)
    plain = jnp.mean(scaled, axis=0, keepdims=True)
    cross = jnp.mean(scaled * normed, axis=0, keepdims=True)
    grad = low_ref[0].astype(F32) + inverse * (scaled - plain - normed * cross)
    own, other = split_halves(place_ref[0] == 0, grad)
    out_ref[0] = own.astype(BF16)
    send_ref[0] = other.astype(BF16)
    sum_gain_ref[...] += token_sum(grad_norm * normed)
    sum_bias_ref[...] += token_sum(grad_norm)
    write_rows((row_gain_ref, row_bias_ref), (sum_gain_ref, sum_bias_ref))


def input_back(place, d_own, d_other, weights, w_other, rows, low, features, start, steps, held):
    count, width, seq = d_own.shape
    feat = rows.shape[1]
    wide = image_block((width, seq), start)
    full = image_block((feat, seq), start)
    held = [] if held is None else [held]
    return pl.pallas_call(
        input_back_kernel,
        out_shape=[
            jax.ShapeDtypeStruct((2 * count, feat // 2, seq), BF16),
            jax.ShapeDtypeStruct((steps, feat // 2, seq), BF16),
            jax.ShapeDtypeStruct((1, feat), F32),
            jax.ShapeDtypeStruct((1, feat), F32),
        ],
        grid_spec=pltpu.PrefetchScalarGridSpec(
            num_scalar_prefetch=1,
            grid=(steps,),
            in_specs=[wide, wide]
            + [once((width // 3, feat))] * 3
            + [once((width, feat)), full, full, once((feat, 8))]
            + [ANYWHERE] * len(held),
            out_specs=[
                pl.BlockSpec((1, feat // 2, seq), lambda i, p: (p[0] * count + start + i, 0, 0)),
                image_block((feat // 2, seq)),
                once((1, feat)),
                once((1, feat)),
            ],
            scratch_shapes=[
                pltpu.VMEM((width, feat), BF16),
                pltpu.VMEM((feat, 1), F32),
                pltpu.VMEM((feat, 1), F32),
            ],
        ),
        input_output_aliases={10: 0} if held else {},
        compiler_params=params(1),
        cost_estimate=cost(4 * steps * seq * feat * width, steps * (11 << 20) + (8 << 20), 0, LONG),
        name="input_back",
    )(place, d_own, d_other, *weights, w_other, rows, low, features, *held)


def widen_kernel(place_ref, mine_ref, other_ref, *out_refs, steps):
    half, step = pl.program_id(1), pl.program_id(2)
    mine = half == place_ref[1]
    value = jnp.where(mine, mine_ref[...], other_ref[...]).astype(F32)
    for index, out_ref in enumerate(out_refs):

        @pl.when(pl.program_id(0) == index)
        def _():
            out_ref[...] = value


def widen(place, mine, other, part, total, steps, count=1):
    feat = mine.shape[1]
    rows = part // steps
    last = 2 * steps - 1

    def mine_spot(w, h, i, p):
        used = 1 - (h - p[1]) * (h - p[1])
        return (w * steps + i * used, 0)

    def other_spot(w, h, i, p):
        used = (h - p[1]) * (h - p[1])
        return (w * steps + i * used, 0)

    def out_spot(index):
        return lambda w, h, i, p: (jnp.clip((w - index) * 2 * steps + h * steps + i, 0, last), 0)

    out = pl.pallas_call(
        functools.partial(widen_kernel, steps=steps),
        out_shape=[jax.ShapeDtypeStruct((total, feat), F32)] * count,
        grid_spec=pltpu.PrefetchScalarGridSpec(
            num_scalar_prefetch=1,
            grid=(count, 2, steps),
            in_specs=[
                pl.BlockSpec((rows, feat), mine_spot),
                pl.BlockSpec((rows, feat), other_spot),
            ],
            out_specs=[pl.BlockSpec((rows, feat), out_spot(index)) for index in range(count)],
        ),
        compiler_params=params(3),
        cost_estimate=cost(0, 8 * total * feat * count, 0, SHORT),
        name="widen",
    )(place, mine, other)
    return out if count > 1 else out[0]


def swap_tensor(value):
    return lax.ppermute(value, "tensor", [(0, 1), (1, 0)])


def swap_core(value):
    return lax.ppermute(value, "dp", [(spot, spot ^ 1) for spot in range(lax.axis_size("dp"))])


def exchange_sum(value, steps):
    total = value
    for step in steps:
        pairs = [(spot, spot ^ step) for spot in range(lax.axis_size("dp"))]
        total += lax.ppermute(value, "dp", pairs)
    return total


def other_weights(weights, spots, rows):
    per_weight = spots // len(weights)
    mine = lax.axis_index("dp")
    start = mine % per_weight * rows
    piece = None
    for index, weight in enumerate(weights):
        short = per_weight * rows - weight.shape[0]
        if short:
            weight = jnp.pad(weight, ((0, short), (0, 0)))
        part = lax.dynamic_slice_in_dim(weight, start, rows, 0)
        piece = part if piece is None else jnp.where(mine // per_weight == index, part, piece)
    return piece


def chip_groups(order):
    spots = lax.axis_size("dp")
    groups = [list(range(core, spots, 2)) for core in range(2)]
    return groups[::-1] if order else groups


def swap_step(value, step):
    return lax.ppermute(value, "dp", [(spot, spot ^ step) for spot in range(lax.axis_size("dp"))])


def side(step):
    return lax.axis_index("dp") // step % 2


def halves(value, step):
    rows = value.shape[0] // 2
    mine = side(step)
    keep = lax.dynamic_slice_in_dim(value, mine * rows, rows, 0)
    return keep, lax.dynamic_slice_in_dim(value, (1 - mine) * rows, rows, 0)


def ranked(mine, other, step):
    first = side(step) == 0
    return jnp.concatenate([jnp.where(first, mine, other), jnp.where(first, other, mine)])


def added(left, right):
    return (left.astype(F32) + right.astype(F32)).astype(BF16)


def both(keep, send):
    return keep.astype(F32) + swap_core(send).astype(F32)


def after(value, *others):
    return lax.optimization_barrier((value, *others))[0]


def whole_device(
    images,
    valid_flags,
    cotangent,
    ln1_gain,
    ln1_bias,
    q_weight,
    q_bias,
    k_weight,
    v_weight,
    v_bias,
    o_weight,
    o_bias,
    ln2_gain,
    ln2_bias,
    fc1_weight,
    fc1_bias,
    fc2_weight,
    fc2_bias,
):
    img_local, seq, half = images.shape
    count = img_local // 2
    feat = 2 * half
    spots = lax.axis_size("dp")
    width = q_weight.shape[1]
    hidden = fc1_weight.shape[1]
    heads = width // HDIM
    tensor = lax.axis_index("tensor")
    core = lax.axis_index("dp") % 2
    place = jnp.concatenate(
        [jnp.stack([tensor, core]).astype(jnp.int32), valid_flags.astype(jnp.int32)]
    )
    images, cotangent = jnp.swapaxes(images, 1, 2), jnp.swapaxes(cotangent, 1, 2)
    in_weights = [q_weight.T, k_weight.T, v_weight.T]
    fc1_own = fc1_weight.T

    def to_send(array, index, images=1):
        return lax.dynamic_slice_in_dim(array, (1 - tensor) * count + index, images, 0)

    small = jnp.concatenate(
        [ln1_gain, ln1_bias, o_bias, ln2_gain, ln2_bias, fc2_bias, q_bias, v_bias, fc1_bias]
    )
    cut_q, cut_v, cut_h = 6 * half, 6 * half + width, 6 * half + 2 * width
    block = quarter_rows(hidden)

    in_piece = other_weights([*in_weights, o_weight], spots, width // (spots // 4))
    first = to_send(images, 0)
    in_piece, first = lax.optimization_barrier((in_piece, first))
    images_other = [swap_tensor(first)]
    in_piece, small_other = swap_tensor(in_piece), swap_tensor(after(small, first))
    mlp_piece = other_weights([fc1_own, fc2_weight], spots, block // 2)
    next_image = to_send(images, 1)
    next_image, images_other[0], in_piece = lax.optimization_barrier(
        (next_image, images_other[0], in_piece)
    )
    in_other = lax.all_gather(in_piece, "dp", axis=0, tiled=True)
    images_other.append(swap_tensor(next_image))

    def features_of(source):
        return source[:cut_q].reshape(6, half)

    feature_own, feature_other = features_of(small), features_of(small_other)
    features = jnp.where(
        tensor == 0,
        jnp.concatenate([feature_own, feature_other], axis=1),
        jnp.concatenate([feature_other, feature_own], axis=1),
    )
    features = jnp.pad(features, ((0, 2), (0, 0))).astype(F32).T
    head_vectors = jnp.stack([small, small_other])[:, cut_q:cut_h].reshape(4, width)
    head_vectors = jnp.pad(head_vectors, ((0, 4), (0, 0))).astype(F32).T
    hidden_vectors = jnp.stack([small, small_other])[:, cut_h:].astype(F32).T

    state = None
    mixed = None
    for index in range(count):
        state = first_norm(
            index,
            count,
            place,
            images,
            images_other[index],
            features,
            in_weights,
            head_vectors,
            state,
        )
        state = list(state)
        if index == 0:
            mlp_piece, state[2] = lax.optimization_barrier((mlp_piece, state[2]))
            mlp_piece = swap_tensor(mlp_piece)
        if index == 1:
            mlp_piece, state[2] = lax.optimization_barrier((mlp_piece, state[2]))
            mlp_other = lax.all_gather(mlp_piece, "dp", axis=0, tiled=True)
        mixed = list(mix(state[2], 0, index, 1, mixed))
        if index + 2 < count:
            next_image = to_send(images, index + 2)
            next_image, images_other[-1], mixed[0] = lax.optimization_barrier(
                (next_image, images_other[-1], mixed[0])
            )
            images_other.append(swap_tensor(next_image))
        elif index + 2 == count:
            late = [to_send(cotangent, spot) for spot in range(count)]
            images_other[-1], mixed[0], *late = lax.optimization_barrier(
                (images_other[-1], mixed[0], *late)
            )
            cot_other = [swap_tensor(value) for value in late]
    rows, normed, qkv_own = state
    qkv_other = project(normed, in_other, head_vectors, width)
    ctx, logs = mix(qkv_other, 1, 0, count, mixed)
    ctx, *cot_other = lax.optimization_barrier((ctx, *cot_other))
    flat = (count, 2 * width, seq)
    resid, low_second, grad_out, sum_fc2b = second_norm(
        place, ctx.reshape(flat), o_weight, in_other, rows, features, cotangent, cot_other
    )

    def stage(keep, place, weights, offset, which, earlier):
        return hidden_stage(
            keep, place, low_second, grad_out, *weights, offset, hidden_vectors, which, earlier
        )

    *held, fc1_o, fc2_o = stage(False, place, (mlp_other, mlp_other), 4, 1, None)
    *stage_other, fc1_k, fc2_k = stage(True, place, (mlp_other, mlp_other), 4, 1, held)
    rows_a = 4 * block // 3 // 8 * 8
    rows_b = 2 * block - rows_a
    fc1_r, fc2_r = swap_core(fc1_o), swap_core(fc2_o)

    def summed(keep, arrived, low, high):
        return (keep[low:high].astype(F32) + arrived[low:high].astype(F32)).astype(BF16)

    piece = summed(fc1_k, fc1_r, 0, rows_a)
    later = (
        summed(fc1_k, fc1_r, rows_a, 2 * block),
        summed(fc2_k, fc2_r, 0, rows_a - rows_b),
        summed(fc2_k, fc2_r, rows_a - rows_b, 2 * block),
    )
    place2, piece, *later = lax.optimization_barrier((place, piece, *later))
    fc1_arrived = [swap_tensor(piece)]
    *held, fc1_o, fc2_o = stage(False, place2, (fc1_own, fc2_weight), 0, 0, None)
    held[2], fc1_arrived[0], *later = lax.optimization_barrier((held[2], fc1_arrived[0], *later))
    fc1_arrived.append(swap_tensor(later[0]))
    fc2_arrived = [swap_tensor(later[1])]
    *stage_own, fc1_k, fc2_k = stage(True, place2, (fc1_own, fc2_weight), 0, 0, held)
    back_own = stage_own[1]
    back_own, fc1_arrived[1], fc2_arrived[0], last = lax.optimization_barrier(
        (back_own, fc1_arrived[1], fc2_arrived[0], later[2])
    )
    g_fc1 = (both(fc1_k, fc1_o) + jnp.concatenate(fc1_arrived).astype(F32)).astype(BF16)
    fc2_r = swap_core(fc2_o)
    g_fc1, fc2_r, back_own = lax.optimization_barrier((g_fc1, fc2_r, back_own))
    fc2_arrived.append(swap_tensor(last))
    g_fc1 = lax.psum(g_fc1, "dp", axis_index_groups=chip_groups(0))
    low_resid, sum_gain2, sum_bias2, sum_ob = resid_back(
        back_own, stage_other[1], fc1_own, mlp_other, resid, grad_out, features
    )
    low_resid, fc2_arrived[1] = lax.optimization_barrier((low_resid, fc2_arrived[1]))
    g_late = fc2_k.astype(F32) + fc2_r.astype(F32) + jnp.concatenate(fc2_arrived).astype(F32)
    g_late = g_late.astype(BF16)
    x_keep, x_send = halves(g_late, 2)
    low_resid, x_keep, x_send = lax.optimization_barrier((low_resid, x_keep, x_send))
    d_ctx, *o_parts = context_back(place, low_resid, ctx.reshape(flat), o_weight, in_other)
    d_ctx = d_ctx.reshape(ctx.shape)
    d_ctx, x_send = lax.optimization_barrier((d_ctx, x_send))
    x_recv = swap_step(x_send, 2)
    wide = (count, 3 * width, seq)
    d_other = mix_back(qkv_other, ctx, logs, d_ctx, 1, 0, count, None).reshape(wide)
    o_send = both(o_parts[2], o_parts[3]).astype(BF16)
    o_pair = both(o_parts[0], o_parts[1])
    d_other, x_recv = lax.optimization_barrier((d_other, x_recv))
    z_keep, z_send = halves(added(x_keep, x_recv), 4)
    d_other, o_send, o_pair, z_keep, z_send = lax.optimization_barrier(
        (d_other, o_send, o_pair, z_keep, z_send)
    )
    z_recv = swap_step(z_send, 4)
    o_arrived = swap_tensor(o_send)
    other_keep, other_send, column_other = project_back(place, normed, d_other)
    o_arrived, other_keep, g_fc1, z_recv = lax.optimization_barrier(
        (o_arrived, other_keep, g_fc1, z_recv)
    )
    far_keep, far_send = halves(added(z_keep, z_recv), 8)
    g_o = (o_pair + o_arrived.astype(F32)).astype(BF16)
    d_ctx, g_o, far_keep, far_send = lax.optimization_barrier((d_ctx, g_o, far_keep, far_send))
    far_recv = swap_step(far_send, 8)
    fc1_other = swap_core(g_fc1)

    d_own = mix_back(qkv_own, ctx, logs, d_ctx, 0, 0, 1, None)
    other_recv = swap_core(other_send)
    third = 3 * width // 2 * 3 // 10 // 8 * 8
    cuts = [0, third, 2 * third, 3 * width // 2]
    pieces = [summed(other_keep, other_recv, *cuts[k : k + 2]) for k in range(3)]
    d_own, far_recv = lax.optimization_barrier((d_own, far_recv))
    block_sum = added(far_keep, far_recv)
    d_own, fc1_other, block_sum, *pieces = lax.optimization_barrier(
        (d_own, fc1_other, block_sum, *pieces)
    )
    qkv_arrived = []
    for index in range(1, count):
        step = 16 >> index
        block_recv = swap_step(block_sum, step)
        qkv_arrived.append(swap_tensor(pieces[index - 1]))
        d_own = mix_back(qkv_own, ctx, logs, d_ctx, 0, index, 1, d_own)
        d_own, qkv_arrived[-1], block_recv, *pieces = lax.optimization_barrier(
            (d_own, qkv_arrived[-1], block_recv, *pieces)
        )
        block_sum = ranked(block_sum, block_recv, step)
        d_own, block_sum = lax.optimization_barrier((d_own, block_sum))
    qkv_arrived += [swap_tensor(value) for value in pieces[count - 1 :]]
    d_own = d_own.reshape(wide)
    own_keep, own_send, column_own = project_back(place, normed, d_own)
    own_keep, d_own, *qkv_arrived = lax.optimization_barrier((own_keep, d_own, *qkv_arrived))

    def inputs(start, steps, held):
        return input_back(
            place, d_own, d_other, in_weights, in_other, rows, low_resid, features, start, steps, held
        )

    def ordered(own, other):
        return jnp.where(tensor == 0, jnp.stack([own, other]), jnp.stack([other, own]))

    def heads_part(vector):
        return vector[:width, 0], vector[2 * width :, 0]

    (q_own, v_own), (q_other, v_other) = heads_part(column_own), heads_part(column_other)
    early_sums = jnp.concatenate(
        [
            jnp.concatenate([sum_ob, sum_gain2, sum_bias2, sum_fc2b], axis=1)[0],
            ordered(
                jnp.concatenate([q_own, v_own, stage_own[2][:, 0]]),
                jnp.concatenate([q_other, v_other, stage_other[2][:, 0]]),
            ).reshape(-1),
        ]
    )
    d_own, early_sums = lax.optimization_barrier((d_own, early_sums))
    in_buffer, in_send, gain_a, bias_a = inputs(0, 1, None)
    block_recv = swap_step(block_sum, 2)
    own_recv, in_buffer, in_send = lax.optimization_barrier(
        (swap_core(own_send), in_buffer, in_send)
    )
    in_arrived = [swap_tensor(in_send)]
    g_qkv = own_keep.astype(F32) + own_recv.astype(F32) + jnp.concatenate(qkv_arrived).astype(F32)
    g_qkv = jnp.concatenate([g_qkv.astype(BF16), g_o])
    g_qkv, in_buffer = lax.optimization_barrier((g_qkv, in_buffer))
    g_qkv = lax.psum(g_qkv, "dp", axis_index_groups=chip_groups(1))
    in_buffer, in_send, gain_b, bias_b = inputs(1, count - 1, in_buffer)
    norm_sums = jnp.concatenate([gain_a + gain_b, bias_a + bias_b], axis=1)
    small_grads = jnp.concatenate([norm_sums[0], early_sums])
    small_swapped = swap_tensor(small_grads)
    in_send, in_arrived[0], act_own, block_recv = lax.optimization_barrier(
        (in_send, in_arrived[0], stage_own[0], block_recv)
    )
    g_late = ranked(block_sum, block_recv, 2)
    act_own, g_late = lax.optimization_barrier((act_own, g_late))
    far = (1 - tensor) * count
    in_arrived.append(swap_tensor(in_send))
    late_other = swap_core(g_late)

    out_buffer, out_send, last_send = layer_result(
        place, act_own, stage_other[0], fc2_weight, mlp_other, resid, features
    )
    in_arrived[1], out_send, out_buffer, small_swapped, late_other = lax.optimization_barrier(
        (in_arrived[1], out_send, out_buffer, small_swapped, late_other)
    )
    small_grads += small_swapped
    out_arrived = [swap_tensor(out_send)]
    out_fc1 = widen(place, g_fc1, fc1_other, 2 * block, hidden, 4)
    input_grad = lax.dynamic_update_slice_in_dim(in_buffer, jnp.concatenate(in_arrived), far, 0)
    out_fc2 = widen(place, g_late, late_other, 2 * block, hidden, 4)

    out_fc1, input_grad, small_grads = lax.optimization_barrier((out_fc1, input_grad, small_grads))
    near = exchange_sum(small_grads, (1, 2, 3))
    out_fc2, near = lax.optimization_barrier((out_fc2, near))
    small_grads = exchange_sum(near, range(4, spots, 4))
    g_qkv, small_grads, out_fc2, out_arrived[0] = lax.optimization_barrier(
        (g_qkv, small_grads, out_fc2, out_arrived[0])
    )
    qkv_other_core = swap_core(g_qkv)
    out_arrived.append(swap_tensor(after(last_send, g_qkv)))
    g_feature = lax.dynamic_slice_in_dim(
        small_grads[: 6 * feat].reshape(6, feat), tensor * half, half, 1
    )
    small_grads = lax.dynamic_index_in_dim(
        small_grads[6 * feat :].reshape(2, 2 * width + hidden), tensor, 0, keepdims=False
    )

    g_q, g_k, g_v, g_o = widen(place, g_qkv, qkv_other_core, width // 2, width, 1, 4)
    g_q, out_arrived[1] = lax.optimization_barrier((g_q, out_arrived[1]))
    layer_out = lax.dynamic_update_slice_in_dim(out_buffer, jnp.concatenate(out_arrived), far, 0)
    return (
        jnp.swapaxes(layer_out, 1, 2),
        jnp.swapaxes(input_grad, 1, 2),
        g_feature[0],
        g_feature[1],
        g_q.T,
        small_grads[:width],
        g_k.T,
        g_v.T,
        small_grads[width : 2 * width],
        g_o,
        g_feature[2],
        g_feature[3],
        g_feature[4],
        out_fc1.T,
        small_grads[2 * width :],
        out_fc2,
        g_feature[5],
    )


def solution(mesh):
    in_specs = (
        P("dp", None, "tensor"),
        P("dp"),
        P("dp", None, "tensor"),
        P("tensor"),
        P("tensor"),
        P(None, "tensor"),
        P("tensor"),
        P(None, "tensor"),
        P(None, "tensor"),
        P("tensor"),
        P("tensor", None),
        P("tensor"),
        P("tensor"),
        P("tensor"),
        P(None, "tensor"),
        P("tensor"),
        P("tensor", None),
        P("tensor"),
    )
    out_specs = (
        P("dp", None, "tensor"),
        P("dp", None, "tensor"),
        P("tensor"),
        P("tensor"),
        P(None, "tensor"),
        P("tensor"),
        P(None, "tensor"),
        P(None, "tensor"),
        P("tensor"),
        P("tensor", None),
        P("tensor"),
        P("tensor"),
        P("tensor"),
        P(None, "tensor"),
        P("tensor"),
        P("tensor", None),
        P("tensor"),
    )
    whole_images = mesh.shape["tensor"] == 2 and mesh.shape["dp"] == 16
    return jax.shard_map(
        whole_device if whole_images else split_device, mesh=mesh, in_specs=in_specs, out_specs=out_specs, check_vma=False
    )
```

```python
import functools
import math

import jax
import jax.numpy as jnp
from jax import lax
from jax.experimental import pallas as pl
from jax.experimental.pallas import tpu as pltpu
from jax.sharding import PartitionSpec as P

HDIM = 72
MICRO = 2


EPS = 1e-06
GELU_C = math.sqrt(2.0 / math.pi)
GELU_A = 0.044715


def matmul(left, right):
    return jnp.dot(left, right, preferred_element_type=jnp.float32)


def left_transposed(left, right):
    return lax.dot_general(
        left, right, (((0,), (0,)), ((), ())), preferred_element_type=jnp.float32
    )


def right_transposed(left, right):
    return lax.dot_general(
        left, right, (((1,), (1,)), ((), ())), preferred_element_type=jnp.float32
    )


def rounded(values):
    return values.astype(jnp.bfloat16).astype(jnp.float32)


def norm_rows(values):
    feat_total = values.shape[1] * lax.axis_size("tensor")
    row_sum, row_square = lax.psum(
        (jnp.sum(values, axis=1), jnp.sum(values * values, axis=1)), "tensor"
    )
    row_mean = row_sum / feat_total
    row_var = row_square / feat_total - row_mean * row_mean
    inverse = lax.rsqrt(row_var + EPS)
    normed = (values - row_mean[:, None]) * inverse[:, None]
    return (normed, inverse)


def norm_back(grad_normed, normed, inverse, gain_vec):
    feat_total = normed.shape[1] * lax.axis_size("tensor")
    scaled = grad_normed * gain_vec.astype(jnp.float32)
    sum_plain, sum_cross = lax.psum(
        (jnp.sum(scaled, axis=1), jnp.sum(scaled * normed, axis=1)), "tensor"
    )
    return inverse[:, None] * (
        scaled - sum_plain[:, None] / feat_total - normed * (sum_cross[:, None] / feat_total)
    )


def gather_rows(shard):
    return lax.all_gather(shard, "tensor", axis=1, tiled=True)


def gather_grads(shard):
    return lax.all_gather(shard, "tensor", axis=1, tiled=True)


def gelu_parts(pre):
    tanh_val = jnp.tanh(GELU_C * (pre + GELU_A * pre * pre * pre))
    value = 0.5 * pre * (1.0 + tanh_val)
    slope = 0.5 * (1.0 + tanh_val) + 0.5 * pre * (1.0 - tanh_val * tanh_val) * GELU_C * (
        1.0 + 3.0 * GELU_A * pre * pre
    )
    return (value, slope)


def split_device(
    images,
    valid_flags,
    cotangent,
    ln1_gain,
    ln1_bias,
    q_weight,
    q_bias,
    k_weight,
    v_weight,
    v_bias,
    o_weight,
    o_bias,
    ln2_gain,
    ln2_bias,
    fc1_weight,
    fc1_bias,
    fc2_weight,
    fc2_bias,
):
    img_local, seq_len, feat_local = images.shape
    per_micro = img_local // MICRO
    rows = per_micro * seq_len
    head_local = q_weight.shape[1] // HDIM
    scale = 1.0 / math.sqrt(HDIM)
    shaped = (per_micro, seq_len, head_local, HDIM)
    split_images = images.reshape(per_micro, MICRO, seq_len, feat_local)
    split_cot = cotangent.reshape(per_micro, MICRO, seq_len, feat_local)
    split_flags = valid_flags.reshape(per_micro, MICRO).astype(jnp.float32)
    param_list = (
        ln1_gain,
        ln1_bias,
        q_weight,
        q_bias,
        k_weight,
        v_weight,
        v_bias,
        o_weight,
        o_bias,
        ln2_gain,
        ln2_bias,
        fc1_weight,
        fc1_bias,
        fc2_weight,
        fc2_bias,
    )
    totals = tuple((jnp.zeros(weight_arr.shape, jnp.float32) for weight_arr in param_list))
    out_list = []
    grad_list = []
    for micro_index in range(MICRO):
        flag_rows = jnp.repeat(split_flags[:, micro_index], seq_len)[:, None]
        inputs = split_images[:, micro_index].reshape(rows, feat_local).astype(jnp.float32)
        normed1, inverse1 = norm_rows(inputs)
        low_first = (normed1 * ln1_gain + ln1_bias).astype(jnp.bfloat16)
        full_first = gather_rows(low_first)
        query = (matmul(full_first, q_weight) + q_bias).astype(jnp.bfloat16)
        keys = matmul(full_first, k_weight).astype(jnp.bfloat16)
        values = (matmul(full_first, v_weight) + v_bias).astype(jnp.bfloat16)
        query4 = query.reshape(shaped)
        keys4 = keys.reshape(shaped)
        values4 = values.reshape(shaped)
        scores = (
            jnp.einsum("nqhd,nkhd->nhqk", query4, keys4, preferred_element_type=jnp.float32) * scale
        )
        log_total = jax.nn.logsumexp(scores, axis=-1)
        probs_low = jnp.exp(scores - log_total[..., None]).astype(jnp.bfloat16)
        mixed = jnp.einsum(
            "nhqk,nkhd->nqhd", probs_low, values4, preferred_element_type=jnp.float32
        )
        context = mixed.reshape(rows, head_local * HDIM).astype(jnp.bfloat16)
        attended = lax.psum_scatter(
            rounded(matmul(context, o_weight)).astype(jnp.bfloat16),
            "tensor",
            scatter_dimension=1,
            tiled=True,
        ).astype(jnp.float32)
        resid = inputs + attended + o_bias
        normed2, inverse2 = norm_rows(resid)
        low_second = (normed2 * ln2_gain + ln2_bias).astype(jnp.bfloat16)
        full_second = gather_rows(low_second)
        hidden_pre = matmul(full_second, fc1_weight) + fc1_bias
        act_value, act_slope = gelu_parts(hidden_pre)
        act_low = act_value.astype(jnp.bfloat16)
        branch = lax.psum_scatter(
            rounded(matmul(act_low, fc2_weight)).astype(jnp.bfloat16),
            "tensor",
            scatter_dimension=1,
            tiled=True,
        ).astype(jnp.float32)
        layer_rows = (resid + branch + fc2_bias) * flag_rows
        out_list.append(layer_rows.astype(jnp.bfloat16).reshape(per_micro, seq_len, feat_local))
        grad_out = (
            split_cot[:, micro_index].reshape(rows, feat_local).astype(jnp.float32) * flag_rows
        )
        grad_full = gather_grads(grad_out.astype(jnp.bfloat16))
        g_fc2w = left_transposed(act_low, grad_full)
        g_fc2b = jnp.sum(grad_out, axis=0)
        hidden_grad = (right_transposed(grad_full, fc2_weight) * act_slope).astype(jnp.bfloat16)
        g_fc1w = left_transposed(full_second, hidden_grad)
        g_fc1b = jnp.sum(hidden_grad.astype(jnp.float32), axis=0)
        grad_second = lax.psum_scatter(
            rounded(right_transposed(hidden_grad, fc1_weight)).astype(jnp.bfloat16),
            "tensor",
            scatter_dimension=1,
            tiled=True,
        ).astype(jnp.float32)
        g_ln2g = jnp.sum(grad_second * normed2, axis=0)
        g_ln2b = jnp.sum(grad_second, axis=0)
        grad_resid = grad_out + norm_back(grad_second, normed2, inverse2, ln2_gain)
        g_ob = jnp.sum(grad_resid, axis=0)
        resid_full = gather_grads(grad_resid.astype(jnp.bfloat16))
        g_ow = left_transposed(context, resid_full)
        grad_context = right_transposed(resid_full, o_weight).astype(jnp.bfloat16)
        context4 = grad_context.reshape(shaped)
        probs = jnp.exp(
            jnp.einsum("nqhd,nkhd->nhqk", query4, keys4, preferred_element_type=jnp.float32) * scale
            - log_total[..., None]
        )
        probs_again = probs.astype(jnp.bfloat16)
        grad_probs = jnp.einsum(
            "nqhd,nkhd->nhqk", context4, values4, preferred_element_type=jnp.float32
        )
        row_delta = jnp.sum(probs * grad_probs, axis=-1)
        grad_scores = (probs * (grad_probs - row_delta[..., None])).astype(jnp.bfloat16)
        grad_query = (
            (
                jnp.einsum(
                    "nhqk,nkhd->nqhd", grad_scores, keys4, preferred_element_type=jnp.float32
                )
                * scale
            )
            .reshape(rows, head_local * HDIM)
            .astype(jnp.bfloat16)
        )
        grad_keys = (
            (
                jnp.einsum(
                    "nhqk,nqhd->nkhd", grad_scores, query4, preferred_element_type=jnp.float32
                )
                * scale
            )
            .reshape(rows, head_local * HDIM)
            .astype(jnp.bfloat16)
        )
        grad_values = (
            jnp.einsum("nhqk,nqhd->nkhd", probs_again, context4, preferred_element_type=jnp.float32)
            .reshape(rows, head_local * HDIM)
            .astype(jnp.bfloat16)
        )
        g_qw = left_transposed(full_first, grad_query)
        g_qb = jnp.sum(grad_query.astype(jnp.float32), axis=0)
        g_kw = left_transposed(full_first, grad_keys)
        g_vw = left_transposed(full_first, grad_values)
        g_vb = jnp.sum(grad_values.astype(jnp.float32), axis=0)
        partial_first = (
            right_transposed(grad_query, q_weight)
            + right_transposed(grad_keys, k_weight)
            + right_transposed(grad_values, v_weight)
        )
        grad_first = lax.psum_scatter(
            rounded(partial_first).astype(jnp.bfloat16), "tensor", scatter_dimension=1, tiled=True
        ).astype(jnp.float32)
        g_ln1g = jnp.sum(grad_first * normed1, axis=0)
        g_ln1b = jnp.sum(grad_first, axis=0)
        grad_input = grad_resid + norm_back(grad_first, normed1, inverse1, ln1_gain)
        grad_list.append(grad_input.astype(jnp.bfloat16).reshape(per_micro, seq_len, feat_local))
        micro_grads = (
            g_ln1g,
            g_ln1b,
            g_qw,
            g_qb,
            g_kw,
            g_vw,
            g_vb,
            g_ow,
            g_ob,
            g_ln2g,
            g_ln2b,
            g_fc1w,
            g_fc1b,
            g_fc2w,
            g_fc2b,
        )
        totals = jax.tree.map(jnp.add, totals, micro_grads)
    totals = (
        lax.psum(totals[0].astype(jnp.bfloat16), "dp").astype(jnp.float32),
        lax.psum(totals[1].astype(jnp.bfloat16), "dp").astype(jnp.float32),
        lax.psum(totals[2].astype(jnp.bfloat16), "dp").astype(jnp.float32),
        lax.psum(totals[3].astype(jnp.bfloat16), "dp").astype(jnp.float32),
        lax.psum(totals[4].astype(jnp.bfloat16), "dp").astype(jnp.float32),
        lax.psum(totals[5].astype(jnp.bfloat16), "dp").astype(jnp.float32),
        lax.psum(totals[6].astype(jnp.bfloat16), "dp").astype(jnp.float32),
        lax.psum(totals[7].astype(jnp.bfloat16), "dp").astype(jnp.float32),
        lax.psum(totals[8].astype(jnp.bfloat16), "dp").astype(jnp.float32),
        lax.psum(totals[9].astype(jnp.bfloat16), "dp").astype(jnp.float32),
        lax.psum(totals[10].astype(jnp.bfloat16), "dp").astype(jnp.float32),
        lax.psum(totals[11].astype(jnp.bfloat16), "dp").astype(jnp.float32),
        lax.psum(totals[12].astype(jnp.bfloat16), "dp").astype(jnp.float32),
        lax.psum(totals[13].astype(jnp.bfloat16), "dp").astype(jnp.float32),
        lax.psum(totals[14].astype(jnp.bfloat16), "dp").astype(jnp.float32),
    )
    layer_out = jnp.stack(out_list, axis=1).reshape(img_local, seq_len, feat_local)
    input_grad = jnp.stack(grad_list, axis=1).reshape(img_local, seq_len, feat_local)
    return (
        layer_out,
        input_grad,
        totals[0],
        totals[1],
        totals[2],
        totals[3],
        totals[4],
        totals[5],
        totals[6],
        totals[7],
        totals[8],
        totals[9],
        totals[10],
        totals[11],
        totals[12],
        totals[13],
        totals[14],
    )


F32 = jnp.float32
BF16 = jnp.bfloat16
LOG2E = math.log2(math.e)
VMEM_BYTES = 58 * 1024 * 1024
COST_SHARE = 0.4
LONG = 4.0
SHORT = 0.05


def dot_nn(left, right):
    return jnp.dot(left, right, preferred_element_type=F32)


def dot_nt(left, right):
    return lax.dot_general(left, right, (((1,), (1,)), ((), ())), preferred_element_type=F32)


def dot_tn(left, right):
    return lax.dot_general(left, right, (((0,), (0,)), ((), ())), preferred_element_type=F32)


def cost(flops, moved, trans=0, share=COST_SHARE):
    return pl.CostEstimate(
        flops=int(flops * share),
        bytes_accessed=int(moved * share),
        transcendentals=int(trans * share),
    )


def params(grid_dims):
    return pltpu.CompilerParams(
        dimension_semantics=("arbitrary",) * grid_dims, vmem_limit_bytes=VMEM_BYTES
    )


def once(shape, spot=None):
    spot = spot or (0,) * len(shape)
    return pl.BlockSpec(shape, lambda *_: spot, pipeline_mode=pl.Buffered(1))


def image_block(shape, offset=0):
    return pl.BlockSpec((1,) + shape, lambda i, *_: (offset + i, 0, 0))


ANYWHERE = pl.BlockSpec(memory_space=pl.ANY)


def column_stats(values):
    mean = jnp.mean(values, axis=0, keepdims=True)
    centred = values - mean
    inverse = lax.rsqrt(jnp.mean(centred * centred, axis=0, keepdims=True) + EPS)
    return centred * inverse, inverse


def join_halves(first, own, other):
    return jnp.concatenate(
        [jnp.where(first, own, other), jnp.where(first, other, own)], axis=0
    )


def split_halves(first, full):
    half = full.shape[0] // 2
    low, high = full[:half], full[half:]
    return jnp.where(first, low, high), jnp.where(first, high, low)


def token_sum(values):
    return jnp.sum(values, axis=1, keepdims=True)


LN1_GAIN, LN1_BIAS, O_BIAS, LN2_GAIN, LN2_BIAS, FC2_BIAS = range(6)


def as_row(column_sum):
    rows = column_sum.shape[0]
    return jnp.broadcast_to(column_sum, (rows, 128)).T[0:1]


def column(ref, index):
    return ref[:, index : index + 1]


def write_rows(row_refs, sum_refs):
    @pl.when(pl.program_id(0) == pl.num_programs(0) - 1)
    def _():
        for row_ref, sum_ref in zip(row_refs, sum_refs):
            row_ref[...] = as_row(sum_ref[...])


def store_heads(out_ref, first, product):
    head_dim = out_ref.shape[2]
    for head in range(product.shape[0] // head_dim):
        out_ref[0, first + head] = product[head * head_dim : (head + 1) * head_dim].astype(BF16)


def first_norm_kernel(
    place_ref, own_ref, other_ref, feature_ref, q_ref, k_ref, v_ref, head_ref, *rest
):
    rows_ref, normed_ref, qkv_ref = rest[-3:]
    full = join_halves(place_ref[0] == 0, own_ref[0].astype(F32), other_ref[0].astype(F32))
    rows_ref[0] = full.astype(BF16)
    normed, _ = column_stats(full)
    low = (normed * column(feature_ref, LN1_GAIN) + column(feature_ref, LN1_BIAS)).astype(BF16)
    normed_ref[0] = low
    heads = qkv_ref.shape[1] // 3
    store_heads(qkv_ref, 0, dot_nn(q_ref[...], low) + column(head_ref, 0))
    store_heads(qkv_ref, heads, dot_nn(k_ref[...], low))
    store_heads(qkv_ref, 2 * heads, dot_nn(v_ref[...], low) + column(head_ref, 1))


def first_norm(index, count, place, images, other, features, weights, head_vectors, earlier):
    _, half, seq = images.shape
    width, feat = weights[0].shape
    groups = 3 * width // HDIM
    held = list(earlier) if earlier else []
    return pl.pallas_call(
        first_norm_kernel,
        out_shape=[
            jax.ShapeDtypeStruct((count, feat, seq), BF16),
            jax.ShapeDtypeStruct((count, feat, seq), BF16),
            jax.ShapeDtypeStruct((count, groups, HDIM, seq), BF16),
        ],
        grid_spec=pltpu.PrefetchScalarGridSpec(
            num_scalar_prefetch=1,
            grid=(1,),
            in_specs=[
                pl.BlockSpec((1, half, seq), lambda i, p: (p[0] * count + index, 0, 0)),
                once((1, half, seq)),
                once((feat, 8)),
                once((width, feat)),
                once((width, feat)),
                once((width, feat)),
                once((width, 8)),
            ]
            + [ANYWHERE] * len(held),
            out_specs=[
                once((1, feat, seq), (index, 0, 0)),
                once((1, feat, seq), (index, 0, 0)),
                once((1, groups, HDIM, seq), (index, 0, 0, 0)),
            ],
        ),
        input_output_aliases={8 + k: k for k in range(len(held))},
        compiler_params=params(1),
        cost_estimate=cost(6 * seq * feat * width, 12 << 20, 0, SHORT),
        name="first_norm",
    )(place, images, other, features, *weights, head_vectors, *held)


def project_kernel(normed_ref, q_ref, k_ref, v_ref, head_ref, qkv_ref):
    low = normed_ref[0]
    heads = qkv_ref.shape[1] // 3
    store_heads(qkv_ref, 0, dot_nn(q_ref[...], low) + column(head_ref, 2))
    store_heads(qkv_ref, heads, dot_nn(k_ref[...], low))
    store_heads(qkv_ref, 2 * heads, dot_nn(v_ref[...], low) + column(head_ref, 3))


def project(normed, weight, head_vectors, width):
    count, feat, seq = normed.shape
    groups = 3 * width // HDIM
    return pl.pallas_call(
        project_kernel,
        grid=(count,),
        out_shape=jax.ShapeDtypeStruct((count, groups, HDIM, seq), BF16),
        in_specs=[
            image_block((feat, seq)),
            once((width, feat), (0, 0)),
            once((width, feat), (1, 0)),
            once((width, feat), (2, 0)),
            once((width, 8)),
        ],
        out_specs=pl.BlockSpec((1, groups, HDIM, seq), lambda i: (i, 0, 0, 0)),
        compiler_params=params(1),
        cost_estimate=cost(6 * count * seq * feat * width, 20 << 20),
        name="project",
    )(normed, weight, weight, weight, head_vectors)


def mix_kernel(q_ref, k_ref, v_ref, *rest, scale):
    out_ref, log_ref = rest[-2:]
    factor = scale * LOG2E
    for head in range(q_ref.shape[1]):
        scores = dot_tn(k_ref[0, head], q_ref[0, head])
        top = jnp.max(scores, axis=0, keepdims=True)
        probs = jnp.exp2((scores - top) * factor)
        total = jnp.sum(probs, axis=0, keepdims=True)
        mixed = dot_nn(v_ref[0, head], probs.astype(BF16))
        out_ref[0, head] = (mixed * (1.0 / total)).astype(BF16)
        log_ref[0, head] = top * factor + jnp.log2(total)


def mix(qkv, half, start, steps, earlier, per_step=1):
    count, groups, head_dim, seq = qkv.shape
    heads = groups // 3
    blocks = heads // per_step
    block = (1, per_step, head_dim, seq)
    held = list(earlier) if earlier else []

    def at(offset):
        return pl.BlockSpec(block, lambda i, j: (start + i, offset + j, 0, 0))

    return pl.pallas_call(
        functools.partial(mix_kernel, scale=1.0 / math.sqrt(head_dim)),
        grid=(steps, blocks),
        out_shape=[
            jax.ShapeDtypeStruct((count, 2 * heads, head_dim, seq), BF16),
            jax.ShapeDtypeStruct((count, 2 * heads, 1, seq), F32),
        ],
        in_specs=[at(0), at(blocks), at(2 * blocks)] + [ANYWHERE] * len(held),
        out_specs=[
            at(half * blocks),
            pl.BlockSpec(
                (1, per_step, 1, seq), lambda i, j: (start + i, half * blocks + j, 0, 0)
            ),
        ],
        input_output_aliases={3 + k: k for k in range(len(held))},
        compiler_params=params(2),
        cost_estimate=cost(
            4 * steps * heads * seq * seq * 256,
            steps * heads * head_dim * seq * 8,
            steps * heads * seq * seq,
            SHORT if steps == 1 else COST_SHARE,
        ),
        name="mix",
    )(qkv, qkv, qkv, *held)


def mix_back_kernel(q_ref, k_ref, v_ref, out_ref, log_ref, grad_ref, *rest, scale, heads):
    d_ref = rest[-1]
    factor = scale * LOG2E
    per_step = q_ref.shape[1]
    first = pl.program_id(1) * per_step
    for head in range(per_step):
        query, keys, values = q_ref[0, head], k_ref[0, head], v_ref[0, head]
        grad = grad_ref[0, head]
        delta = jnp.sum(grad.astype(F32) * out_ref[0, head].astype(F32), axis=0, keepdims=True)
        probs = jnp.exp2(dot_tn(keys, query) * factor - log_ref[0, head])
        grad_scores = (probs * (dot_tn(values, grad) - delta)).astype(BF16)
        d_ref[0, 2 * heads + first + head] = dot_nt(grad, probs.astype(BF16)).astype(BF16)
        d_ref[0, first + head] = (dot_nn(keys, grad_scores) * scale).astype(BF16)
        d_ref[0, heads + first + head] = (dot_nt(query, grad_scores) * scale).astype(BF16)


def mix_back(qkv, out, log_total, grad, half, start, steps, earlier, per_step=4):
    count, groups, head_dim, seq = qkv.shape
    heads = groups // 3
    blocks = heads // per_step
    block = (1, per_step, head_dim, seq)
    held = [] if earlier is None else [earlier]

    def at(offset):
        return pl.BlockSpec(block, lambda i, j: (start + i, offset + j, 0, 0))

    return pl.pallas_call(
        functools.partial(mix_back_kernel, scale=1.0 / math.sqrt(head_dim), heads=heads),
        grid=(steps, blocks),
        out_shape=jax.ShapeDtypeStruct(qkv.shape, BF16),
        in_specs=[
            at(0),
            at(blocks),
            at(2 * blocks),
            at(half * blocks),
            pl.BlockSpec((1, per_step, 1, seq), lambda i, j: (start + i, half * blocks + j, 0, 0)),
            at(half * blocks),
        ]
        + [ANYWHERE] * len(held),
        input_output_aliases={6: 0} if held else {},
        out_specs=pl.BlockSpec((1, groups, head_dim, seq), lambda i, j: (start + i, 0, 0, 0)),
        compiler_params=params(2),
        cost_estimate=cost(
            10 * steps * heads * seq * seq * 256,
            steps * heads * head_dim * seq * 16,
            steps * heads * seq * seq,
            SHORT if steps == 1 else COST_SHARE,
        ),
        name="mix_back",
    )(qkv, qkv, qkv, out, log_total, grad, *held)


def second_norm_kernel(
    place_ref,
    ctx_ref,
    w_own_ref,
    w_other_ref,
    rows_ref,
    feature_ref,
    cot_own_ref,
    *rest,
):
    *cot_refs, resid_ref, low_ref, grad_ref, row_ref, w_ref, sum_ref = rest
    step = pl.program_id(0)
    half = w_own_ref.shape[0]

    @pl.when(step == 0)
    def _():
        w_ref[:half] = w_own_ref[...]
        w_ref[half:] = w_other_ref[...]
        sum_ref[...] = jnp.zeros_like(sum_ref)

    resid = rows_ref[0].astype(F32) + dot_tn(w_ref[...], ctx_ref[0])
    resid += column(feature_ref, O_BIAS)
    resid_ref[0] = resid.astype(BF16)
    normed, _ = column_stats(resid)
    low_ref[0] = (
        normed * column(feature_ref, LN2_GAIN) + column(feature_ref, LN2_BIAS)
    ).astype(BF16)
    flag = place_ref[2 + place_ref[0] * pl.num_programs(0) + step].astype(F32)
    cot_other = cot_refs[0][0]
    for index in range(1, len(cot_refs)):
        cot_other = jnp.where(step == index, cot_refs[index][0], cot_other)
    grad = flag * join_halves(
        place_ref[0] == 0, cot_own_ref[0].astype(F32), cot_other.astype(F32)
    )
    grad_ref[0] = grad.astype(BF16)
    sum_ref[...] += token_sum(grad)
    write_rows((row_ref,), (sum_ref,))


def second_norm(place, ctx, w_own, w_other, rows, features, cot, cot_other):
    count, feat, seq = rows.shape
    half = w_own.shape[0]
    full = image_block((feat, seq))
    return pl.pallas_call(
        second_norm_kernel,
        out_shape=[
            jax.ShapeDtypeStruct((count, feat, seq), BF16),
            jax.ShapeDtypeStruct((count, feat, seq), BF16),
            jax.ShapeDtypeStruct((count, feat, seq), BF16),
            jax.ShapeDtypeStruct((1, feat), F32),
        ],
        grid_spec=pltpu.PrefetchScalarGridSpec(
            num_scalar_prefetch=1,
            grid=(count,),
            in_specs=[
                full,
                once((half, feat)),
                once((half, feat), (3, 0)),
                full,
                once((feat, 8)),
                pl.BlockSpec((1, feat // 2, seq), lambda i, p: (p[0] * count + i, 0, 0)),
            ]
            + [once((1, feat // 2, seq))] * count,
            out_specs=[full, full, full, once((1, feat))],
            scratch_shapes=[pltpu.VMEM((feat, feat), BF16), pltpu.VMEM((feat, 1), F32)],
        ),
        compiler_params=params(1),
        cost_estimate=cost(4 * count * seq * half * feat, 40 << 20),
        name="second_norm",
    )(place, ctx, w_own, w_other, rows, features, cot, *cot_other)


def hidden_kernel(place_ref, low_ref, grad_ref, fc1_ref, fc2_ref, bias_ref, *rest, which):
    act_ref, back_ref, gb_ref, g1_ref, g2_ref = rest[-5:]
    g1, g2, gb = None, None, None
    for image in range(low_ref.shape[0]):
        low, grad = low_ref[image], grad_ref[image]
        pre = dot_nn(fc1_ref[...], low) + column(bias_ref, which)
        square = pre * pre
        tanh_val = jnp.tanh(pre * (GELU_C + (GELU_C * GELU_A) * square))
        half = 0.5 * tanh_val + 0.5
        act = pre * half
        slope = half + act * (1.0 - half) * (2 * GELU_C + (6 * GELU_C * GELU_A) * square)
        act = act.astype(BF16)
        act_ref[image] = act
        back = (dot_nn(fc2_ref[...], grad) * slope).astype(BF16)
        back_ref[image] = back
        parts = dot_nt(back, low), dot_nt(act, grad), token_sum(back.astype(F32))
        g1 = parts[0] if g1 is None else g1 + parts[0]
        g2 = parts[1] if g2 is None else g2 + parts[1]
        gb = parts[2] if gb is None else gb + parts[2]
    gb_ref[...] = gb
    g1_ref[...] = g1.astype(BF16)
    g2_ref[...] = g2.astype(BF16)


def quarter_rows(hidden):
    return (-(-hidden // 4) + 7) // 8 * 8


def hidden_stage(keep, place, low, grad, fc1, fc2, fc2_offset, bias, which, earlier):
    count, feat, seq = low.shape
    hidden = bias.shape[0]
    block = quarter_rows(hidden)
    held = list(earlier) if earlier else []

    def chunk(j, p):
        return j + 2 * (p[1] if keep else 1 - p[1])

    weight = pl.BlockSpec((block, feat), lambda j, p: (chunk(j, p), 0))
    tokens = pl.BlockSpec((count, block, seq), lambda j, p: (0, chunk(j, p), 0))
    grads = pl.BlockSpec((block, feat), lambda j, p: (j, 0))
    part = jax.ShapeDtypeStruct((2 * block, feat), BF16)
    return pl.pallas_call(
        functools.partial(hidden_kernel, which=which),
        out_shape=[
            jax.ShapeDtypeStruct((count, hidden, seq), BF16),
            jax.ShapeDtypeStruct((count, hidden, seq), BF16),
            jax.ShapeDtypeStruct((hidden, 1), F32),
            part,
            part,
        ],
        grid_spec=pltpu.PrefetchScalarGridSpec(
            num_scalar_prefetch=1,
            grid=(2,),
            in_specs=[
                once((count, feat, seq)),
                once((count, feat, seq)),
                weight,
                pl.BlockSpec((block, feat), lambda j, p: (fc2_offset + chunk(j, p), 0)),
                pl.BlockSpec((block, 2), lambda j, p: (chunk(j, p), 0)),
            ]
            + [ANYWHERE] * len(held),
            out_specs=[
                tokens,
                tokens,
                pl.BlockSpec((block, 1), lambda j, p: (chunk(j, p), 0)),
                grads,
                grads,
            ],
        ),
        input_output_aliases={6 + k: k for k in range(len(held))},
        compiler_params=params(1),
        cost_estimate=cost(4 * count * seq * feat * hidden, 30 << 20, 0, LONG),
        name="hidden_stage",
    )(place, low, grad, fc1, fc2, bias, *held)


def layer_kernel(
    place_ref,
    act_own_ref,
    act_other_ref,
    w_own_ref,
    w_other_ref,
    resid_ref,
    b_ref,
    out_ref,
    send_ref,
    last_ref,
):
    step, count = pl.program_id(0), pl.num_programs(0)
    hidden = act_own_ref.shape[1]
    branch = dot_tn(w_own_ref[:hidden], act_own_ref[0])
    branch += dot_tn(w_other_ref[:hidden], act_other_ref[0])
    flag = place_ref[2 + place_ref[0] * count + step].astype(F32)
    result = (resid_ref[0].astype(F32) + branch + column(b_ref, FC2_BIAS)) * flag
    own, other = split_halves(place_ref[0] == 0, result)
    out_ref[0] = own.astype(BF16)
    other = other.astype(BF16)

    @pl.when(step < count - 1)
    def _():
        send_ref[0] = other

    @pl.when(step == count - 1)
    def _():
        last_ref[0] = other


def layer_result(place, act_own, act_other, w_own, w_other, resid, features):
    count, feat, seq = resid.shape
    hidden = act_own.shape[1]
    full = image_block((hidden, seq))
    padded = 4 * quarter_rows(hidden)
    part = (1, feat // 2, seq)
    return pl.pallas_call(
        layer_kernel,
        out_shape=[
            jax.ShapeDtypeStruct((2 * count, feat // 2, seq), BF16),
            jax.ShapeDtypeStruct((count - 1, feat // 2, seq), BF16),
            jax.ShapeDtypeStruct(part, BF16),
        ],
        grid_spec=pltpu.PrefetchScalarGridSpec(
            num_scalar_prefetch=1,
            grid=(count,),
            in_specs=[
                full,
                full,
                once((hidden, feat)),
                once((padded, feat), (1, 0)),
                image_block((feat, seq)),
                once((feat, 8)),
            ],
            out_specs=[
                pl.BlockSpec(part, lambda i, p: (p[0] * count + i, 0, 0)),
                pl.BlockSpec(part, lambda i, p: (jnp.minimum(i, count - 2), 0, 0)),
                once(part),
            ],
        ),
        compiler_params=params(1),
        cost_estimate=cost(4 * count * seq * feat * hidden, count * (12 << 20), 0, LONG),
        name="layer_result",
    )(place, act_own, act_other, w_own, w_other, resid, features)


def resid_back_kernel(
    back_own_ref,
    back_other_ref,
    w_own_ref,
    w_other_ref,
    resid_ref,
    grad_ref,
    gain_ref,
    low_ref,
    row_gain_ref,
    row_bias_ref,
    row_ob_ref,
    sum_gain_ref,
    sum_bias_ref,
    sum_ob_ref,
):
    hidden = back_own_ref.shape[1]
    grad_norm = dot_tn(w_own_ref[:hidden], back_own_ref[0])
    grad_norm += dot_tn(w_other_ref[:hidden], back_other_ref[0])
    normed, inverse = column_stats(resid_ref[0].astype(F32))
    scaled = grad_norm * column(gain_ref, LN2_GAIN)
    plain = jnp.mean(scaled, axis=0, keepdims=True)
    cross = jnp.mean(scaled * normed, axis=0, keepdims=True)
    grad = grad_ref[0].astype(F32) + inverse * (scaled - plain - normed * cross)
    low_ref[0] = grad.astype(BF16)

    @pl.when(pl.program_id(0) == 0)
    def _():
        sum_gain_ref[...] = jnp.zeros_like(sum_gain_ref)
        sum_bias_ref[...] = jnp.zeros_like(sum_bias_ref)
        sum_ob_ref[...] = jnp.zeros_like(sum_ob_ref)

    sum_gain_ref[...] += token_sum(grad_norm * normed)
    sum_bias_ref[...] += token_sum(grad_norm)
    sum_ob_ref[...] += token_sum(grad)
    write_rows((row_gain_ref, row_bias_ref, row_ob_ref), (sum_gain_ref, sum_bias_ref, sum_ob_ref))


def resid_back(back_own, back_other, w_own, w_other, resid, grad, gain):
    count, feat, seq = resid.shape
    hidden = back_own.shape[1]
    padded = 4 * quarter_rows(hidden)
    wide = image_block((hidden, seq))
    full = image_block((feat, seq))
    return pl.pallas_call(
        resid_back_kernel,
        grid=(count,),
        out_shape=[jax.ShapeDtypeStruct((count, feat, seq), BF16)]
        + [jax.ShapeDtypeStruct((1, feat), F32)] * 3,
        in_specs=[
            wide,
            wide,
            once((hidden, feat)),
            once((padded, feat)),
            full,
            full,
            once((feat, 8)),
        ],
        out_specs=[full] + [once((1, feat))] * 3,
        scratch_shapes=[pltpu.VMEM((feat, 1), F32)] * 3,
        compiler_params=params(1),
        cost_estimate=cost(4 * count * seq * feat * hidden, 50 << 20),
        name="resid_back",
    )(back_own, back_other, w_own, w_other, resid, grad, gain)


def context_back_kernel(
    place_ref,
    low_ref,
    ctx_ref,
    w_own_ref,
    w_other_ref,
    d_ref,
    own_keep_ref,
    own_send_ref,
    other_keep_ref,
    other_send_ref,
    acc_ref,
):
    step = pl.program_id(0)
    low = low_ref[0]
    half = w_own_ref.shape[0]
    d_ref[0, :half] = dot_nn(w_own_ref[...], low).astype(BF16)
    d_ref[0, half:] = dot_nn(w_other_ref[...], low).astype(BF16)
    product = dot_nt(ctx_ref[0], low)

    @pl.when(step == 0)
    def _():
        acc_ref[...] = product

    @pl.when(step > 0)
    def _():
        acc_ref[...] += product

    @pl.when(step == pl.num_programs(0) - 1)
    def _():
        part = half // 2
        keep = place_ref[1] * part
        send = part - keep
        own_keep_ref[...] = acc_ref[pl.ds(pl.multiple_of(keep, 8), part)].astype(BF16)
        own_send_ref[...] = acc_ref[pl.ds(pl.multiple_of(send, 8), part)].astype(BF16)
        other_keep_ref[...] = acc_ref[pl.ds(pl.multiple_of(half + keep, 8), part)].astype(BF16)
        other_send_ref[...] = acc_ref[pl.ds(pl.multiple_of(half + send, 8), part)].astype(BF16)


def context_back(place, low, ctx, w_own, w_other):
    count, feat, seq = low.shape
    half = w_own.shape[0]
    full = image_block((feat, seq))
    part = jax.ShapeDtypeStruct((half // 2, feat), BF16)
    return pl.pallas_call(
        context_back_kernel,
        out_shape=[jax.ShapeDtypeStruct((count, 2 * half, seq), BF16)] + [part] * 4,
        grid_spec=pltpu.PrefetchScalarGridSpec(
            num_scalar_prefetch=1,
            grid=(count,),
            in_specs=[
                full,
                image_block((2 * half, seq)),
                once((half, feat)),
                once((half, feat), (3, 0)),
            ],
            out_specs=[image_block((2 * half, seq))] + [once((half // 2, feat))] * 4,
            scratch_shapes=[pltpu.VMEM((2 * half, feat), F32)],
        ),
        compiler_params=params(1),
        cost_estimate=cost(8 * count * seq * half * feat, 25 << 20),
        name="context_back",
    )(place, low, ctx, w_own, w_other)


def project_back_kernel(place_ref, normed_ref, d_ref, keep_ref, send_ref, col_ref, acc_ref):
    step = pl.program_id(0)
    product = dot_nt(d_ref[0], normed_ref[0])
    column = token_sum(d_ref[0].astype(F32))

    @pl.when(step == 0)
    def _():
        acc_ref[...] = product
        col_ref[...] = column

    @pl.when(step > 0)
    def _():
        acc_ref[...] += product
        col_ref[...] += column

    @pl.when(step == pl.num_programs(0) - 1)
    def _():
        part = keep_ref.shape[0] // 3
        keep = place_ref[1] * part
        for index in range(3):
            rows = slice(index * part, (index + 1) * part)
            first = 2 * index * part
            keep_rows = pl.ds(pl.multiple_of(first + keep, 8), part)
            send_rows = pl.ds(pl.multiple_of(first + part - keep, 8), part)
            keep_ref[rows] = acc_ref[keep_rows].astype(BF16)
            send_ref[rows] = acc_ref[send_rows].astype(BF16)


def project_back(place, normed, d_qkv):
    count, feat, seq = normed.shape
    width = d_qkv.shape[1]
    part = jax.ShapeDtypeStruct((width // 2, feat), BF16)
    return pl.pallas_call(
        project_back_kernel,
        out_shape=[part, part, jax.ShapeDtypeStruct((width, 1), F32)],
        grid_spec=pltpu.PrefetchScalarGridSpec(
            num_scalar_prefetch=1,
            grid=(count,),
            in_specs=[image_block((feat, seq)), image_block((width, seq))],
            out_specs=[
                once((width // 2, feat)),
                once((width // 2, feat)),
                once((width, 1)),
            ],
            scratch_shapes=[pltpu.VMEM((width, feat), F32)],
        ),
        compiler_params=params(1),
        cost_estimate=cost(2 * count * seq * feat * width, 20 << 20),
        name="project_back",
    )(place, normed, d_qkv)


def input_back_kernel(
    place_ref,
    d_own_ref,
    d_other_ref,
    q_ref,
    k_ref,
    v_ref,
    w_other_ref,
    rows_ref,
    low_ref,
    gain_ref,
    *rest,
):
    out_ref, send_ref, row_gain_ref, row_bias_ref, w_ref, sum_gain_ref, sum_bias_ref = rest[-7:]
    width = q_ref.shape[0]

    @pl.when(pl.program_id(0) == 0)
    def _():
        w_ref[:width] = q_ref[...]
        w_ref[width : 2 * width] = k_ref[...]
        w_ref[2 * width :] = v_ref[...]
        sum_gain_ref[...] = jnp.zeros_like(sum_gain_ref)
        sum_bias_ref[...] = jnp.zeros_like(sum_bias_ref)

    grad_norm = dot_tn(w_ref[...], d_own_ref[0]) + dot_tn(w_other_ref[...], d_other_ref[0])
    normed, inverse = column_stats(rows_ref[0].astype(F32))
    scaled = grad_norm * column(gain_ref, LN1_GAIN)
    plain = jnp.mean(scaled, axis=0, keepdims=True)
    cross = jnp.mean(scaled * normed, axis=0, keepdims=True)
    grad = low_ref[0].astype(F32) + inverse * (scaled - plain - normed * cross)
    own, other = split_halves(place_ref[0] == 0, grad)
    out_ref[0] = own.astype(BF16)
    send_ref[0] = other.astype(BF16)
    sum_gain_ref[...] += token_sum(grad_norm * normed)
    sum_bias_ref[...] += token_sum(grad_norm)
    write_rows((row_gain_ref, row_bias_ref), (sum_gain_ref, sum_bias_ref))


def input_back(place, d_own, d_other, weights, w_other, rows, low, features, start, steps, held):
    count, width, seq = d_own.shape
    feat = rows.shape[1]
    wide = image_block((width, seq), start)
    full = image_block((feat, seq), start)
    held = [] if held is None else [held]
    return pl.pallas_call(
        input_back_kernel,
        out_shape=[
            jax.ShapeDtypeStruct((2 * count, feat // 2, seq), BF16),
            jax.ShapeDtypeStruct((steps, feat // 2, seq), BF16),
            jax.ShapeDtypeStruct((1, feat), F32),
            jax.ShapeDtypeStruct((1, feat), F32),
        ],
        grid_spec=pltpu.PrefetchScalarGridSpec(
            num_scalar_prefetch=1,
            grid=(steps,),
            in_specs=[wide, wide]
            + [once((width // 3, feat))] * 3
            + [once((width, feat)), full, full, once((feat, 8))]
            + [ANYWHERE] * len(held),
            out_specs=[
                pl.BlockSpec((1, feat // 2, seq), lambda i, p: (p[0] * count + start + i, 0, 0)),
                image_block((feat // 2, seq)),
                once((1, feat)),
                once((1, feat)),
            ],
            scratch_shapes=[
                pltpu.VMEM((width, feat), BF16),
                pltpu.VMEM((feat, 1), F32),
                pltpu.VMEM((feat, 1), F32),
            ],
        ),
        input_output_aliases={10: 0} if held else {},
        compiler_params=params(1),
        cost_estimate=cost(4 * steps * seq * feat * width, steps * (11 << 20) + (8 << 20), 0, LONG),
        name="input_back",
    )(place, d_own, d_other, *weights, w_other, rows, low, features, *held)


def widen_kernel(place_ref, mine_ref, other_ref, *out_refs, steps):
    half, step = pl.program_id(1), pl.program_id(2)
    mine = half == place_ref[1]
    value = jnp.where(mine, mine_ref[...], other_ref[...]).astype(F32)
    for index, out_ref in enumerate(out_refs):

        @pl.when(pl.program_id(0) == index)
        def _():
            out_ref[...] = value


def widen(place, mine, other, part, total, steps, count=1):
    feat = mine.shape[1]
    rows = part // steps
    last = 2 * steps - 1

    def mine_spot(w, h, i, p):
        used = 1 - (h - p[1]) * (h - p[1])
        return (w * steps + i * used, 0)

    def other_spot(w, h, i, p):
        used = (h - p[1]) * (h - p[1])
        return (w * steps + i * used, 0)

    def out_spot(index):
        return lambda w, h, i, p: (jnp.clip((w - index) * 2 * steps + h * steps + i, 0, last), 0)

    out = pl.pallas_call(
        functools.partial(widen_kernel, steps=steps),
        out_shape=[jax.ShapeDtypeStruct((total, feat), F32)] * count,
        grid_spec=pltpu.PrefetchScalarGridSpec(
            num_scalar_prefetch=1,
            grid=(count, 2, steps),
            in_specs=[
                pl.BlockSpec((rows, feat), mine_spot),
                pl.BlockSpec((rows, feat), other_spot),
            ],
            out_specs=[pl.BlockSpec((rows, feat), out_spot(index)) for index in range(count)],
        ),
        compiler_params=params(3),
        cost_estimate=cost(0, 8 * total * feat * count, 0, SHORT),
        name="widen",
    )(place, mine, other)
    return out if count > 1 else out[0]


def swap_tensor(value):
    return lax.ppermute(value, "tensor", [(0, 1), (1, 0)])


def swap_core(value):
    return lax.ppermute(value, "dp", [(spot, spot ^ 1) for spot in range(lax.axis_size("dp"))])


def exchange_sum(value, steps):
    total = value
    for step in steps:
        pairs = [(spot, spot ^ step) for spot in range(lax.axis_size("dp"))]
        total += lax.ppermute(value, "dp", pairs)
    return total


def other_weights(weights, spots, rows):
    per_weight = spots // len(weights)
    mine = lax.axis_index("dp")
    start = mine % per_weight * rows
    piece = None
    for index, weight in enumerate(weights):
        short = per_weight * rows - weight.shape[0]
        if short:
            weight = jnp.pad(weight, ((0, short), (0, 0)))
        part = lax.dynamic_slice_in_dim(weight, start, rows, 0)
        piece = part if piece is None else jnp.where(mine // per_weight == index, part, piece)
    return piece


def chip_groups(order):
    spots = lax.axis_size("dp")
    groups = [list(range(core, spots, 2)) for core in range(2)]
    return groups[::-1] if order else groups


def swap_step(value, step):
    return lax.ppermute(value, "dp", [(spot, spot ^ step) for spot in range(lax.axis_size("dp"))])


def side(step):
    return lax.axis_index("dp") // step % 2


def halves(value, step):
    rows = value.shape[0] // 2
    mine = side(step)
    keep = lax.dynamic_slice_in_dim(value, mine * rows, rows, 0)
    return keep, lax.dynamic_slice_in_dim(value, (1 - mine) * rows, rows, 0)


def ranked(mine, other, step):
    first = side(step) == 0
    return jnp.concatenate([jnp.where(first, mine, other), jnp.where(first, other, mine)])


def added(left, right):
    return (left.astype(F32) + right.astype(F32)).astype(BF16)


def both(keep, send):
    return keep.astype(F32) + swap_core(send).astype(F32)


def after(value, *others):
    return lax.optimization_barrier((value, *others))[0]


def whole_device(
    images,
    valid_flags,
    cotangent,
    ln1_gain,
    ln1_bias,
    q_weight,
    q_bias,
    k_weight,
    v_weight,
    v_bias,
    o_weight,
    o_bias,
    ln2_gain,
    ln2_bias,
    fc1_weight,
    fc1_bias,
    fc2_weight,
    fc2_bias,
):
    img_local, seq, half = images.shape
    count = img_local // 2
    feat = 2 * half
    spots = lax.axis_size("dp")
    width = q_weight.shape[1]
    hidden = fc1_weight.shape[1]
    heads = width // HDIM
    tensor = lax.axis_index("tensor")
    core = lax.axis_index("dp") % 2
    place = jnp.concatenate(
        [jnp.stack([tensor, core]).astype(jnp.int32), valid_flags.astype(jnp.int32)]
    )
    images, cotangent = jnp.swapaxes(images, 1, 2), jnp.swapaxes(cotangent, 1, 2)
    in_weights = [q_weight.T, k_weight.T, v_weight.T]
    fc1_own = fc1_weight.T

    def to_send(array, index, images=1):
        return lax.dynamic_slice_in_dim(array, (1 - tensor) * count + index, images, 0)

    small = jnp.concatenate(
        [ln1_gain, ln1_bias, o_bias, ln2_gain, ln2_bias, fc2_bias, q_bias, v_bias, fc1_bias]
    )
    cut_q, cut_v, cut_h = 6 * half, 6 * half + width, 6 * half + 2 * width
    block = quarter_rows(hidden)

    in_piece = other_weights([*in_weights, o_weight], spots, width // (spots // 4))
    first = to_send(images, 0)
    in_piece, first = lax.optimization_barrier((in_piece, first))
    images_other = [swap_tensor(first)]
    in_piece, small_other = swap_tensor(in_piece), swap_tensor(after(small, first))
    mlp_piece = other_weights([fc1_own, fc2_weight], spots, block // 2)
    next_image = to_send(images, 1)
    next_image, images_other[0], in_piece = lax.optimization_barrier(
        (next_image, images_other[0], in_piece)
    )
    in_other = lax.all_gather(in_piece, "dp", axis=0, tiled=True)
    images_other.append(swap_tensor(next_image))

    def features_of(source):
        return source[:cut_q].reshape(6, half)

    feature_own, feature_other = features_of(small), features_of(small_other)
    features = jnp.where(
        tensor == 0,
        jnp.concatenate([feature_own, feature_other], axis=1),
        jnp.concatenate([feature_other, feature_own], axis=1),
    )
    features = jnp.pad(features, ((0, 2), (0, 0))).astype(F32).T
    head_vectors = jnp.stack([small, small_other])[:, cut_q:cut_h].reshape(4, width)
    head_vectors = jnp.pad(head_vectors, ((0, 4), (0, 0))).astype(F32).T
    hidden_vectors = jnp.stack([small, small_other])[:, cut_h:].astype(F32).T

    state = None
    mixed = None
    for index in range(count):
        state = first_norm(
            index,
            count,
            place,
            images,
            images_other[index],
            features,
            in_weights,
            head_vectors,
            state,
        )
        state = list(state)
        if index == 0:
            mlp_piece, state[2] = lax.optimization_barrier((mlp_piece, state[2]))
            mlp_piece = swap_tensor(mlp_piece)
        if index == 1:
            mlp_piece, state[2] = lax.optimization_barrier((mlp_piece, state[2]))
            mlp_other = lax.all_gather(mlp_piece, "dp", axis=0, tiled=True)
        mixed = list(mix(state[2], 0, index, 1, mixed))
        if index + 2 < count:
            next_image = to_send(images, index + 2)
            next_image, images_other[-1], mixed[0] = lax.optimization_barrier(
                (next_image, images_other[-1], mixed[0])
            )
            images_other.append(swap_tensor(next_image))
        elif index + 2 == count:
            late = [to_send(cotangent, spot) for spot in range(count)]
            images_other[-1], mixed[0], *late = lax.optimization_barrier(
                (images_other[-1], mixed[0], *late)
            )
            cot_other = [swap_tensor(value) for value in late]
    rows, normed, qkv_own = state
    qkv_other = project(normed, in_other, head_vectors, width)
    ctx, logs = mix(qkv_other, 1, 0, count, mixed)
    ctx, *cot_other = lax.optimization_barrier((ctx, *cot_other))
    flat = (count, 2 * width, seq)
    resid, low_second, grad_out, sum_fc2b = second_norm(
        place, ctx.reshape(flat), o_weight, in_other, rows, features, cotangent, cot_other
    )

    def stage(keep, place, weights, offset, which, earlier):
        return hidden_stage(
            keep, place, low_second, grad_out, *weights, offset, hidden_vectors, which, earlier
        )

    *held, fc1_o, fc2_o = stage(False, place, (mlp_other, mlp_other), 4, 1, None)
    *stage_other, fc1_k, fc2_k = stage(True, place, (mlp_other, mlp_other), 4, 1, held)
    rows_a = 4 * block // 3 // 8 * 8
    rows_b = 2 * block - rows_a
    fc1_r, fc2_r = swap_core(fc1_o), swap_core(fc2_o)

    def summed(keep, arrived, low, high):
        return (keep[low:high].astype(F32) + arrived[low:high].astype(F32)).astype(BF16)

    piece = summed(fc1_k, fc1_r, 0, rows_a)
    later = (
        summed(fc1_k, fc1_r, rows_a, 2 * block),
        summed(fc2_k, fc2_r, 0, rows_a - rows_b),
        summed(fc2_k, fc2_r, rows_a - rows_b, 2 * block),
    )
    place2, piece, *later = lax.optimization_barrier((place, piece, *later))
    fc1_arrived = [swap_tensor(piece)]
    *held, fc1_o, fc2_o = stage(False, place2, (fc1_own, fc2_weight), 0, 0, None)
    held[2], fc1_arrived[0], *later = lax.optimization_barrier((held[2], fc1_arrived[0], *later))
    fc1_arrived.append(swap_tensor(later[0]))
    fc2_arrived = [swap_tensor(later[1])]
    *stage_own, fc1_k, fc2_k = stage(True, place2, (fc1_own, fc2_weight), 0, 0, held)
    back_own = stage_own[1]
    back_own, fc1_arrived[1], fc2_arrived[0], last = lax.optimization_barrier(
        (back_own, fc1_arrived[1], fc2_arrived[0], later[2])
    )
    g_fc1 = (both(fc1_k, fc1_o) + jnp.concatenate(fc1_arrived).astype(F32)).astype(BF16)
    fc2_r = swap_core(fc2_o)
    g_fc1, fc2_r, back_own = lax.optimization_barrier((g_fc1, fc2_r, back_own))
    fc2_arrived.append(swap_tensor(last))
    g_fc1 = lax.psum(g_fc1, "dp", axis_index_groups=chip_groups(0))
    low_resid, sum_gain2, sum_bias2, sum_ob = resid_back(
        back_own, stage_other[1], fc1_own, mlp_other, resid, grad_out, features
    )
    low_resid, fc2_arrived[1] = lax.optimization_barrier((low_resid, fc2_arrived[1]))
    g_late = fc2_k.astype(F32) + fc2_r.astype(F32) + jnp.concatenate(fc2_arrived).astype(F32)
    g_late = g_late.astype(BF16)
    x_keep, x_send = halves(g_late, 2)
    low_resid, x_keep, x_send = lax.optimization_barrier((low_resid, x_keep, x_send))
    d_ctx, *o_parts = context_back(place, low_resid, ctx.reshape(flat), o_weight, in_other)
    d_ctx = d_ctx.reshape(ctx.shape)
    d_ctx, x_send = lax.optimization_barrier((d_ctx, x_send))
    x_recv = swap_step(x_send, 2)
    wide = (count, 3 * width, seq)
    d_other = mix_back(qkv_other, ctx, logs, d_ctx, 1, 0, count, None).reshape(wide)
    o_send = both(o_parts[2], o_parts[3]).astype(BF16)
    o_pair = both(o_parts[0], o_parts[1])
    d_other, x_recv = lax.optimization_barrier((d_other, x_recv))
    z_keep, z_send = halves(added(x_keep, x_recv), 4)
    d_other, o_send, o_pair, z_keep, z_send = lax.optimization_barrier(
        (d_other, o_send, o_pair, z_keep, z_send)
    )
    z_recv = swap_step(z_send, 4)
    o_arrived = swap_tensor(o_send)
    other_keep, other_send, column_other = project_back(place, normed, d_other)
    o_arrived, other_keep, g_fc1, z_recv = lax.optimization_barrier(
        (o_arrived, other_keep, g_fc1, z_recv)
    )
    far_keep, far_send = halves(added(z_keep, z_recv), 8)
    g_o = (o_pair + o_arrived.astype(F32)).astype(BF16)
    d_ctx, g_o, far_keep, far_send = lax.optimization_barrier((d_ctx, g_o, far_keep, far_send))
    far_recv = swap_step(far_send, 8)
    fc1_other = swap_core(g_fc1)

    d_own = mix_back(qkv_own, ctx, logs, d_ctx, 0, 0, 1, None)
    other_recv = swap_core(other_send)
    third = 3 * width // 2 * 3 // 10 // 8 * 8
    cuts = [0, third, 2 * third, 3 * width // 2]
    pieces = [summed(other_keep, other_recv, *cuts[k : k + 2]) for k in range(3)]
    d_own, far_recv = lax.optimization_barrier((d_own, far_recv))
    block_sum = added(far_keep, far_recv)
    d_own, fc1_other, block_sum, *pieces = lax.optimization_barrier(
        (d_own, fc1_other, block_sum, *pieces)
    )
    qkv_arrived = []
    for index in range(1, count):
        step = 16 >> index
        block_recv = swap_step(block_sum, step)
        qkv_arrived.append(swap_tensor(pieces[index - 1]))
        d_own = mix_back(qkv_own, ctx, logs, d_ctx, 0, index, 1, d_own)
        d_own, qkv_arrived[-1], block_recv, *pieces = lax.optimization_barrier(
            (d_own, qkv_arrived[-1], block_recv, *pieces)
        )
        block_sum = ranked(block_sum, block_recv, step)
        d_own, block_sum = lax.optimization_barrier((d_own, block_sum))
    qkv_arrived += [swap_tensor(value) for value in pieces[count - 1 :]]
    d_own = d_own.reshape(wide)
    own_keep, own_send, column_own = project_back(place, normed, d_own)
    own_keep, d_own, *qkv_arrived = lax.optimization_barrier((own_keep, d_own, *qkv_arrived))

    def inputs(start, steps, held):
        return input_back(
            place, d_own, d_other, in_weights, in_other, rows, low_resid, features, start, steps, held
        )

    def ordered(own, other):
        return jnp.where(tensor == 0, jnp.stack([own, other]), jnp.stack([other, own]))

    def heads_part(vector):
        return vector[:width, 0], vector[2 * width :, 0]

    (q_own, v_own), (q_other, v_other) = heads_part(column_own), heads_part(column_other)
    early_sums = jnp.concatenate(
        [
            jnp.concatenate([sum_ob, sum_gain2, sum_bias2, sum_fc2b], axis=1)[0],
            ordered(
                jnp.concatenate([q_own, v_own, stage_own[2][:, 0]]),
                jnp.concatenate([q_other, v_other, stage_other[2][:, 0]]),
            ).reshape(-1),
        ]
    )
    d_own, early_sums = lax.optimization_barrier((d_own, early_sums))
    in_buffer, in_send, gain_a, bias_a = inputs(0, 1, None)
    block_recv = swap_step(block_sum, 2)
    own_recv, in_buffer, in_send = lax.optimization_barrier(
        (swap_core(own_send), in_buffer, in_send)
    )
    in_arrived = [swap_tensor(in_send)]
    g_qkv = own_keep.astype(F32) + own_recv.astype(F32) + jnp.concatenate(qkv_arrived).astype(F32)
    g_qkv = jnp.concatenate([g_qkv.astype(BF16), g_o])
    g_qkv, in_buffer = lax.optimization_barrier((g_qkv, in_buffer))
    g_qkv = lax.psum(g_qkv, "dp", axis_index_groups=chip_groups(1))
    in_buffer, in_send, gain_b, bias_b = inputs(1, count - 1, in_buffer)
    norm_sums = jnp.concatenate([gain_a + gain_b, bias_a + bias_b], axis=1)
    small_grads = jnp.concatenate([norm_sums[0], early_sums])
    small_swapped = swap_tensor(small_grads)
    in_send, in_arrived[0], act_own, block_recv = lax.optimization_barrier(
        (in_send, in_arrived[0], stage_own[0], block_recv)
    )
    g_late = ranked(block_sum, block_recv, 2)
    act_own, g_late = lax.optimization_barrier((act_own, g_late))
    far = (1 - tensor) * count
    in_arrived.append(swap_tensor(in_send))
    late_other = swap_core(g_late)

    out_buffer, out_send, last_send = layer_result(
        place, act_own, stage_other[0], fc2_weight, mlp_other, resid, features
    )
    in_arrived[1], out_send, out_buffer, small_swapped, late_other = lax.optimization_barrier(
        (in_arrived[1], out_send, out_buffer, small_swapped, late_other)
    )
    small_grads += small_swapped
    out_arrived = [swap_tensor(out_send)]
    out_fc1 = widen(place, g_fc1, fc1_other, 2 * block, hidden, 4)
    input_grad = lax.dynamic_update_slice_in_dim(in_buffer, jnp.concatenate(in_arrived), far, 0)
    out_fc2 = widen(place, g_late, late_other, 2 * block, hidden, 4)

    out_fc1, input_grad, small_grads = lax.optimization_barrier((out_fc1, input_grad, small_grads))
    near = exchange_sum(small_grads, (1, 2, 3))
    out_fc2, near = lax.optimization_barrier((out_fc2, near))
    small_grads = exchange_sum(near, range(4, spots, 4))
    g_qkv, small_grads, out_fc2, out_arrived[0] = lax.optimization_barrier(
        (g_qkv, small_grads, out_fc2, out_arrived[0])
    )
    qkv_other_core = swap_core(g_qkv)
    out_arrived.append(swap_tensor(after(last_send, g_qkv)))
    g_feature = lax.dynamic_slice_in_dim(
        small_grads[: 6 * feat].reshape(6, feat), tensor * half, half, 1
    )
    small_grads = lax.dynamic_index_in_dim(
        small_grads[6 * feat :].reshape(2, 2 * width + hidden), tensor, 0, keepdims=False
    )

    g_q, g_k, g_v, g_o = widen(place, g_qkv, qkv_other_core, width // 2, width, 2, 4)
    g_q, out_arrived[1] = lax.optimization_barrier((g_q, out_arrived[1]))
    layer_out = lax.dynamic_update_slice_in_dim(out_buffer, jnp.concatenate(out_arrived), far, 0)
    return (
        jnp.swapaxes(layer_out, 1, 2),
        jnp.swapaxes(input_grad, 1, 2),
        g_feature[0],
        g_feature[1],
        g_q.T,
        small_grads[:width],
        g_k.T,
        g_v.T,
        small_grads[width : 2 * width],
        g_o,
        g_feature[2],
        g_feature[3],
        g_feature[4],
        out_fc1.T,
        small_grads[2 * width :],
        out_fc2,
        g_feature[5],
    )


def solution(mesh):
    in_specs = (
        P("dp", None, "tensor"),
        P("dp"),
        P("dp", None, "tensor"),
        P("tensor"),
        P("tensor"),
        P(None, "tensor"),
        P("tensor"),
        P(None, "tensor"),
        P(None, "tensor"),
        P("tensor"),
        P("tensor", None),
        P("tensor"),
        P("tensor"),
        P("tensor"),
        P(None, "tensor"),
        P("tensor"),
        P("tensor", None),
        P("tensor"),
    )
    out_specs = (
        P("dp", None, "tensor"),
        P("dp", None, "tensor"),
        P("tensor"),
        P("tensor"),
        P(None, "tensor"),
        P("tensor"),
        P(None, "tensor"),
        P(None, "tensor"),
        P("tensor"),
        P("tensor", None),
        P("tensor"),
        P("tensor"),
        P("tensor"),
        P(None, "tensor"),
        P("tensor"),
        P("tensor", None),
        P("tensor"),
    )
    whole_images = mesh.shape["tensor"] == 2 and mesh.shape["dp"] == 16
    return jax.shard_map(
        whole_device if whole_images else split_device, mesh=mesh, in_specs=in_specs, out_specs=out_specs, check_vma=False
    )
```
